32 devices in a mesh: fsdp: 2 (over core), context: 4 (over y, x), tensor: 4 (over z).
Axes of the slice: x: 2, y: 2, z: 4, core: 2. Of those that a mesh axis runs over, the one named last changes fastest.
Arguments:
- inputs: bfloat16 [2, 2, 1280, 2048], P(None, 'fsdp', ('context', 'tensor')), may hold values from -6 to 6
- segments: int32 [2, 2, 1280], P(None, 'fsdp'), may hold values from 0 to 7, never falling along the last dimension, each value on 1 to 640 neighbouring positions
- norm_gain: float32 [2048], replicated, may hold values from 0.5 to 1.5
- branch_weight: bfloat16 [2048, 2560], P(('fsdp', 'context'), 'tensor'), may hold values from -0.125 to 0.125
- inner_weight: bfloat16 [2048, 2560], P(('fsdp', 'context'), 'tensor'), may hold values from -0.125 to 0.125
- conv_weight: float32 [4, 2560], P(None, 'tensor'), may hold values from -3 to 3
- conv_bias: float32 [2560], P('tensor'), may hold values from -3 to 3
- rate_weight: bfloat16 [16, 160, 160], P('tensor'), may hold values from -0.5 to 0.5
- rate_bias: float32 [2560], P('tensor'), may hold values from -4 to 4
- input_weight: bfloat16 [16, 160, 160], P('tensor'), may hold values from -0.5 to 0.5
- input_bias: float32 [2560], P('tensor'), may hold values from -4 to 4
- decay_param: float32 [2560], P('tensor'), may hold values from 4 to 11
- out_weight: bfloat16 [2560, 2048], P('tensor', ('fsdp', 'context')), may hold values from -0.5 to 0.5
- mlp_gain: float32 [2048], replicated, may hold values from 0.5 to 1.5
- gate_weight: bfloat16 [2048, 6144], P(('fsdp', 'context'), 'tensor'), may hold values from -0.125 to 0.125
- up_weight: bfloat16 [2048, 6144], P(('fsdp', 'context'), 'tensor'), may hold values from -0.125 to 0.125
- down_weight: bfloat16 [6144, 2048], P('tensor', ('fsdp', 'context')), may hold values from -0.15625 to 0.15625
- cotangent: bfloat16 [2, 2, 1280, 2048], P(None, 'fsdp', ('context', 'tensor')), may hold values from -6 to 6
Outputs:
- block_out: bfloat16 [2, 2, 1280, 2048], P(None, 'fsdp', ('context', 'tensor'))
- input_grad: float32 [2, 2, 1280, 2048], P(None, 'fsdp', ('context', 'tensor'))
- norm_gain_grad: float32 [2048], replicated
- branch_weight_grad: float32 [2048, 2560], P(('fsdp', 'context'), 'tensor')
- inner_weight_grad: float32 [2048, 2560], P(('fsdp', 'context'), 'tensor')
- conv_weight_grad: float32 [4, 2560], P(None, 'tensor')
- conv_bias_grad: float32 [2560], P('tensor')
- rate_weight_grad: float32 [16, 160, 160], P('tensor')
- rate_bias_grad: float32 [2560], P('tensor')
- input_weight_grad: float32 [16, 160, 160], P('tensor')
- input_bias_grad: float32 [2560], P('tensor')
- decay_param_grad: float32 [2560], P('tensor')
- out_weight_grad: float32 [2560, 2048], P('tensor', ('fsdp', 'context'))
- mlp_gain_grad: float32 [2048], replicated
- gate_weight_grad: float32 [2048, 6144], P(('fsdp', 'context'), 'tensor')
- up_weight_grad: float32 [2048, 6144], P(('fsdp', 'context'), 'tensor')
- down_weight_grad: float32 [6144, 2048], P('tensor', ('fsdp', 'context'))
The draws below stay inside these ranges and needn't reach their ends.
Inputs may be any that keep to these rules, and one draw needn't show every extreme that they name: `segments`: along each sequence the numbers never fall; each document is one run of 1 to 640 positions, every number of 0 to 7 is used in each sequence, and one document of each sequence has exactly 640 positions.
All inputs are finite; a program needn't handle non-finite values.
Results may differ from the reference program's by a relative error of at most 0.014.
Values may be sent and summed in bfloat16 or wider, within the bound.
No kernel may reach another device: no remote copies, remote signals or barrier semaphores. Data moves between devices by JAX's collectives and lax.ppermute only.
A program may use at most 256 MiB of HBM per device.

```python
import math
import jax
import jax.numpy as jnp
import numpy as np
from jax import lax

D = 2048
FF = 6144
BLOCKS = 16
BW = 160
CONV = 4
CPOW = 8
LEN = 1280
MICRO = 2
DOCS = 8
RNN = 2560
DOC_MOST = 640
SEQS = 2


def level_of(key, shape, shards, least, largest):
    def one(position, shards_of):
        draws = jax.random.uniform(jax.random.fold_in(jax.random.fold_in(key, 6), position), (shards_of,), jnp.float32, least / len(shards), largest / len(shards))
        return jnp.repeat(jnp.exp(draws), shape[position] // shards_of).reshape((-1,) + (1,) * (len(shape) - position - 1))

    loudness = one(*shards[0])
    for cut in shards[1:]:
        loudness = loudness * one(*cut)
    return loudness


def profile(number_of, total, limit, skew):
    portions = [(1 << 20) // math.isqrt(rank ** skew) + 1 for rank in range(2, number_of + 1)]
    surplus, counts = total - limit - (number_of - 1), [1] * (number_of - 1)
    while surplus > 0:
        movable = [i for i in range(number_of - 1) if counts[i] < limit]
        whole, remaining = sum([portions[i] for i in movable]), surplus
        for i in movable:
            more = min(limit - counts[i], max(1, remaining * portions[i] // whole), surplus)
            counts[i] = counts[i] + more
            surplus = surplus - more
    return np.array([limit] + counts)


def ragged(rng, count, total, reach, lean):
    if count == 2:
        one = jax.random.randint(rng, (), max(1, total - reach), min(reach, total - 1) + 1)
        return jnp.stack([one, total - one])
    lengths = jnp.asarray(profile(count, total, reach, lean), jnp.int32)
    pairs = (count - 1) // 2
    giver, sink = lengths[1:1 + 2 * pairs:2], lengths[2:2 + 2 * pairs:2]
    room = jnp.minimum(giver - 1, reach - sink)
    shifted = jax.random.randint(jax.random.fold_in(rng, 1), (pairs,), 0, 1 << 20) % (room + 1)
    lengths = lengths.at[1:1 + 2 * pairs:2].set(giver - shifted).at[2:2 + 2 * pairs:2].set(sink + shifted)
    return lengths[jax.random.permutation(jax.random.fold_in(rng, 2), count)]


def gaussian(rng, dims, deviation, bound, shards=(), dtype=jnp.bfloat16):
    gain = level_of(rng, dims, shards, -0.22, 0.18) if shards else 1.0
    values = jax.random.normal(rng, dims, jnp.float32) * deviation * gain
    return jnp.minimum(jnp.maximum(values, -bound), bound).astype(dtype)


def setup_inputs(seed: int = 0) -> dict:
    streams_of = jax.random.split(jax.random.key(seed), 19)
    return {
        "inputs": gaussian(streams_of[0], (MICRO, SEQS, LEN, D), 1.0, 6.0, ((1, 2), (2, 16))),
        "segments": jax.vmap(lambda own: jnp.searchsorted(jnp.cumsum(ragged(own, DOCS, LEN, DOC_MOST, 2)), jnp.arange(LEN), side="right"))(jax.random.split(streams_of[1], MICRO * SEQS)).reshape((MICRO, SEQS, LEN)).astype(jnp.int32),
        "norm_gain": jnp.clip(1.0 + 0.1 * jax.random.normal(streams_of[2], (D,), jnp.float32), 0.5, 1.5),
        "branch_weight": gaussian(streams_of[3], (D, RNN), D ** -0.5, 0.125, ((0, 8), (1, 4))),
        "inner_weight": gaussian(streams_of[4], (D, RNN), D ** -0.5, 0.125, ((0, 8), (1, 4))),
        "conv_weight": gaussian(streams_of[5], (CONV, RNN), 0.5, 3.0, ((1, 4),), jnp.float32),
        "conv_bias": gaussian(streams_of[6], (RNN,), 0.5, 3.0, ((0, 4),), jnp.float32),
        "rate_weight": gaussian(streams_of[7], (BLOCKS, BW, BW), BW ** -0.5, 0.5, ((0, 4),)),
        "rate_bias": gaussian(streams_of[8], (RNN,), 1.0, 4.0, ((0, 4),), jnp.float32),
        "input_weight": gaussian(streams_of[9], (BLOCKS, BW, BW), BW ** -0.5, 0.5, ((0, 4),)),
        "input_bias": gaussian(streams_of[10], (RNN,), 1.0, 4.0, ((0, 4),), jnp.float32),
        "decay_param": jnp.clip(4.0 + 7.0 * jax.random.uniform(streams_of[11], (RNN,), jnp.float32) ** level_of(streams_of[11], (RNN,), ((0, 4),), -0.2, 0.2), 4.0, 11.0),
        "out_weight": gaussian(streams_of[12], (RNN, D), (RNN // 16) ** -0.5, 0.5, ((0, 4), (1, 8))),
        "mlp_gain": jnp.clip(1.0 + 0.1 * jax.random.normal(streams_of[13], (D,), jnp.float32), 0.5, 1.5),
        "gate_weight": gaussian(streams_of[14], (D, FF), D ** -0.5, 0.125, ((0, 8), (1, 4))),
        "up_weight": gaussian(streams_of[15], (D, FF), D ** -0.5, 0.125, ((0, 8), (1, 4))),
        "down_weight": gaussian(streams_of[16], (FF, D), (FF // 4) ** -0.5, 0.15625, ((0, 4), (1, 8))),
        "cotangent": gaussian(streams_of[17], (MICRO, SEQS, LEN, D), 1.0, 6.0, ((1, 2), (2, 16))),
    }


EPS = 1e-06

@jax.custom_vjp
def low(v):
    return lax.optimization_barrier(v.astype(jnp.bfloat16)).astype(jnp.float32)

@jax.custom_vjp
def low_back(v):
    return v

def low_keep(v):
    return (low(v), None)

def low_pass(kept, grad):
    return (grad,)

def back_keep(v):
    return (v, None)

def back_low(kept, grad):
    return (low(grad),)
low.defvjp(low_keep, low_pass)
low_back.defvjp(back_keep, back_low)

def rms_norm(values, gain_vec):
    return values * lax.rsqrt(lax.optimization_barrier(jnp.mean(values * values, axis=-1, keepdims=True)) + EPS) * gain_vec

def matmul(left_arr, right_arr):
    return jnp.dot(left_arr, right_arr, precision=lax.Precision.HIGHEST)

def block_mix(values, weight):
    shaped = values.reshape(values.shape[0], BLOCKS, BW)
    return jnp.einsum('lnb,nbc->lnc', shaped, weight, precision=lax.Precision.HIGHEST).reshape(values.shape)

def combine(earlier, following):
    return (earlier[0] * following[0], following[0] * earlier[1] + following[1])

def layer(tokens, seg_row, params):
    norm_gain, branch_w, inner_w, conv_w, conv_b, rate_w, rate_b, input_w, input_b, decay_param, out_w, mlp_gain, gate_w, up_w, down_w = params
    normed = low_back(low(rms_norm(tokens, norm_gain)))
    branch_pre = low_back(matmul(normed, branch_w))
    inner = low_back(low(matmul(normed, inner_w)))
    padded = jnp.concatenate([jnp.zeros((CONV - 1, inner.shape[1]), jnp.float32), inner], axis=0)
    seg_pad = jnp.concatenate([jnp.full((CONV - 1,), -1, jnp.int32), seg_row.astype(jnp.int32)])
    current = seg_pad[CONV - 1:]
    conv_out = conv_b + conv_w[0] * inner
    for offset in range(1, CONV):
        same_doc = (seg_pad[CONV - 1 - offset:CONV - 1 - offset + LEN] == current).astype(jnp.float32)[:, None]
        conv_out = conv_out + conv_w[offset] * padded[CONV - 1 - offset:CONV - 1 - offset + LEN] * same_doc
    starts = (seg_pad[CONV - 2:CONV - 2 + LEN] != current)[:, None]
    conv_low = low(conv_out)
    rate_pre = low_back(block_mix(conv_low, rate_w) + rate_b)
    input_pre = low_back(block_mix(conv_low, input_w) + input_b)
    log_rate = -CPOW * jax.nn.softplus(-decay_param) * jax.nn.sigmoid(rate_pre)
    decays = jnp.where(starts, 0.0, jnp.exp(log_rate))
    input_scale = jnp.where(starts, 1.0, jnp.sqrt(-jnp.expm1(2.0 * log_rate)))
    drives = input_scale * jax.nn.sigmoid(input_pre) * conv_low
    states = lax.associative_scan(combine, (decays, drives), axis=0)[1]
    mixed = low(states * jax.nn.gelu(branch_pre))
    residual = tokens + low_back(matmul(mixed, out_w))
    normed_two = low_back(low(rms_norm(residual, mlp_gain)))
    gate_pre = low_back(matmul(normed_two, gate_w))
    up_pre = low_back(matmul(normed_two, up_w))
    hidden = low(jax.nn.gelu(gate_pre) * up_pre)
    return residual + low_back(matmul(hidden, down_w))

def reference(inputs, segments, norm_gain, branch_weight, inner_weight, conv_weight, conv_bias, rate_weight, rate_bias, input_weight, input_bias, decay_param, out_weight, mlp_gain, gate_weight, up_weight, down_weight, cotangent):
    params = tuple((param_arr.astype(jnp.float32) for param_arr in (norm_gain, branch_weight, inner_weight, conv_weight, conv_bias, rate_weight, rate_bias, input_weight, input_bias, decay_param, out_weight, mlp_gain, gate_weight, up_weight, down_weight)))
    flat_inputs = inputs.astype(jnp.float32).reshape(-1, LEN, D)
    flat_segs = segments.reshape(-1, LEN).astype(jnp.int32)
    flat_cotan = cotangent.astype(jnp.float32).reshape(-1, LEN, D)

    def one_sequence(totals, seq_item):
        tokens, seg_row, cot_row = seq_item

        def forward(token_arr, param_set):
            return layer(token_arr, seg_row, param_set)
        result, pull_back = jax.vjp(forward, tokens, params)
        token_grad, param_grads = pull_back(cot_row)
        return (jax.tree.map(jnp.add, totals, param_grads), (result.astype(jnp.bfloat16), token_grad))
    zero_grads = jax.tree.map(jnp.zeros_like, params)
    totals, (block_seq, grad_seq) = lax.scan(one_sequence, zero_grads, (flat_inputs, flat_segs, flat_cotan))
    return (block_seq.reshape(inputs.shape), grad_seq.reshape(inputs.shape), totals[0], totals[1], totals[2], totals[3], totals[4], totals[5], totals[6], totals[7], totals[8], totals[9], totals[10], totals[11], totals[12], totals[13], totals[14])
```

```python
from functools import partial

import jax
import jax.numpy as jnp
from jax import lax
from jax.experimental import pallas as pl
from jax.experimental.pallas import tpu as pltpu
from jax.sharding import PartitionSpec as P

CONV = 4
CPOW = 8
EPS = 1e-06
TILE = 8
F32 = jnp.float32
BF16 = jnp.bfloat16
GELU_A = 0.7978845608028654
GELU_B = 0.044715


def shift(value, axis, by):
    size = lax.axis_size(axis)
    return lax.ppermute(value, axis, [(i, (i + by) % size) for i in range(size)])


def step_by(value, axis, by):
    size = lax.axis_size(axis)
    return lax.ppermute(value, axis, [(i, i + by) for i in range(size) if 0 <= i + by < size])


def widen(block):
    size = lax.axis_size("tensor")
    return jnp.concatenate([block] + [shift(block, "tensor", k) for k in range(1, size)], axis=0)


def narrow(partial_low):
    size = lax.axis_size("tensor")
    rows = partial_low.shape[0] // size
    total = partial_low[:rows].astype(F32)
    for k in range(1, size):
        total = total + shift(partial_low[k * rows : (k + 1) * rows], "tensor", -k).astype(F32)
    return total


def sum_over(value, axis):
    size = lax.axis_size(axis)
    parts = [value] + [shift(value, axis, k) for k in range(1, size)]
    total = parts[0].astype(F32)
    for part in parts[1:]:
        total = total + part.astype(F32)
    return total


def matmul(left, right):
    return jnp.dot(left, right, preferred_element_type=F32)


def matmul_nt(left, right):
    return lax.dot_general(left, right, (((1,), (1,)), ((), ())), preferred_element_type=F32)


def matmul_tn(left, right):
    return lax.dot_general(left, right, (((0,), (0,)), ((), ())), preferred_element_type=F32)


def gelu_parts(v):
    th = jnp.tanh(GELU_A * (v + GELU_B * (v * v * v)))
    half = 0.5 * (1.0 + th)
    slope = half + 0.5 * v * (1.0 - th * th) * (GELU_A * (1.0 + 3.0 * GELU_B * (v * v)))
    return v * half, slope


def neg_expm1(z):
    series = 1.0 + z * (1.0 / 10.0)
    for n in (9.0, 8.0, 7.0, 6.0, 5.0, 4.0, 3.0, 2.0):
        series = 1.0 + z * (1.0 / n) * series
    return jnp.where(z > -0.5, -z * series, 1.0 - jnp.exp(z))


def sigmoid(v):
    return 1.0 / (1.0 + jnp.exp(-v))


def tile_scan(coeffs, offsets, reverse):
    rows, width = coeffs.shape
    a = coeffs.reshape(rows // TILE, TILE, width)
    b = offsets.reshape(rows // TILE, TILE, width)
    place = lax.broadcasted_iota(jnp.int32, a.shape, 1)
    for s in (1, 2, 4):
        if reverse:
            inside, turn = place < TILE - s, TILE - s
        else:
            inside, turn = place >= s, s
        a_far = pltpu.roll(a, turn, 1)
        b_far = pltpu.roll(b, turn, 1)
        b = jnp.where(inside, b + a * b_far, b)
        a = jnp.where(inside, a * a_far, a)
    return a, b


def forward_kernel(
    pos_ref, inner_ref, halo_ref, mask_ref, par_ref, wg_ref,
    conv_ref, pre_ref, decay_ref, prod_ref, state_ref, last_ref, ext, run,
):
    rows = inner_ref.shape[0]
    step = pl.program_id(0)

    @pl.when(step == 0)
    def _():
        ext[0:TILE] = halo_ref[...].astype(F32)
        run[0:1] = jnp.ones_like(run[0:1])
        run[1:2] = jnp.zeros_like(run[1:2])

    inner = inner_ref[...].astype(BF16).astype(F32)
    ext[TILE : TILE + rows] = inner
    mask = mask_ref[...]
    conv = par_ref[CONV : CONV + 1] + par_ref[0:1] * inner
    for k in range(1, CONV):
        conv = conv + par_ref[k : k + 1] * ext[TILE - k : TILE - k + rows] * mask[:, k - 1 : k]
    ext[0:TILE] = inner[rows - TILE :]
    conv_low = conv.astype(BF16)
    conv_ref[...] = conv_low
    pre = jnp.dot(conv_low, wg_ref[...], preferred_element_type=F32)
    width = inner.shape[1]
    rate_pre = pre[:, :width] + par_ref[CONV + 2 : CONV + 3]
    input_pre = pre[:, width:] + par_ref[CONV + 3 : CONV + 4]
    pre_ref[:, :width] = rate_pre
    pre_ref[:, width:] = input_pre
    log_rate = par_ref[CONV + 1 : CONV + 2] * sigmoid(rate_pre)
    starts = mask[:, CONV - 1 : CONV] > 0.5
    decays = jnp.where(starts, 0.0, jnp.exp(log_rate))
    scale = jnp.where(starts, 1.0, jnp.sqrt(neg_expm1(2.0 * log_rate)))
    drives = scale * sigmoid(input_pre) * conv_low.astype(F32)
    decay_ref[...] = decays
    a, b = tile_scan(decays, drives, False)
    prod, state = run[0:1], run[1:2]
    for i in range(rows // TILE):
        prods = a[i] * prod
        states = b[i] + a[i] * state
        prod_ref[i * TILE : (i + 1) * TILE] = prods
        state_ref[i * TILE : (i + 1) * TILE] = states
        prod, state = prods[TILE - 1 :], states[TILE - 1 :]
    run[0:1] = prod
    run[1:2] = state
    last_ref[0:1] = prod
    last_ref[1:2] = state


def reverse_kernel(
    pos_ref, mixed_ref, branch_ref, states_ref, decay_ref,
    low_ref, prod_ref, grad_ref, first_ref, ext, run,
):
    rows = mixed_ref.shape[0]
    step = pl.program_id(0)

    @pl.when(step == 0)
    def _():
        ext[rows : rows + TILE] = jnp.ones_like(ext[rows : rows + TILE])
        run[0:1] = jnp.ones_like(run[0:1])
        run[1:2] = jnp.zeros_like(run[1:2])

    mixed = mixed_ref[...]
    value, slope = gelu_parts(branch_ref[...])
    low_ref[...] = (mixed * states_ref[...] * slope).astype(BF16)
    decays = decay_ref[...]
    ext[0:rows] = decays
    following = ext[1 : rows + 1]
    ext[rows : rows + TILE] = decays[0:TILE]
    a, b = tile_scan(following, mixed * value, True)
    prod, grad = run[0:1], run[1:2]
    for i in reversed(range(rows // TILE)):
        prods = a[i] * prod
        grads = b[i] + a[i] * grad
        prod_ref[i * TILE : (i + 1) * TILE] = prods
        grad_ref[i * TILE : (i + 1) * TILE] = grads
        prod, grad = prods[0:1], grads[0:1]
    run[0:1] = prod
    run[1:2] = grad
    first_ref[0:1] = decays[0:1] * prod
    first_ref[1:2] = decays[0:1] * grad


def gates_kernel(
    pos_ref, prod_ref, grad_ref, in_ref, prev_ref, state_in_ref, states_ref, decay_ref, pre_ref, conv_ref,
    inner_ref, inner_prev_ref, halo_ref, mask_ref, par_ref, wg_ref,
    low_ref, inner_grad_ref, edge_ref, sums_ref, ext, later,
):
    rows, width = prod_ref.shape
    step = pl.program_id(0)
    at_start = step == pl.num_programs(0) - 1

    @pl.when(step == 0)
    def _():
        sums_ref[...] = jnp.zeros_like(sums_ref)
        later[...] = jnp.zeros_like(later)

    mask = mask_ref[...]
    starts = mask[:, CONV - 1 : CONV] > 0.5
    drive_grad = grad_ref[...] + prod_ref[...] * in_ref[...]
    ext[TILE : TILE + rows] = states_ref[...]
    ext[TILE - 1 : TILE] = jnp.where(at_start, state_in_ref[...], prev_ref[TILE - 1 : TILE])
    prev_states = ext[TILE - 1 : TILE - 1 + rows]
    rate = sigmoid(pre_ref[:, :width])
    gate = sigmoid(pre_ref[:, width:])
    conv = conv_ref[...].astype(F32)
    slope = par_ref[CONV + 1 : CONV + 2]
    log_rate = slope * rate
    decays = decay_ref[...]
    raw = jnp.sqrt(neg_expm1(2.0 * log_rate))
    scale = jnp.where(starts, 1.0, raw)
    scale_grad = drive_grad * gate * conv
    log_grad = jnp.where(
        starts, 0.0, drive_grad * prev_states * decays - scale_grad * (decays * decays) / raw
    )
    rate_low = (log_grad * slope * rate * (1.0 - rate)).astype(BF16)
    input_low = (drive_grad * scale * conv * gate * (1.0 - gate)).astype(BF16)
    low_ref[:, :width] = rate_low
    low_ref[:, width:] = input_low
    both = jnp.concatenate([rate_low, input_low], axis=1)
    conv_grad = drive_grad * scale * gate + lax.dot_general(
        both, wg_ref[...], (((1,), (1,)), ((), ())), preferred_element_type=F32
    )
    inner = inner_ref[...].astype(BF16).astype(F32)
    before = jnp.where(at_start, halo_ref[...].astype(F32), inner_prev_ref[...].astype(BF16).astype(F32))
    ext[0:TILE] = before
    ext[TILE : TILE + rows] = inner

    def total(values):
        return jnp.sum(values, axis=0, keepdims=True)

    sums_ref[0:1] += total(conv_grad * inner)
    sums_ref[CONV : CONV + 1] += total(conv_grad)
    sums_ref[CONV + 1 : CONV + 2] += total(log_grad * rate)
    sums_ref[CONV + 2 : CONV + 3] += total(rate_low.astype(F32))
    sums_ref[CONV + 3 : CONV + 4] += total(input_low.astype(F32))
    inner_grad = par_ref[0:1] * conv_grad
    heads = []
    for k in range(1, CONV):
        masked = conv_grad * mask[:, k - 1 : k]
        sums_ref[k : k + 1] += total(masked * ext[TILE - k : TILE - k + rows])
        heads.append(masked[0:TILE] * par_ref[k : k + 1])
    for k in range(1, CONV):
        masked = par_ref[k : k + 1] * (conv_grad * mask[:, k - 1 : k])
        ext[0:rows] = masked
        ext[rows : rows + TILE] = later[k - 1]
        inner_grad = inner_grad + ext[k : k + rows]
        later[k - 1] = heads[k - 1]
    inner_grad_ref[...] = inner_grad.astype(inner_grad_ref.dtype)

    @pl.when(at_start)
    def _():
        edge_ref[...] = jnp.zeros_like(edge_ref)
        for back in range(1, CONV):
            row = heads[back - 1][0:1]
            for k in range(back + 1, CONV):
                row = row + heads[k - 1][k - back : k - back + 1]
            edge_ref[TILE - back : TILE - back + 1] = row


def rows_spec(rows, width, parts, column=0, reverse=False):
    def where(step, pos):
        place = parts - 1 - step if reverse else step
        return (lax.rem(pos[0] - place + parts, parts), column)

    return pl.BlockSpec((rows, width), where)


def ordered_spec(rows, width, parts, reverse=False):
    return pl.BlockSpec((rows, width), lambda step, pos: ((parts - 1 - step if reverse else step), 0))


def before_spec(rows, width, parts, column=0):
    tiles = rows // TILE

    def where(step, pos):
        place = jnp.maximum(parts - 2 - step, 0)
        return (lax.rem(pos[0] - place + parts, parts) * tiles + tiles - 1, column)

    return pl.BlockSpec((TILE, width), where)


def whole_spec(shape):
    return pl.BlockSpec(shape, lambda step, pos: (0,) * len(shape))


def call(kernel, parts, in_specs, out_specs, out_shape, scratch, flops, moved):
    return pl.pallas_call(
        kernel,
        out_shape=out_shape,
        grid_spec=pltpu.PrefetchScalarGridSpec(
            num_scalar_prefetch=1, grid=(parts,), in_specs=in_specs, out_specs=out_specs, scratch_shapes=scratch
        ),
        cost_estimate=pl.CostEstimate(flops=flops, bytes_accessed=moved, transcendentals=flops // 100),
    )


def forward_scan(pos, both_pre, halo, mask, params, gate_w, parts):
    total, width = both_pre.shape[0], params.shape[1]
    rows = total // parts
    spec = partial(rows_spec, rows, width, parts)
    shape = jax.ShapeDtypeStruct
    return call(
        forward_kernel, parts,
        [spec(column=1), whole_spec(halo.shape), ordered_spec(rows, mask.shape[1], parts),
         whole_spec(params.shape), whole_spec(gate_w.shape)],
        [spec(), rows_spec(rows, 2 * width, parts), spec(), spec(), spec(), whole_spec((2, width))],
        [shape((total, width), BF16), shape((total, 2 * width), F32), shape((total, width), F32),
         shape((total, width), F32), shape((total, width), F32), shape((2, width), F32)],
        [pltpu.VMEM((rows + TILE, width), F32), pltpu.VMEM((TILE, width), F32)],
        4 * total * width * width + 400 * total * width, 30 * total * width + 4 * width * width,
    )(pos, both_pre, halo, mask, params, gate_w)


def reverse_scan(pos, mixed_grad, both_pre, states, decays, parts):
    total, width = states.shape
    rows = total // parts
    spec = rows_spec(rows, width, parts, reverse=True)
    shape = jax.ShapeDtypeStruct
    return call(
        reverse_kernel, parts,
        [spec, spec, spec, spec],
        [spec, spec, spec, whole_spec((2, width))],
        [shape((total, width), BF16), shape((total, width), F32), shape((total, width), F32),
         shape((2, width), F32)],
        [pltpu.VMEM((rows + TILE, width), F32), pltpu.VMEM((TILE, width), F32)],
        400 * total * width, 26 * total * width,
    )(pos, mixed_grad, both_pre, states, decays)


def gates_back(pos, prods, grads, grad_in, states, state_in, decays, pre, conv_low, both_pre, halo, mask,
               params, gate_w, parts):
    total, width = states.shape
    rows = total // parts
    spec = partial(rows_spec, rows, width, parts, reverse=True)
    shape = jax.ShapeDtypeStruct
    return call(
        gates_kernel, parts,
        [spec(), spec(), whole_spec((1, width)), before_spec(rows, width, parts), whole_spec((1, width)),
         spec(), spec(), rows_spec(rows, 2 * width, parts, reverse=True), spec(), spec(column=1),
         before_spec(rows, width, parts, column=1), whole_spec(halo.shape),
         ordered_spec(rows, mask.shape[1], parts, reverse=True), whole_spec(params.shape),
         whole_spec(gate_w.shape)],
        [rows_spec(rows, 2 * width, parts, reverse=True), spec(), whole_spec((TILE, width)),
         whole_spec((TILE, width))],
        [shape((total, 2 * width), BF16), shape((total, width), F32), shape((TILE, width), F32),
         shape((TILE, width), F32)],
        [pltpu.VMEM((rows + TILE, width), F32), pltpu.VMEM((CONV - 1, TILE, width), F32)],
        4 * total * width * width + 800 * total * width, 40 * total * width + 4 * width * width,
    )(pos, prods, grads, grad_in, states, state_in, states, decays, pre, conv_low, both_pre, both_pre, halo, mask,
      params, gate_w)


def carry_over(ends, direction):
    size = lax.axis_size("context")
    incoming = jnp.zeros_like(ends[1:2])
    parts = [step_by(ends, "context", direction * k) for k in range(1, size)]
    for part in reversed(parts):
        incoming = part[1:2] + part[0:1] * incoming
    return incoming


def block_diagonal(weight):
    count, rows, cols = weight.shape
    return jnp.concatenate(
        [jnp.pad(weight[i], ((0, 0), (i * cols, (count - 1 - i) * cols))) for i in range(count)], axis=0
    )


def diagonal_blocks(dense, count):
    rows, cols = dense.shape[0] // count, dense.shape[1] // count
    return jnp.stack([dense[i * rows : (i + 1) * rows, i * cols : (i + 1) * cols] for i in range(count)])


def per_device(
    inputs, segments, norm_gain, branch_weight, inner_weight, conv_weight, conv_bias, rate_weight, rate_bias,
    input_weight, input_bias, decay_param, out_weight, mlp_gain, gate_weight, up_weight, down_weight, cotangent,
):
    micro, seqs, rows, model = inputs.shape
    parts = lax.axis_size("tensor")
    span = rows * parts
    width = conv_bias.shape[0]
    blocks = rate_weight.shape[0]
    units = gate_weight.shape[1]
    chains = [(m, s) for m in range(micro) for s in range(seqs)]
    context_pos = lax.axis_index("context")
    tensor_pos = lax.axis_index("tensor")
    pos = tensor_pos.reshape(1).astype(jnp.int32)
    owners = ("fsdp", "context")

    both_w = lax.all_gather(jnp.concatenate([branch_weight, inner_weight], 1), owners, axis=0, tiled=True)
    out_w = lax.all_gather(out_weight, owners, axis=1, tiled=True)
    pair_w = lax.all_gather(jnp.concatenate([gate_weight, up_weight], 1), owners, axis=0, tiled=True)
    down_w = lax.all_gather(down_weight, owners, axis=1, tiled=True)
    gate_w = jnp.concatenate([block_diagonal(rate_weight), block_diagonal(input_weight)], axis=1)
    slope = -CPOW * jax.nn.softplus(-decay_param)
    params = jnp.concatenate(
        [conv_weight, conv_bias[None], slope[None], rate_bias[None], input_bias[None]], axis=0
    )

    def unit_rows(values):
        return values * lax.rsqrt(jnp.mean(values * values, axis=-1, keepdims=True) + EPS)

    def norm_back(values, grad, gain):
        inv = lax.rsqrt(jnp.mean(values * values, axis=-1, keepdims=True) + EPS)
        unit = values * inv
        scaled = grad * gain
        return inv * (scaled - unit * jnp.mean(scaled * unit, axis=-1, keepdims=True)), jnp.sum(grad * unit, axis=0)

    def masks_of(row):
        pad = jnp.concatenate([jnp.full((CONV - 1,), -1, jnp.int32), row])
        ext = lax.dynamic_slice_in_dim(pad, context_pos * span, span + CONV - 1)
        own = ext[CONV - 1 :]
        cols = [(ext[CONV - 1 - k : CONV - 1 - k + span] == own).astype(F32) for k in range(1, CONV)]
        return jnp.stack(cols + [1.0 - cols[0]], axis=1)

    last_block = lax.rem(tensor_pos + 1, parts)
    tail_row = last_block * rows + rows - TILE

    saved = []
    for m, s in chains:
        x_rows = inputs[m, s].astype(F32)
        mask = masks_of(segments[m, s])
        wide_one = widen((unit_rows(x_rows) * norm_gain).astype(BF16))
        wide_cot = widen(cotangent[m, s])
        both_pre = matmul(wide_one, both_w)
        tail = lax.dynamic_slice(both_pre, (tail_row, width), (TILE, width)).astype(BF16)
        halo = step_by(tail, "context", 1)
        conv_low, pre, decays, prods, locals_, ends = forward_scan(
            pos, both_pre, halo, mask, params, gate_w, parts
        )
        state_in = carry_over(ends, 1)
        states = locals_ + prods * state_in
        mixed_low = (states * jax.nn.gelu(both_pre[:, :width])).astype(BF16)
        residual = x_rows + narrow(matmul(mixed_low, out_w).astype(BF16))
        wide_two = widen((unit_rows(residual) * mlp_gain).astype(BF16))
        pair_pre = matmul(wide_two, pair_w)
        gate_val, gate_slope = gelu_parts(pair_pre[:, :units])
        up_pre = pair_pre[:, units:]
        hidden_low = (gate_val * up_pre).astype(BF16)
        block_out = (residual + narrow(matmul(hidden_low, down_w).astype(BF16))).astype(BF16)
        hidden_grad = matmul_nt(wide_cot, down_w)
        pair_low = jnp.concatenate(
            [(hidden_grad * up_pre * gate_slope).astype(BF16), (hidden_grad * gate_val).astype(BF16)], axis=1
        )
        two_grad = narrow(matmul_nt(pair_low, pair_w).astype(BF16)).astype(BF16).astype(F32)
        norm_term, gain_two = norm_back(residual, two_grad, mlp_gain)
        resid_grad = cotangent[m, s].astype(F32) + norm_term
        wide_resid = widen(resid_grad.astype(BF16))
        mixed_grad = matmul_nt(wide_resid, out_w)
        branch_low, rev_prods, rev_grads, firsts = reverse_scan(pos, mixed_grad, both_pre, states, decays, parts)
        grad_in = carry_over(firsts, -1)
        gates_low, inner_grad, edge, sums = gates_back(
            pos, rev_prods, rev_grads, grad_in, states, state_in, decays, pre, conv_low, both_pre, halo, mask,
            params, gate_w, parts,
        )
        edge_in = step_by(edge, "context", -1)
        tail_grad = lax.dynamic_slice(inner_grad, (tail_row, 0), (TILE, width)) + edge_in
        inner_low = lax.dynamic_update_slice(inner_grad, tail_grad, (tail_row, 0)).astype(BF16)
        both_low = jnp.concatenate([branch_low, inner_low], axis=1)
        one_part = matmul_nt(both_low, both_w).astype(BF16)
        gain_one = jnp.sum(one_part.astype(F32) * wide_one.astype(F32), axis=0)
        one_grad = narrow(one_part).astype(BF16).astype(F32)
        norm_term_one, _ = norm_back(x_rows, one_grad, norm_gain)
        saved.append(
            dict(
                block_out=block_out, input_grad=resid_grad + norm_term_one, one=wide_one, both=both_low,
                mixed=mixed_low, resid=wide_resid, two=wide_two, pair=pair_low, hidden=hidden_low, cot=wide_cot,
                conv=conv_low, gates=gates_low, sums=sums, gain_one=gain_one, gain_two=gain_two,
            )
        )

    def joined(name):
        return jnp.concatenate([item[name] for item in saved], axis=0)

    def added(name):
        total = saved[0][name]
        for item in saved[1:]:
            total = total + item[name]
        return total

    def stacked(name):
        return jnp.stack([item[name] for item in saved]).reshape(micro, seqs, rows, model)

    def share(term, dim):
        return lax.psum_scatter(term.astype(BF16), owners, scatter_dimension=dim, tiled=True).astype(F32)

    down_grad = share(matmul_tn(joined("hidden"), joined("cot")), 1)
    pair_grad = share(matmul_tn(joined("two"), joined("pair")), 0)
    out_grad = share(matmul_tn(joined("mixed"), joined("resid")), 1)
    both_grad = share(matmul_tn(joined("one"), joined("both")), 0)
    gates_term = matmul_tn(joined("conv"), joined("gates"))
    gate_blocks = jnp.concatenate(
        [diagonal_blocks(gates_term[:, :width], blocks), diagonal_blocks(gates_term[:, width:], blocks)], axis=0
    )
    gate_blocks = sum_over(sum_over(gate_blocks.astype(BF16), "fsdp").astype(BF16), "context")
    sums = sum_over(sum_over(added("sums"), "fsdp"), "context")
    gains = jnp.stack([added("gain_one") / norm_gain, added("gain_two")])
    gains = sum_over(sum_over(sum_over(gains, "fsdp"), "context"), "tensor")
    return (
        stacked("block_out"),
        stacked("input_grad"),
        gains[0],
        both_grad[:, :width],
        both_grad[:, width:],
        sums[:CONV],
        sums[CONV],
        gate_blocks[:blocks],
        sums[CONV + 2],
        gate_blocks[blocks:],
        sums[CONV + 3],
        sums[CONV + 1] * (CPOW * jax.nn.sigmoid(-decay_param)),
        out_grad,
        gains[1],
        pair_grad[:, :units],
        pair_grad[:, units:],
        down_grad,
    )


def solution(mesh):
    tokens = P(None, "fsdp", ("context", "tensor"), None)
    by_rows = P(("fsdp", "context"), "tensor")
    by_cols = P("tensor", ("fsdp", "context"))
    channel = P("tensor")
    taps = P(None, "tensor")
    blocks = P("tensor", None, None)
    return jax.shard_map(
        per_device,
        mesh=mesh,
        in_specs=(
            tokens, P(None, "fsdp", None), P(), by_rows, by_rows, taps, channel, blocks, channel, blocks, channel,
            channel, by_cols, P(), by_rows, by_rows, by_cols, tokens,
        ),
        out_specs=(
            tokens, tokens, P(), by_rows, by_rows, taps, channel, blocks, channel, blocks, channel, channel,
            by_cols, P(), by_rows, by_rows, by_cols,
        ),
        check_vma=False,
    )
```

```python
from functools import partial

import jax
import jax.numpy as jnp
from jax import lax
from jax.experimental import pallas as pl
from jax.experimental.pallas import tpu as pltpu
from jax.sharding import PartitionSpec as P

CONV = 4
CPOW = 8
EPS = 1e-06
TILE = 8
F32 = jnp.float32
BF16 = jnp.bfloat16
GELU_A = 0.7978845608028654
GELU_B = 0.044715
LONG = 10**4
RATE = 1e10


def shift(value, axis, by):
    size = lax.axis_size(axis)
    return lax.ppermute(value, axis, [(i, (i + by) % size) for i in range(size)])


def step_by(value, axis, by):
    size = lax.axis_size(axis)
    return lax.ppermute(value, axis, [(i, i + by) for i in range(size) if 0 <= i + by < size])


def sum_over(value, axis):
    size = lax.axis_size(axis)
    parts = [value] + [shift(value, axis, k) for k in range(1, size)]
    total = parts[0].astype(F32)
    for part in parts[1:]:
        total = total + part.astype(F32)
    return total


def gelu_parts(v):
    th = jnp.tanh(GELU_A * (v + GELU_B * (v * v * v)))
    half = 0.5 * (1.0 + th)
    slope = half + 0.5 * v * (1.0 - th * th) * (GELU_A * (1.0 + 3.0 * GELU_B * (v * v)))
    return v * half, slope


def neg_expm1(z):
    series = 1.0 + z * (1.0 / 10.0)
    for n in (9.0, 8.0, 7.0, 6.0, 5.0, 4.0, 3.0, 2.0):
        series = 1.0 + z * (1.0 / n) * series
    return jnp.where(z > -0.5, -z * series, 1.0 - jnp.exp(z))


def sigmoid(v):
    return 1.0 / (1.0 + jnp.exp(-v))


def tile_scan(coeffs, offsets, reverse):
    rows, width = coeffs.shape
    a = coeffs.reshape(rows // TILE, TILE, width)
    b = offsets.reshape(rows // TILE, TILE, width)
    place = lax.broadcasted_iota(jnp.int32, a.shape, 1)
    for s in (1, 2, 4):
        if reverse:
            inside, turn = place < TILE - s, TILE - s
        else:
            inside, turn = place >= s, s
        a_far = pltpu.roll(a, turn, 1)
        b_far = pltpu.roll(b, turn, 1)
        b = jnp.where(inside, b + a * b_far, b)
        a = jnp.where(inside, a * a_far, a)
    return a, b


def forward_kernel(
    inner_ref, halo_ref, mask_ref, par_ref, wg_ref,
    conv_ref, pre_ref, decay_ref, prod_ref, state_ref, last_ref, ext, run,
):
    rows = inner_ref.shape[0]
    step = pl.program_id(0)

    @pl.when(step == 0)
    def _():
        ext[0:TILE] = halo_ref[...].astype(F32)
        run[0:1] = jnp.ones_like(run[0:1])
        run[1:2] = jnp.zeros_like(run[1:2])

    inner = inner_ref[...].astype(BF16).astype(F32)
    ext[TILE : TILE + rows] = inner
    mask = mask_ref[...]
    conv = par_ref[CONV : CONV + 1] + par_ref[0:1] * inner
    for k in range(1, CONV):
        conv = conv + par_ref[k : k + 1] * ext[TILE - k : TILE - k + rows] * mask[:, k - 1 : k]
    ext[0:TILE] = inner[rows - TILE :]
    conv_low = conv.astype(BF16)
    conv_ref[...] = conv_low
    pre = jnp.dot(conv_low, wg_ref[...], preferred_element_type=F32)
    width = inner.shape[1]
    rate_pre = pre[:, :width] + par_ref[CONV + 2 : CONV + 3]
    input_pre = pre[:, width:] + par_ref[CONV + 3 : CONV + 4]
    pre_ref[:, :width] = rate_pre
    pre_ref[:, width:] = input_pre
    log_rate = par_ref[CONV + 1 : CONV + 2] * sigmoid(rate_pre)
    starts = mask[:, CONV - 1 : CONV] > 0.5
    decays = jnp.where(starts, 0.0, jnp.exp(log_rate))
    scale = jnp.where(starts, 1.0, jnp.sqrt(neg_expm1(2.0 * log_rate)))
    drives = scale * sigmoid(input_pre) * conv_low.astype(F32)
    decay_ref[...] = decays
    a, b = tile_scan(decays, drives, False)
    prod, state = run[0:1], run[1:2]
    for i in range(rows // TILE):
        prods = a[i] * prod
        states = b[i] + a[i] * state
        prod_ref[i * TILE : (i + 1) * TILE] = prods
        state_ref[i * TILE : (i + 1) * TILE] = states
        prod, state = prods[TILE - 1 :], states[TILE - 1 :]
    run[0:1] = prod
    run[1:2] = state
    last_ref[0:1] = prod
    last_ref[1:2] = state


def reverse_kernel(
    many, *refs
):
    blocks, refs = refs[: many + 1], refs[many + 1 :]
    (weight_ref, branch_ref, states_ref, decay_ref, wide_ref,
     low_ref, prod_ref, grad_ref, first_ref, mixed_all, ext, run) = refs
    rows = branch_ref.shape[0]
    step = pl.program_id(0)
    place = pl.num_programs(0) - 1 - step

    @pl.when(step == 0)
    def _():
        ext[rows : rows + TILE] = jnp.ones_like(ext[rows : rows + TILE])
        run[0:1] = jnp.ones_like(run[0:1])
        run[1:2] = jnp.zeros_like(run[1:2])
        assemble(blocks, wide_ref)
        mixed_all[...] = dot_nt(wide_ref[...], weight_ref[...])

    mixed = mixed_all[pl.ds(pl.multiple_of(place * rows, TILE), rows)]
    value, slope = gelu_parts(branch_ref[...])
    low_ref[...] = (mixed * states_ref[...] * slope).astype(BF16)
    decays = decay_ref[...]
    ext[0:rows] = decays
    following = ext[1 : rows + 1]
    ext[rows : rows + TILE] = decays[0:TILE]
    a, b = tile_scan(following, mixed * value, True)
    prod, grad = run[0:1], run[1:2]
    for i in reversed(range(rows // TILE)):
        prods = a[i] * prod
        grads = b[i] + a[i] * grad
        prod_ref[i * TILE : (i + 1) * TILE] = prods
        grad_ref[i * TILE : (i + 1) * TILE] = grads
        prod, grad = prods[0:1], grads[0:1]
    run[0:1] = prod
    run[1:2] = grad
    first_ref[0:1] = decays[0:1] * prod
    first_ref[1:2] = decays[0:1] * grad


def gates_kernel(
    prod_ref, grad_ref, in_ref, prev_ref, state_in_ref, states_ref, decay_ref, pre_ref, conv_ref,
    inner_ref, inner_prev_ref, halo_ref, mask_ref, par_ref, wg_ref,
    low_ref, inner_grad_ref, edge_ref, sums_ref, ext, later,
):
    rows, width = prod_ref.shape
    step = pl.program_id(0)
    at_start = step == pl.num_programs(0) - 1

    @pl.when(step == 0)
    def _():
        sums_ref[...] = jnp.zeros_like(sums_ref)
        later[...] = jnp.zeros_like(later)

    mask = mask_ref[...]
    starts = mask[:, CONV - 1 : CONV] > 0.5
    drive_grad = grad_ref[...] + prod_ref[...] * in_ref[...]
    ext[TILE : TILE + rows] = states_ref[...]
    ext[TILE - 1 : TILE] = jnp.where(at_start, state_in_ref[...], prev_ref[TILE - 1 : TILE])
    prev_states = ext[TILE - 1 : TILE - 1 + rows]
    rate = sigmoid(pre_ref[:, :width])
    gate = sigmoid(pre_ref[:, width:])
    conv = conv_ref[...].astype(F32)
    slope = par_ref[CONV + 1 : CONV + 2]
    log_rate = slope * rate
    decays = decay_ref[...]
    raw = jnp.sqrt(neg_expm1(2.0 * log_rate))
    scale = jnp.where(starts, 1.0, raw)
    scale_grad = drive_grad * gate * conv
    log_grad = jnp.where(
        starts, 0.0, drive_grad * prev_states * decays - scale_grad * (decays * decays) / raw
    )
    rate_low = (log_grad * slope * rate * (1.0 - rate)).astype(BF16)
    input_low = (drive_grad * scale * conv * gate * (1.0 - gate)).astype(BF16)
    low_ref[:, :width] = rate_low
    low_ref[:, width:] = input_low
    both = jnp.concatenate([rate_low, input_low], axis=1)
    conv_grad = drive_grad * scale * gate + lax.dot_general(
        both, wg_ref[...], (((1,), (1,)), ((), ())), preferred_element_type=F32
    )
    inner = inner_ref[...].astype(BF16).astype(F32)
    before = jnp.where(at_start, halo_ref[...].astype(F32), inner_prev_ref[...].astype(BF16).astype(F32))
    ext[0:TILE] = before
    ext[TILE : TILE + rows] = inner

    def total(values):
        return jnp.sum(values, axis=0, keepdims=True)

    sums_ref[0:1] += total(conv_grad * inner)
    sums_ref[CONV : CONV + 1] += total(conv_grad)
    sums_ref[CONV + 1 : CONV + 2] += total(log_grad * rate)
    sums_ref[CONV + 2 : CONV + 3] += total(rate_low.astype(F32))
    sums_ref[CONV + 3 : CONV + 4] += total(input_low.astype(F32))
    inner_grad = par_ref[0:1] * conv_grad
    heads = []
    for k in range(1, CONV):
        masked = conv_grad * mask[:, k - 1 : k]
        sums_ref[k : k + 1] += total(masked * ext[TILE - k : TILE - k + rows])
        heads.append(masked[0:TILE] * par_ref[k : k + 1])
    for k in range(1, CONV):
        masked = par_ref[k : k + 1] * (conv_grad * mask[:, k - 1 : k])
        ext[0:rows] = masked
        ext[rows : rows + TILE] = later[k - 1]
        inner_grad = inner_grad + ext[k : k + rows]
        later[k - 1] = heads[k - 1]
    inner_grad_ref[...] = inner_grad.astype(inner_grad_ref.dtype)

    @pl.when(at_start)
    def _():
        edge_ref[...] = jnp.zeros_like(edge_ref)
        for back in range(1, CONV):
            row = heads[back - 1][0:1]
            for k in range(back + 1, CONV):
                row = row + heads[k - 1][k - back : k - back + 1]
            edge_ref[TILE - back : TILE - back + 1] = row


def rows_spec(rows, width, parts, column=0, reverse=False):
    return pl.BlockSpec((rows, width), lambda step: (parts - 1 - step if reverse else step, column))


def before_spec(rows, width, parts, column=0):
    tiles = rows // TILE
    return pl.BlockSpec(
        (TILE, width), lambda step: (jnp.maximum(parts - 2 - step, 0) * tiles + tiles - 1, column)
    )


def whole_spec(shape):
    return pl.BlockSpec(shape, lambda step: (0,) * len(shape))


def dot_nt(left, right):
    return lax.dot_general(left, right, (((1,), (1,)), ((), ())), preferred_element_type=F32)


def dot_tn(left, right):
    return lax.dot_general(left, right, (((0,), (0,)), ((), ())), preferred_element_type=F32)


class Clock:
    def __init__(self):
        self.tick = jnp.zeros((TILE, 128), F32)

    def call(self, kernel, grid, operands, in_specs, out_specs, out_shape, scratch=(), after=(), cost=3.0):
        count, extra, outs = len(operands), len(after) + 1, len(out_shape)

        def body(*refs):
            given, refs = refs[:count], refs[count + extra :]
            kernel(*given, *refs[:outs], *refs[outs + 1 :])
            refs[outs][...] = jnp.zeros_like(refs[outs])

        whole = pl.BlockSpec((TILE, 128), lambda *step: (0, 0))
        *results, self.tick = pl.pallas_call(
            body,
            out_shape=list(out_shape) + [jax.ShapeDtypeStruct((TILE, 128), F32)],
            grid=grid,
            in_specs=list(in_specs) + [pl.BlockSpec(memory_space=pl.ANY)] * extra,
            out_specs=list(out_specs) + [whole],
            scratch_shapes=list(scratch),
            cost_estimate=pl.CostEstimate(flops=int(cost * RATE), bytes_accessed=int(cost * RATE), transcendentals=0),
        )(*operands, *after, self.tick)
        return results


def shape(dims, dtype):
    return jax.ShapeDtypeStruct(dims, dtype)


def held(array):
    dims = array.shape
    return pl.BlockSpec(dims, lambda *step: (0,) * len(dims), pipeline_mode=pl.Buffered(1))


def kept(dims):
    return pl.BlockSpec(dims, lambda *step: (0,) * len(dims))


def place_spec():
    return pl.BlockSpec(memory_space=pltpu.SMEM)


def spread(copies, apart):
    if not apart:
        return [lax.all_to_all(copies, "tensor", split_axis=0, concat_axis=0, tiled=True)]
    return [copies] + [shift(copies, "tensor", k) for k in range(1, lax.axis_size("tensor"))]


def gathered_sums(parts):
    if len(parts) == 1:
        return [lax.all_to_all(parts[0], "tensor", split_axis=0, concat_axis=0, tiled=True)]
    return [parts[0]] + [shift(parts[k], "tensor", k) for k in range(1, len(parts))]


def assemble(refs, wide_ref):
    place, blocks = refs[0], refs[1:]
    if len(blocks) == 1:
        wide_ref[...] = blocks[0][...]
        return
    rows = blocks[0].shape[0]
    for k, block in enumerate(blocks):
        owner = lax.rem(place[0] - k + len(blocks), len(blocks))
        wide_ref[pl.ds(pl.multiple_of(owner * rows, 2 * TILE), rows)] = block[...]


def deal(values, place, outs, work):
    if len(outs) == 1:
        outs[0][...] = values.astype(BF16)
        return
    work[...] = values
    rows = outs[0].shape[0]
    for k, out in enumerate(outs):
        owner = lax.rem(place[0] + k, len(outs))
        out[...] = work[pl.ds(pl.multiple_of(owner * rows, 2 * TILE), rows)].astype(BF16)


def added(refs, rows):
    if len(refs) == 1:
        count = refs[0].shape[0] // rows
        terms = [refs[0][k * rows : (k + 1) * rows].astype(F32) for k in range(count)]
    else:
        terms = [ref[...].astype(F32) for ref in refs]
    return sum(terms[1:], terms[0])


def repeat_to(ref, values, rows):
    for k in range(ref.shape[0] // rows):
        ref[k * rows : (k + 1) * rows] = values


def mean_of(values):
    return jnp.mean(values, axis=-1, keepdims=True)


def first_kernel(x_ref, gain_ref, out_ref):
    x = x_ref[...].astype(F32)
    repeat_to(out_ref, (x * lax.rsqrt(mean_of(x * x) + EPS) * gain_ref[...]).astype(BF16), x_ref.shape[0])


def first(clock, x, gain, copies):
    rows, model = x.shape
    return clock.call(
        first_kernel, (1,), [x, gain], [held(x), held(gain)],
        [kept((copies * rows, model))], [shape((copies * rows, model), BF16)],
        cost=0.2,
    )[0]


def copies_kernel(*refs):
    out_ref = refs[-1]
    rows = refs[0].shape[0]
    for k in range(out_ref.shape[0] // rows):
        out_ref[k * rows : (k + 1) * rows] = refs[k % (len(refs) - 1)][...]


def all_copies(clock, arrays, copies, after):
    rows, model = arrays[0].shape
    total = rows * len(arrays) * copies
    return clock.call(
        copies_kernel, (1,), arrays, [held(a) for a in arrays], [kept((total, model))],
        [shape((total, model), BF16)], after=after,
        cost=3.0,
    )[0]


def project_kernel(many, *refs):
    blocks, (weight_ref, wide_ref, out_ref, halo_ref) = refs[: many + 1], refs[many + 1 :]

    @pl.when(pl.program_id(0) == 0)
    def _():
        assemble(blocks, wide_ref)

    value = jnp.dot(wide_ref[...], weight_ref[...], preferred_element_type=F32)
    out_ref[...] = value

    @pl.when(pl.program_id(0) == pl.num_programs(0) - 1)
    def _():
        halo_ref[...] = value[value.shape[0] - TILE :].astype(BF16)


def project(clock, place, blocks, weight, after=()):
    model, cols = weight.shape
    rows = sum(block.shape[0] for block in blocks)
    width = cols // 2
    return clock.call(
        partial(project_kernel, len(blocks)), (2,), [place, *blocks, weight],
        [place_spec()] + [held(b) for b in blocks] + [pl.BlockSpec((model, width), lambda j: (0, j))],
        [kept((rows, model)), pl.BlockSpec((rows, width), lambda j: (0, j)), kept((TILE, width))],
        [shape((rows, model), BF16), shape((rows, cols), F32), shape((TILE, width), BF16)], after=after,
        cost=6.0,
    )


def mix_kernel(outs, place_ref, local_ref, prod_ref, in_ref, branch_ref, weight_ref, *refs):
    states_ref, mixed_ref = refs[:2]

    @pl.when(pl.program_id(0) == 0)
    def _():
        states = local_ref[...] + prod_ref[...] * in_ref[...]
        states_ref[...] = states
        mixed_ref[...] = (states * gelu_parts(branch_ref[...])[0]).astype(BF16)

    value = jnp.dot(mixed_ref[...], weight_ref[...], preferred_element_type=F32)
    deal(value, place_ref, refs[2 : 2 + outs], refs[-1])


def part_specs(rows, cols, tile, outs):
    return (
        [pl.BlockSpec((rows // outs, tile), lambda j: (0, j))] * outs,
        [shape((rows // outs, cols), BF16)] * outs,
        pltpu.VMEM((rows, tile), F32),
    )


def mix_out(clock, place, local, prods, state_in, both_pre, weight, outs, tile, after=()):
    rows, width = local.shape
    cols = weight.shape[1]
    part_spec, part_shape, work = part_specs(rows, cols, tile, outs)
    results = clock.call(
        partial(mix_kernel, outs), (cols // tile,), [place, local, prods, state_in, both_pre, weight],
        [place_spec(), held(local), held(prods), held(state_in),
         pl.BlockSpec((rows, width), lambda j: (0, 0), pipeline_mode=pl.Buffered(1)),
         pl.BlockSpec((width, tile), lambda j: (0, j))],
        [kept((rows, width)), kept((rows, width))] + part_spec,
        [shape((rows, width), F32), shape((rows, width), BF16)] + part_shape, [work], after,
        cost=5.7,
    )
    return results[0], results[1], results[2:]


def second_kernel(x_ref, gain_ref, *refs):
    terms, (resid_ref, out_ref) = refs[:-2], refs[-2:]
    rows = x_ref.shape[0]
    resid = x_ref[...].astype(F32) + added(terms, rows)
    resid_ref[...] = resid
    repeat_to(out_ref, (resid * lax.rsqrt(mean_of(resid * resid) + EPS) * gain_ref[...]).astype(BF16), rows)


def second(clock, x, gain, terms, copies):
    rows, model = x.shape
    return clock.call(
        second_kernel, (1,), [x, gain, *terms], [held(x), held(gain)] + [held(t) for t in terms],
        [kept((rows, model)), kept((copies * rows, model))],
        [shape((rows, model), F32), shape((copies * rows, model), BF16)],
        cost=3.0,
    )


def mlp_kernel(two_many, turn, turns, unit, outs, *refs):
    two_blocks, refs = refs[: two_many + 1], refs[two_many + 1 :]
    cot_all, gate_ref, up_ref, down_ref, two_ref, cot_ref, hidden_ref, pair_ref = refs[:8]
    parts, acc = refs[8 : 8 + outs], refs[-1]
    step = pl.program_id(0)

    @pl.when(step == 0)
    def _():
        assemble(two_blocks, two_ref)
        rows = unit
        for k in range(two_ref.shape[0] // rows):
            start = (k * turns + turn) * rows
            cot_ref[k * rows : (k + 1) * rows] = cot_all[start : start + rows]

    two = two_ref[...]
    gate_w, up_w = gate_ref[...], up_ref[...]
    gate_val, gate_slope = gelu_parts(jnp.dot(two, gate_w, preferred_element_type=F32))
    up_pre = jnp.dot(two, up_w, preferred_element_type=F32)
    hidden_ref[...] = (gate_val * up_pre).astype(BF16)
    hidden_grad = dot_nt(cot_ref[...], down_ref[...])
    gate_low = (hidden_grad * up_pre * gate_slope).astype(BF16)
    up_low = (hidden_grad * gate_val).astype(BF16)
    pair_ref[0] = gate_low
    pair_ref[1] = up_low
    term = dot_nt(gate_low, gate_w) + dot_nt(up_low, up_w)

    @pl.when(step == 0)
    def _():
        acc[...] = term

    @pl.when(step > 0)
    def _():
        acc[...] += term

    @pl.when(step == pl.num_programs(0) - 1)
    def _():
        rows = parts[0].shape[0]
        for k, out in enumerate(parts):
            start = 0 if outs == 1 else pl.multiple_of(lax.rem(two_blocks[0][0] + k, outs) * rows, 2 * TILE)
            out[...] = acc[pl.ds(start, rows)].astype(BF16)


def mlp(clock, place, two_blocks, cot_all, turn, turns, unit, pair_w, down_w, outs, tile, after=()):
    units, model = down_w.shape
    rows = sum(block.shape[0] for block in two_blocks)
    steps = units // tile
    results = clock.call(
        partial(mlp_kernel, len(two_blocks), turn, turns, unit, outs), (steps,),
        [place, *two_blocks, cot_all, pair_w, pair_w, down_w],
        [place_spec()] + [held(b) for b in two_blocks + [cot_all]]
        + [pl.BlockSpec((model, tile), lambda j: (0, j)), pl.BlockSpec((model, tile), lambda j: (0, steps + j)),
           pl.BlockSpec((tile, model), lambda j: (j, 0))],
        [kept((rows, model)), kept((rows, model)), pl.BlockSpec((rows, tile), lambda j: (0, j)),
         pl.BlockSpec((2, rows, tile), lambda j: (0, 0, j))] + [kept((rows // outs, model))] * outs,
        [shape((rows, model), BF16), shape((rows, model), BF16), shape((rows, units), BF16),
         shape((2, rows, units), BF16)] + [shape((rows // outs, model), BF16)] * outs,
        [pltpu.VMEM((rows, model), F32)], after,
        cost=27.0,
    )
    return *results[:4], results[4:]


def down_kernel(count, unit, *refs):
    right, out_ref = refs[count], refs[-1]
    for i in range(count):
        value = jnp.dot(refs[i][...], right[...], preferred_element_type=F32).astype(BF16)
        for k in range(value.shape[0] // unit):
            start = (k * count + i) * unit
            out_ref[start : start + unit] = value[k * unit : (k + 1) * unit]


def down_out(clock, lefts, right, unit, tile):
    depth, cols = right.shape
    count = len(lefts)
    total = count * lefts[0].shape[0]
    return clock.call(
        partial(down_kernel, count, unit), (cols // tile,), [*lefts, right],
        [held(a) for a in lefts] + [pl.BlockSpec((depth, tile), lambda j: (0, j))],
        [pl.BlockSpec((total, tile), lambda j: (0, j))], [shape((total, cols), BF16)],
        cost=0.01,
    )[0]


def norm_grad(values, grad, gain):
    inv = lax.rsqrt(mean_of(values * values) + EPS)
    unit = values * inv
    scaled = grad * gain
    return inv * (scaled - unit * mean_of(scaled * unit)), grad * unit


def third_kernel(resid_ref, cot_ref, gain_ref, *refs):
    terms, (grad_ref, low_ref, sum_ref) = refs[:-3], refs[-3:]
    rows = resid_ref.shape[0]
    grad = added(terms, rows).astype(BF16).astype(F32)
    term, product = norm_grad(resid_ref[...], grad, gain_ref[...])
    total = cot_ref[...].astype(F32) + term
    grad_ref[...] = total
    sum_ref[...] = jnp.sum(product, axis=0, keepdims=True)
    repeat_to(low_ref, total.astype(BF16), rows)


def third(clock, resid, cot, gain, terms, copies, cost):
    rows, model = resid.shape
    return clock.call(
        third_kernel, (1,), [resid, cot, gain, *terms], [held(resid), held(cot), held(gain)] + [held(t) for t in terms],
        [kept((rows, model)), kept((copies * rows, model)), kept((1, model))],
        [shape((rows, model), F32), shape((copies * rows, model), BF16), shape((1, model), F32)],
        cost=cost,
    )


def back_kernel(outs, place_ref, branch_ref, inner_ref, edge_ref, weight_ref, one_ref, *refs):
    both_ref, gain_ref = refs[:2]
    rows, width = branch_ref.shape

    @pl.when(pl.program_id(0) == 0)
    def _():
        both_ref[:, :width] = branch_ref[...]
        both_ref[: rows - 2 * TILE, width:] = inner_ref[: rows - 2 * TILE].astype(BF16)
        last = inner_ref[rows - 2 * TILE :]
        fixed = jnp.concatenate([last[:TILE], last[TILE:] + edge_ref[...]], axis=0)
        both_ref[rows - 2 * TILE :, width:] = fixed.astype(BF16)

    value = dot_nt(both_ref[...], weight_ref[...])
    gain_ref[...] = jnp.sum(value * one_ref[...].astype(F32), axis=0, keepdims=True)
    deal(value, place_ref, refs[2 : 2 + outs], refs[-1])


def back_one(clock, place, branch_low, inner_grad, edge_in, weight, wide_one, outs, tile):
    rows, width = branch_low.shape
    model = weight.shape[0]
    part_spec, part_shape, work = part_specs(rows, model, tile, outs)
    results = clock.call(
        partial(back_kernel, outs), (model // tile,), [place, branch_low, inner_grad, edge_in, weight, wide_one],
        [place_spec(), held(branch_low), held(inner_grad), held(edge_in),
         pl.BlockSpec((tile, 2 * width), lambda j: (j, 0)), pl.BlockSpec((rows, tile), lambda j: (0, j))],
        [kept((rows, 2 * width)), pl.BlockSpec((1, tile), lambda j: (0, j))] + part_spec,
        [shape((rows, 2 * width), BF16), shape((1, model), F32)] + part_shape, [work],
        cost=6.2,
    )
    return results[0], results[1], results[2:]


def last_kernel(x_ref, resid_ref, gain_ref, *refs):
    terms, out_ref = refs[:-1], refs[-1]
    grad = added(terms, x_ref.shape[0]).astype(BF16).astype(F32)
    out_ref[...] = resid_ref[...] + norm_grad(x_ref[...].astype(F32), grad, gain_ref[...])[0]


def last(clock, x, resid_grad, gain, terms):
    return clock.call(
        last_kernel, (1,), [x, resid_grad, gain, *terms],
        [held(x), held(resid_grad), held(gain)] + [held(t) for t in terms],
        [kept(resid_grad.shape)], [shape(resid_grad.shape, F32)], cost=LONG,
    )[0]


def out_kernel(count, *refs):
    terms, outs = refs[count], refs[count + 1 :]
    rows = refs[0].shape[0]
    for i in range(count):
        total = refs[i][...]
        for k in range(terms.shape[0] // (count * rows)):
            start = (k * count + i) * rows
            total = total + terms[start : start + rows].astype(F32)
        outs[i][...] = total.astype(BF16)


def block_results(clock, residuals, terms):
    count = len(residuals)
    dims = residuals[0].shape
    return clock.call(
        partial(out_kernel, count), (1,), [*residuals, terms], [held(r) for r in residuals] + [held(terms)],
        [kept(dims)] * count, [shape(dims, BF16)] * count,
        cost=3.0,
    )


def term_kernel(count, *refs):
    out_ref = refs[-1]
    total = None
    for i in range(count):
        right = refs[count + i]
        value = dot_tn(refs[i][...], right[0] if len(right.shape) == 3 else right[...])
        total = value if total is None else total + value
    out_ref[...] = total.astype(out_ref.dtype)


def weight_term(clock, lefts, rights, tile, cost, after=()):
    count = len(lefts)
    rows, depth = lefts[0].shape
    halves = rights[0].shape[0] if rights[0].ndim == 3 else 1
    cols = rights[0].shape[-1]
    if halves == 1:
        grid, left_at, out_at = (depth // tile,), (lambda j: (0, j)), (lambda j: (j, 0))
        right_spec = held(rights[0])
    else:
        grid, left_at, out_at = (halves, depth // tile), (lambda h, j: (0, j)), (lambda h, j: (j, h))
        right_spec = pl.BlockSpec((1, rows, cols), lambda h, j: (h, 0, 0))
    return clock.call(
        partial(term_kernel, count), grid, [*lefts, *rights],
        [pl.BlockSpec((rows, tile), left_at)] * count + [right_spec] * count,
        [pl.BlockSpec((tile, cols), out_at)], [shape((depth, halves * cols), BF16)], after=after,
        cost=cost,
    )[0]


def diagonal_kernel(count, cells, *refs):
    out_ref, work = refs[-2:]
    total = None
    for i in range(count):
        value = dot_tn(refs[i][...], refs[count + i][...])
        total = value if total is None else total + value
    work[...] = total
    cell = out_ref.shape[1]
    for i in range(cells):
        for h in range(2):
            col = (h * cells + i) * cell
            out_ref[h * cells + i] = work[i * cell : (i + 1) * cell, col : col + cell].astype(BF16)


def diagonal_terms(clock, lefts, rights, cells):
    count = len(lefts)
    width = lefts[0].shape[1]
    cell = width // cells
    return clock.call(
        partial(diagonal_kernel, count, cells), (1,), [*lefts, *rights],
        [held(a) for a in lefts] + [held(a) for a in rights],
        [kept((2 * cells, cell, cell))], [shape((2 * cells, cell, cell), BF16)],
        [pltpu.VMEM((width, 2 * width), F32)],
        cost=4.5,
    )[0]


def widen_kernel(width, in_ref, *outs):
    value = in_ref[...].astype(F32)
    for i, out in enumerate(outs):
        out[...] = value[:, i * width : (i + 1) * width]


def finish(clock, low, pieces):
    rows, cols = low.shape
    width = cols // pieces
    return clock.call(
        partial(widen_kernel, width), (1,), [low], [held(low)], [kept((rows, width))] * pieces,
        [shape((rows, width), F32)] * pieces, cost=LONG,
    )


def sum_kernel(*refs):
    refs[-1][...] = added(refs[:-1], refs[0].shape[0]).astype(refs[-1].dtype)


def sum_of(clock, arrays, dtype):
    dims = arrays[0].shape
    return clock.call(
        sum_kernel, (1,), arrays, [held(a) for a in arrays], [kept(dims)], [shape(dims, dtype)], cost=1.0,
    )[0]


def everyone(value, axis):
    return [value] + [shift(value, axis, k) for k in range(1, lax.axis_size(axis))]


def forward_scan(clock, both_pre, halo, mask, params, gate_w, parts):
    total, width = both_pre.shape[0], params.shape[1]
    rows = total // parts
    spec = partial(rows_spec, rows, width, parts)
    return clock.call(
        forward_kernel, (parts,), [both_pre, halo, mask, params, gate_w],
        [spec(column=1), held(halo), rows_spec(rows, mask.shape[1], parts), held(params), held(gate_w)],
        [spec(), rows_spec(rows, 2 * width, parts), spec(), spec(), spec(), kept((2, width))],
        [shape((total, width), BF16), shape((total, 2 * width), F32), shape((total, width), F32),
         shape((total, width), F32), shape((total, width), F32), shape((2, width), F32)],
        [pltpu.VMEM((rows + TILE, width), F32), pltpu.VMEM((TILE, width), F32)],
        cost=7.0,
    )


def reverse_scan(clock, place, blocks, out_w, both_pre, states, decays, parts, after=()):
    total, width = states.shape
    rows = total // parts
    model = out_w.shape[1]
    spec = rows_spec(rows, width, parts, reverse=True)
    return clock.call(
        partial(reverse_kernel, len(blocks)), (parts,), [place, *blocks, out_w, both_pre, states, decays],
        [place_spec()] + [held(b) for b in blocks] + [held(out_w), spec, spec, spec],
        [kept((total, model)), spec, spec, spec, kept((2, width))],
        [shape((total, model), BF16), shape((total, width), BF16), shape((total, width), F32),
         shape((total, width), F32), shape((2, width), F32)],
        [pltpu.VMEM((total, width), F32), pltpu.VMEM((rows + TILE, width), F32), pltpu.VMEM((TILE, width), F32)],
        after,
        cost=7.5,
    )


def gates_back(clock, prods, grads, grad_in, states, state_in, decays, pre, conv_low, both_pre, halo, mask,
               params, gate_w, parts):
    total, width = states.shape
    rows = total // parts
    spec = partial(rows_spec, rows, width, parts, reverse=True)
    return clock.call(
        gates_kernel, (parts,),
        [prods, grads, grad_in, states, state_in, states, decays, pre, conv_low, both_pre, both_pre, halo, mask,
         params, gate_w],
        [spec(), spec(), held(grad_in), before_spec(rows, width, parts), held(state_in),
         spec(), spec(), rows_spec(rows, 2 * width, parts, reverse=True), spec(), spec(column=1),
         before_spec(rows, width, parts, column=1), held(halo),
         rows_spec(rows, mask.shape[1], parts, reverse=True), held(params), held(gate_w)],
        [rows_spec(rows, 2 * width, parts, reverse=True), spec(), kept((TILE, width)), kept((TILE, width))],
        [shape((total, 2 * width), BF16), shape((total, width), F32), shape((TILE, width), F32),
         shape((TILE, width), F32)],
        [pltpu.VMEM((rows + TILE, width), F32), pltpu.VMEM((CONV - 1, TILE, width), F32)],
        cost=8.5,
    )


def carry_over(ends, direction):
    size = lax.axis_size("context")
    incoming = jnp.zeros_like(ends[1:2])
    parts = [step_by(ends, "context", direction * k) for k in range(1, size)]
    for part in reversed(parts):
        incoming = part[1:2] + part[0:1] * incoming
    return incoming


def carry_all(ends, direction):
    stacked = jnp.concatenate([e[:1] for e in ends] + [e[1:] for e in ends], axis=0)
    count = len(ends)
    incoming = jnp.zeros_like(stacked[:count])
    for part in reversed([step_by(stacked, "context", direction * k) for k in range(1, lax.axis_size("context"))]):
        incoming = part[count:] + part[:count] * incoming
    return [incoming[i : i + 1] for i in range(count)]


def block_diagonal(weight):
    count, rows, cols = weight.shape
    return jnp.concatenate(
        [jnp.pad(weight[i], ((0, 0), (i * cols, (count - 1 - i) * cols))) for i in range(count)], axis=0
    )


def per_device(
    inputs, segments, norm_gain, branch_weight, inner_weight, conv_weight, conv_bias, rate_weight, rate_bias,
    input_weight, input_bias, decay_param, out_weight, mlp_gain, gate_weight, up_weight, down_weight, cotangent,
):
    micro, seqs, rows, model = inputs.shape
    parts = lax.axis_size("tensor")
    span = rows * parts
    width = conv_bias.shape[0]
    blocks = rate_weight.shape[0]
    chains = [(m, s) for m in range(micro) for s in range(seqs)]
    context_pos = lax.axis_index("context")
    owners = ("fsdp", "context")

    both_w = lax.all_gather(jnp.concatenate([branch_weight, inner_weight], 1), owners, axis=0, tiled=True)
    out_w = lax.all_gather(out_weight, owners, axis=1, tiled=True)
    pair_w = lax.all_gather(jnp.concatenate([gate_weight, up_weight], 1), owners, axis=0, tiled=True)
    down_w = lax.all_gather(down_weight, owners, axis=1, tiled=True)
    gate_w = jnp.concatenate([block_diagonal(rate_weight), block_diagonal(input_weight)], axis=1)
    slope = -CPOW * jax.nn.softplus(-decay_param)
    params = jnp.concatenate(
        [conv_weight, conv_bias[None], slope[None], rate_bias[None], input_bias[None]], axis=0
    )

    def masks_of(row):
        pad = jnp.concatenate([jnp.full((CONV - 1,), -1, jnp.int32), row])
        ext = lax.dynamic_slice_in_dim(pad, context_pos * span, span + CONV - 1)
        own = ext[CONV - 1 :]
        cols = [(ext[CONV - 1 - k : CONV - 1 - k + span] == own).astype(F32) for k in range(1, CONV)]
        return jnp.stack(cols + [1.0 - cols[0]], axis=1)

    count = len(chains)
    turns = range(count)
    apart = [i % 2 == 1 for i in turns]
    copies = [1 if a else parts for a in apart]
    outs = [parts if a else 1 for a in apart]
    place = lax.axis_index("tensor").reshape(1).astype(jnp.int32)
    x_rows = [inputs[m, s] for m, s in chains]
    cot_rows = [cotangent[m, s] for m, s in chains]
    gain_one_row, gain_two_row = norm_gain[None], mlp_gain[None]
    mask = [masks_of(segments[m, s]) for m, s in chains]
    clock = Clock()

    def share(term, dim):
        return lax.psum_scatter(term, owners, scatter_dimension=dim, tiled=True)

    normed = [first(clock, x_rows[0], gain_one_row, copies[0])]
    cot_copies = all_copies(clock, cot_rows, parts, (gate_w, params, *mask))
    normed += [first(clock, x_rows[i], gain_one_row, copies[i]) for i in turns if i]
    one_blocks = [spread(normed[i], apart[i]) for i in turns]
    (cot_all,) = spread(cot_copies, False)
    projections = [project(clock, place, one_blocks[i], both_w) for i in turns]
    wide_one, both_pre, tails = map(list, zip(*projections))
    halo = [step_by(t, "context", 1) for t in tails]
    scans = [forward_scan(clock, both_pre[i], halo[i], mask[i], params, gate_w, parts) for i in turns]
    conv_low, pre, decays, prods, locals_, ends = map(list, zip(*scans))
    state_in = [carry_over(end, 1) for end in ends]
    mixes = [
        mix_out(clock, place, locals_[i], prods[i], state_in[i], both_pre[i], out_w, outs[i], 512,
                () if i else (cot_all,))
        for i in turns
    ]
    states, mixed_low, out_part = map(list, zip(*mixes))
    out_terms = [gathered_sums(p) for p in out_part]
    seconds = [second(clock, x_rows[i], gain_two_row, out_terms[i], copies[i]) for i in turns]
    residual = [t[0] for t in seconds]
    two_blocks = [spread(seconds[i][1], apart[i]) for i in turns]
    mlps = [
        mlp(clock, place, two_blocks[i], cot_all, i, count, rows, pair_w, down_w, outs[i], 256) for i in turns
    ]
    wide_two, wide_cot, hidden_low, pair_low, two_part = map(list, zip(*mlps))
    two_terms = [gathered_sums(p) for p in two_part]

    thirds = []
    for i in turns:
        thirds.append(third(clock, residual[i], cot_rows[i], gain_two_row, two_terms[i], copies[i], 0.01 if i else 3.4))
        if i == 0:
            pair_term = weight_term(clock, wide_two, pair_low, 256, 21.0)
    resid_grad, resid_low, gain_two = map(list, zip(*thirds))
    resid_blocks = [spread(resid_low[i], apart[i]) for i in turns]
    pair_grad = share(pair_term, 0)
    (down_terms,) = gathered_sums([down_out(clock, hidden_low, down_w, rows, 512)])
    down_term = weight_term(clock, hidden_low, wide_cot, 256, 0.01)
    down_grad = share(down_term, 1)

    reversed_ = [
        reverse_scan(clock, place, resid_blocks[i], out_w, both_pre[i], states[i], decays[i], parts) for i in turns
    ]
    wide_resid, branch_low, rev_prods, rev_grads, ends_back = map(list, zip(*reversed_))
    grad_in = carry_all(ends_back, -1)
    out_term = weight_term(clock, mixed_low, wide_resid, 128, 7.0)
    out_grad = share(out_term, 1)
    backs = []
    for i in turns:
        backs.append(gates_back(
            clock, rev_prods[i], rev_grads[i], grad_in[i], states[i], state_in[i], decays[i], pre[i], conv_low[i],
            both_pre[i], halo[i], mask[i], params, gate_w, parts,
        ))
    gates_low, inner_grad, edge, sums = map(list, zip(*backs))
    edge_in = [step_by(e, "context", -1) for e in edge]
    gate_blocks = diagonal_terms(clock, conv_low, gates_low, blocks)
    ones = []
    for i in turns:
        ones.append(back_one(
            clock, place, branch_low[i], inner_grad[i], edge_in[i], both_w, wide_one[i], outs[i], 512
        ))
        if i == 0:
            block_out = block_results(clock, residual, down_terms)
    both_low, gain_one, one_part = map(list, zip(*ones))
    one_terms = [gathered_sums(p) for p in one_part]
    both_term = weight_term(clock, wide_one, both_low, 256, 11.0)
    both_grad = share(both_term, 0)
    gate_blocks = sum_of(clock, everyone(gate_blocks, "fsdp"), BF16)
    gate_blocks = sum_of(clock, everyone(gate_blocks, "context"), F32)
    input_grad = [last(clock, x_rows[i], resid_grad[i], gain_one_row, one_terms[i]) for i in turns]
    gate_grad, up_grad = finish(clock, pair_grad, 2)
    (down_grad,) = finish(clock, down_grad, 1)
    (out_grad,) = finish(clock, out_grad, 1)
    branch_grad, inner_grad_w = finish(clock, both_grad, 2)

    def stacked(values):
        return jnp.stack(values).reshape(micro, seqs, rows, model)

    gains = jnp.concatenate([sum(gain_one) / gain_one_row, sum(gain_two)])
    small = jnp.concatenate([sum(sums).reshape(1, -1), gains.reshape(1, -1)], axis=1)
    small = sum_over(sum_over(small, "fsdp"), "context")
    sums = small[:, : TILE * width].reshape(TILE, width)
    gains = sum_over(small[:, TILE * width :], "tensor").reshape(2, model)
    return (
        stacked(block_out),
        stacked(input_grad),
        gains[0],
        branch_grad,
        inner_grad_w,
        sums[:CONV],
        sums[CONV],
        gate_blocks[:blocks],
        sums[CONV + 2],
        gate_blocks[blocks:],
        sums[CONV + 3],
        sums[CONV + 1] * (CPOW * jax.nn.sigmoid(-decay_param)),
        out_grad,
        gains[1],
        gate_grad,
        up_grad,
        down_grad,
    )


def solution(mesh):
    tokens = P(None, "fsdp", ("context", "tensor"), None)
    by_rows = P(("fsdp", "context"), "tensor")
    by_cols = P("tensor", ("fsdp", "context"))
    channel = P("tensor")
    taps = P(None, "tensor")
    blocks = P("tensor", None, None)
    return jax.shard_map(
        per_device,
        mesh=mesh,
        in_specs=(
            tokens, P(None, "fsdp", None), P(), by_rows, by_rows, taps, channel, blocks, channel, blocks, channel,
            channel, by_cols, P(), by_rows, by_rows, by_cols, tokens,
        ),
        out_specs=(
            tokens, tokens, P(), by_rows, by_rows, taps, channel, blocks, channel, blocks, channel, channel,
            by_cols, P(), by_rows, by_rows, by_cols,
        ),
        check_vma=False,
    )
```

```python
from functools import partial

import jax
import jax.numpy as jnp
from jax import lax
from jax.experimental import pallas as pl
from jax.experimental.pallas import tpu as pltpu
from jax.sharding import PartitionSpec as P

CONV = 4
CPOW = 8
EPS = 1e-06
TILE = 8
F32 = jnp.float32
BF16 = jnp.bfloat16
GELU_A = 0.7978845608028654
GELU_B = 0.044715
LONG = 10**4
RATE = 3e9


def shift(value, axis, by):
    size = lax.axis_size(axis)
    return lax.ppermute(value, axis, [(i, (i + by) % size) for i in range(size)])


def step_by(value, axis, by):
    size = lax.axis_size(axis)
    return lax.ppermute(value, axis, [(i, i + by) for i in range(size) if 0 <= i + by < size])


def sum_over(value, axis):
    size = lax.axis_size(axis)
    parts = [value] + [shift(value, axis, k) for k in range(1, size)]
    total = parts[0].astype(F32)
    for part in parts[1:]:
        total = total + part.astype(F32)
    return total


def gelu_parts(v):
    th = jnp.tanh(GELU_A * (v + GELU_B * (v * v * v)))
    half = 0.5 * (1.0 + th)
    slope = half + 0.5 * v * (1.0 - th * th) * (GELU_A * (1.0 + 3.0 * GELU_B * (v * v)))
    return v * half, slope


def neg_expm1(z):
    series = 1.0 + z * (1.0 / 10.0)
    for n in (9.0, 8.0, 7.0, 6.0, 5.0, 4.0, 3.0, 2.0):
        series = 1.0 + z * (1.0 / n) * series
    return jnp.where(z > -0.5, -z * series, 1.0 - jnp.exp(z))


def sigmoid(v):
    return 1.0 / (1.0 + jnp.exp(-v))


def tile_scan(coeffs, offsets, reverse):
    rows, width = coeffs.shape
    a = coeffs.reshape(rows // TILE, TILE, width)
    b = offsets.reshape(rows // TILE, TILE, width)
    place = lax.broadcasted_iota(jnp.int32, a.shape, 1)
    for s in (1, 2, 4):
        if reverse:
            inside, turn = place < TILE - s, TILE - s
        else:
            inside, turn = place >= s, s
        a_far = pltpu.roll(a, turn, 1)
        b_far = pltpu.roll(b, turn, 1)
        b = jnp.where(inside, b + a * b_far, b)
        a = jnp.where(inside, a * a_far, a)
    return a, b


def forward_kernel(
    inner_ref, halo_ref, mask_ref, par_ref, wg_ref,
    conv_ref, pre_ref, decay_ref, prod_ref, state_ref, last_ref, ext, run,
):
    rows = inner_ref.shape[0]
    step = pl.program_id(0)

    @pl.when(step == 0)
    def _():
        ext[0:TILE] = halo_ref[...].astype(F32)
        run[0:1] = jnp.ones_like(run[0:1])
        run[1:2] = jnp.zeros_like(run[1:2])

    inner = inner_ref[...].astype(BF16).astype(F32)
    ext[TILE : TILE + rows] = inner
    mask = mask_ref[...]
    conv = par_ref[CONV : CONV + 1] + par_ref[0:1] * inner
    for k in range(1, CONV):
        conv = conv + par_ref[k : k + 1] * ext[TILE - k : TILE - k + rows] * mask[:, k - 1 : k]
    ext[0:TILE] = inner[rows - TILE :]
    conv_low = conv.astype(BF16)
    conv_ref[...] = conv_low
    pre = jnp.dot(conv_low, wg_ref[...], preferred_element_type=F32)
    width = inner.shape[1]
    rate_pre = pre[:, :width] + par_ref[CONV + 2 : CONV + 3]
    input_pre = pre[:, width:] + par_ref[CONV + 3 : CONV + 4]
    pre_ref[:, :width] = rate_pre
    pre_ref[:, width:] = input_pre
    log_rate = par_ref[CONV + 1 : CONV + 2] * sigmoid(rate_pre)
    starts = mask[:, CONV - 1 : CONV] > 0.5
    decays = jnp.where(starts, 0.0, jnp.exp(log_rate))
    scale = jnp.where(starts, 1.0, jnp.sqrt(neg_expm1(2.0 * log_rate)))
    drives = scale * sigmoid(input_pre) * conv_low.astype(F32)
    decay_ref[...] = decays
    a, b = tile_scan(decays, drives, False)
    prod, state = run[0:1], run[1:2]
    for i in range(rows // TILE):
        prods = a[i] * prod
        states = b[i] + a[i] * state
        prod_ref[i * TILE : (i + 1) * TILE] = prods
        state_ref[i * TILE : (i + 1) * TILE] = states
        prod, state = prods[TILE - 1 :], states[TILE - 1 :]
    run[0:1] = prod
    run[1:2] = state
    last_ref[0:1] = prod
    last_ref[1:2] = state


def reverse_kernel(
    many, *refs
):
    blocks, refs = refs[: many + 1], refs[many + 1 :]
    (weight_ref, branch_ref, states_ref, decay_ref, wide_ref,
     low_ref, prod_ref, grad_ref, first_ref, mixed_all, ext, run) = refs
    rows = branch_ref.shape[0]
    step = pl.program_id(0)
    place = pl.num_programs(0) - 1 - step

    @pl.when(step == 0)
    def _():
        ext[rows : rows + TILE] = jnp.ones_like(ext[rows : rows + TILE])
        run[0:1] = jnp.ones_like(run[0:1])
        run[1:2] = jnp.zeros_like(run[1:2])
        assemble(blocks, wide_ref)
        mixed_all[...] = jnp.dot(wide_ref[...], weight_ref[...], preferred_element_type=F32)

    mixed = mixed_all[pl.ds(pl.multiple_of(place * rows, TILE), rows)]
    value, slope = gelu_parts(branch_ref[...])
    low_ref[...] = (mixed * states_ref[...] * slope).astype(BF16)
    decays = decay_ref[...]
    ext[0:rows] = decays
    following = ext[1 : rows + 1]
    ext[rows : rows + TILE] = decays[0:TILE]
    a, b = tile_scan(following, mixed * value, True)
    prod, grad = run[0:1], run[1:2]
    for i in reversed(range(rows // TILE)):
        prods = a[i] * prod
        grads = b[i] + a[i] * grad
        prod_ref[i * TILE : (i + 1) * TILE] = prods
        grad_ref[i * TILE : (i + 1) * TILE] = grads
        prod, grad = prods[0:1], grads[0:1]
    run[0:1] = prod
    run[1:2] = grad
    first_ref[0:1] = decays[0:1] * prod
    first_ref[1:2] = decays[0:1] * grad


def gates_kernel(
    prod_ref, grad_ref, in_ref, prev_ref, state_in_ref, states_ref, decay_ref, pre_ref, conv_ref,
    inner_ref, inner_prev_ref, halo_ref, mask_ref, par_ref, wg_ref,
    low_ref, inner_grad_ref, edge_ref, sums_ref, ext, later,
):
    rows, width = prod_ref.shape
    step = pl.program_id(0)
    at_start = step == pl.num_programs(0) - 1

    @pl.when(step == 0)
    def _():
        sums_ref[...] = jnp.zeros_like(sums_ref)
        later[...] = jnp.zeros_like(later)

    mask = mask_ref[...]
    starts = mask[:, CONV - 1 : CONV] > 0.5
    drive_grad = grad_ref[...] + prod_ref[...] * in_ref[...]
    ext[TILE : TILE + rows] = states_ref[...]
    ext[TILE - 1 : TILE] = jnp.where(at_start, state_in_ref[...], prev_ref[TILE - 1 : TILE])
    prev_states = ext[TILE - 1 : TILE - 1 + rows]
    rate = sigmoid(pre_ref[:, :width])
    gate = sigmoid(pre_ref[:, width:])
    conv = conv_ref[...].astype(F32)
    slope = par_ref[CONV + 1 : CONV + 2]
    log_rate = slope * rate
    decays = decay_ref[...]
    raw = jnp.sqrt(neg_expm1(2.0 * log_rate))
    scale = jnp.where(starts, 1.0, raw)
    scale_grad = drive_grad * gate * conv
    log_grad = jnp.where(
        starts, 0.0, drive_grad * prev_states * decays - scale_grad * (decays * decays) / raw
    )
    rate_low = (log_grad * slope * rate * (1.0 - rate)).astype(BF16)
    input_low = (drive_grad * scale * conv * gate * (1.0 - gate)).astype(BF16)
    low_ref[:, :width] = rate_low
    low_ref[:, width:] = input_low
    both = jnp.concatenate([rate_low, input_low], axis=1)
    conv_grad = drive_grad * scale * gate + lax.dot_general(
        both, wg_ref[...], (((1,), (1,)), ((), ())), preferred_element_type=F32
    )
    inner = inner_ref[...].astype(BF16).astype(F32)
    before = jnp.where(at_start, halo_ref[...].astype(F32), inner_prev_ref[...].astype(BF16).astype(F32))
    ext[0:TILE] = before
    ext[TILE : TILE + rows] = inner

    def total(values):
        return jnp.sum(values, axis=0, keepdims=True)

    sums_ref[0:1] += total(conv_grad * inner)
    sums_ref[CONV : CONV + 1] += total(conv_grad)
    sums_ref[CONV + 1 : CONV + 2] += total(log_grad * rate)
    sums_ref[CONV + 2 : CONV + 3] += total(rate_low.astype(F32))
    sums_ref[CONV + 3 : CONV + 4] += total(input_low.astype(F32))
    inner_grad = par_ref[0:1] * conv_grad
    heads = []
    for k in range(1, CONV):
        masked = conv_grad * mask[:, k - 1 : k]
        sums_ref[k : k + 1] += total(masked * ext[TILE - k : TILE - k + rows])
        heads.append(masked[0:TILE] * par_ref[k : k + 1])
    for k in range(1, CONV):
        masked = par_ref[k : k + 1] * (conv_grad * mask[:, k - 1 : k])
        ext[0:rows] = masked
        ext[rows : rows + TILE] = later[k - 1]
        inner_grad = inner_grad + ext[k : k + rows]
        later[k - 1] = heads[k - 1]
    inner_grad_ref[...] = inner_grad.astype(inner_grad_ref.dtype)

    @pl.when(at_start)
    def _():
        edge_ref[...] = jnp.zeros_like(edge_ref)
        for back in range(1, CONV):
            row = heads[back - 1][0:1]
            for k in range(back + 1, CONV):
                row = row + heads[k - 1][k - back : k - back + 1]
            edge_ref[TILE - back : TILE - back + 1] = row


def rows_spec(rows, width, parts, column=0, reverse=False):
    return pl.BlockSpec((rows, width), lambda step: (parts - 1 - step if reverse else step, column))


def before_spec(rows, width, parts, column=0):
    tiles = rows // TILE
    return pl.BlockSpec(
        (TILE, width), lambda step: (jnp.maximum(parts - 2 - step, 0) * tiles + tiles - 1, column)
    )


def whole_spec(shape):
    return pl.BlockSpec(shape, lambda step: (0,) * len(shape))


def dot_nt(left, right):
    return lax.dot_general(left, right, (((1,), (1,)), ((), ())), preferred_element_type=F32)


def dot_tn(left, right):
    return lax.dot_general(left, right, (((0,), (0,)), ((), ())), preferred_element_type=F32)


COSTS = (
    0.2, 3, 0.2, 6, 6, 7, 7, 5.7, 5.7, 3, 3, 27, 27, 3.4, 21, 60, 0.01, 0.01, 7.5, 7.5, 6, 7, 8, 40.0, 40.0, 0.01, 0.01, 0.01, 0.01, 0.01, 0.01, 0.01, 0.01, 0.01, 3, 10000.0, 1, 3,
)


class Clock:
    def __init__(self):
        self.tick = jnp.zeros((TILE, 128), F32)
        self.calls = 0

    def call(self, kernel, grid, operands, in_specs, out_specs, out_shape, scratch=(), after=(), cost=3.0):
        cost = COSTS[self.calls] if self.calls < len(COSTS) else cost
        self.calls += 1
        count, extra, outs = len(operands), len(after) + 1, len(out_shape)

        def body(*refs):
            given, refs = refs[:count], refs[count + extra :]
            kernel(*given, *refs[:outs], *refs[outs + 1 :])
            refs[outs][...] = jnp.zeros_like(refs[outs])

        whole = pl.BlockSpec((TILE, 128), lambda *step: (0, 0))
        *results, self.tick = pl.pallas_call(
            body,
            out_shape=list(out_shape) + [jax.ShapeDtypeStruct((TILE, 128), F32)],
            grid=grid,
            in_specs=list(in_specs) + [pl.BlockSpec(memory_space=pl.ANY)] * extra,
            out_specs=list(out_specs) + [whole],
            scratch_shapes=list(scratch),
            cost_estimate=pl.CostEstimate(flops=int(cost * RATE), bytes_accessed=int(cost * RATE), transcendentals=0),
        )(*operands, *after, self.tick)
        return results


def shape(dims, dtype):
    return jax.ShapeDtypeStruct(dims, dtype)


def held(array):
    dims = array.shape
    return pl.BlockSpec(dims, lambda *step: (0,) * len(dims), pipeline_mode=pl.Buffered(1))


def kept(dims):
    return pl.BlockSpec(dims, lambda *step: (0,) * len(dims))


def place_spec():
    return pl.BlockSpec(memory_space=pltpu.SMEM)


def spread(copies, apart):
    if not apart:
        return [lax.all_to_all(copies, "tensor", split_axis=0, concat_axis=0, tiled=True)]
    return [copies] + [shift(copies, "tensor", k) for k in range(1, lax.axis_size("tensor"))]


def gathered_sums(parts):
    if len(parts) == 1:
        return [lax.all_to_all(parts[0], "tensor", split_axis=0, concat_axis=0, tiled=True)]
    return [parts[0]] + [shift(parts[k], "tensor", k) for k in range(1, len(parts))]


def assemble(refs, wide_ref):
    place, blocks = refs[0], refs[1:]
    if len(blocks) == 1:
        wide_ref[...] = blocks[0][...]
        return
    rows = blocks[0].shape[0]
    for k, block in enumerate(blocks):
        owner = lax.rem(place[0] - k + len(blocks), len(blocks))
        wide_ref[pl.ds(pl.multiple_of(owner * rows, 2 * TILE), rows)] = block[...]


def deal(values, place, outs, work):
    if len(outs) == 1:
        outs[0][...] = values.astype(BF16)
        return
    work[...] = values
    rows = outs[0].shape[0]
    for k, out in enumerate(outs):
        owner = lax.rem(place[0] + k, len(outs))
        out[...] = work[pl.ds(pl.multiple_of(owner * rows, 2 * TILE), rows)].astype(BF16)


def added(refs, rows):
    if len(refs) == 1:
        count = refs[0].shape[0] // rows
        terms = [refs[0][k * rows : (k + 1) * rows].astype(F32) for k in range(count)]
    else:
        terms = [ref[...].astype(F32) for ref in refs]
    return sum(terms[1:], terms[0])


def repeat_to(ref, values, rows):
    for k in range(ref.shape[0] // rows):
        ref[k * rows : (k + 1) * rows] = values


def mean_of(values):
    return jnp.mean(values, axis=-1, keepdims=True)


def first_kernel(x_ref, gain_ref, out_ref):
    x = x_ref[...].astype(F32)
    repeat_to(out_ref, (x * lax.rsqrt(mean_of(x * x) + EPS) * gain_ref[...]).astype(BF16), x_ref.shape[0])


def first(clock, x, gain, copies):
    rows, model = x.shape
    return clock.call(
        first_kernel, (1,), [x, gain], [held(x), held(gain)],
        [kept((copies * rows, model))], [shape((copies * rows, model), BF16)],
        cost=0.2,
    )[0]


def copies_kernel(*refs):
    out_ref = refs[-1]
    rows = refs[0].shape[0]
    for k in range(out_ref.shape[0] // rows):
        out_ref[k * rows : (k + 1) * rows] = refs[k % (len(refs) - 1)][...]


def all_copies(clock, arrays, copies, after):
    rows, model = arrays[0].shape
    total = rows * len(arrays) * copies
    return clock.call(
        copies_kernel, (1,), arrays, [held(a) for a in arrays], [kept((total, model))],
        [shape((total, model), BF16)], after=after,
        cost=3.0,
    )[0]


def project_kernel(many, *refs):
    blocks, (weight_ref, wide_ref, out_ref, halo_ref) = refs[: many + 1], refs[many + 1 :]

    @pl.when(pl.program_id(0) == 0)
    def _():
        assemble(blocks, wide_ref)

    value = jnp.dot(wide_ref[...], weight_ref[...], preferred_element_type=F32)
    out_ref[...] = value

    @pl.when(pl.program_id(0) == pl.num_programs(0) - 1)
    def _():
        halo_ref[...] = value[value.shape[0] - TILE :].astype(BF16)


def project(clock, place, blocks, weight, cols, after=()):
    model = weight.shape[0]
    rows = sum(block.shape[0] for block in blocks)
    width = cols // 2
    return clock.call(
        partial(project_kernel, len(blocks)), (2,), [place, *blocks, weight],
        [place_spec()] + [held(b) for b in blocks] + [pl.BlockSpec((model, width), lambda j: (0, j))],
        [kept((rows, model)), pl.BlockSpec((rows, width), lambda j: (0, j)), kept((TILE, width))],
        [shape((rows, model), BF16), shape((rows, cols), F32), shape((TILE, width), BF16)], after=after,
        cost=6.0,
    )


def mix_kernel(outs, place_ref, local_ref, prod_ref, in_ref, branch_ref, weight_ref, *refs):
    states_ref, mixed_ref = refs[:2]

    @pl.when(pl.program_id(0) == 0)
    def _():
        states = local_ref[...] + prod_ref[...] * in_ref[...]
        states_ref[...] = states
        mixed_ref[...] = (states * gelu_parts(branch_ref[...])[0]).astype(BF16)

    value = dot_nt(mixed_ref[...], weight_ref[...])
    deal(value, place_ref, refs[2 : 2 + outs], refs[-1])


def part_specs(rows, cols, tile, outs):
    return (
        [pl.BlockSpec((rows // outs, tile), lambda j: (0, j))] * outs,
        [shape((rows // outs, cols), BF16)] * outs,
        pltpu.VMEM((rows, tile), F32),
    )


def mix_out(clock, place, local, prods, state_in, both_pre, weight, outs, tile, after=()):
    rows, width = local.shape
    cols = weight.shape[0]
    part_spec, part_shape, work = part_specs(rows, cols, tile, outs)
    results = clock.call(
        partial(mix_kernel, outs), (cols // tile,), [place, local, prods, state_in, both_pre, weight],
        [place_spec(), held(local), held(prods), held(state_in),
         pl.BlockSpec((rows, width), lambda j: (0, 0), pipeline_mode=pl.Buffered(1)),
         pl.BlockSpec((tile, width), lambda j: (j, 2))],
        [kept((rows, width)), kept((rows, width))] + part_spec,
        [shape((rows, width), F32), shape((rows, width), BF16)] + part_shape, [work], after,
        cost=5.7,
    )
    return results[0], results[1], results[2:]


def second_kernel(x_ref, gain_ref, *refs):
    terms, (resid_ref, out_ref) = refs[:-2], refs[-2:]
    rows = x_ref.shape[0]
    resid = x_ref[...].astype(F32) + added(terms, rows)
    resid_ref[...] = resid
    repeat_to(out_ref, (resid * lax.rsqrt(mean_of(resid * resid) + EPS) * gain_ref[...]).astype(BF16), rows)


def second(clock, x, gain, terms, copies, after=()):
    rows, model = x.shape
    return clock.call(
        second_kernel, (1,), [x, gain, *terms], [held(x), held(gain)] + [held(t) for t in terms],
        [kept((rows, model)), kept((copies * rows, model))],
        [shape((rows, model), F32), shape((copies * rows, model), BF16)],
        after=after,
        cost=3.0,
    )


def mlp_kernel(two_many, turn, turns, unit, outs, *refs):
    two_blocks, refs = refs[: two_many + 1], refs[two_many + 1 :]
    cot_all, gate_ref, up_ref, down_ref, two_ref, cot_ref, hidden_ref, pair_ref = refs[:8]
    parts, acc = refs[8 : 8 + outs], refs[-1]
    step = pl.program_id(0)

    @pl.when(step == 0)
    def _():
        assemble(two_blocks, two_ref)
        rows = unit
        for k in range(two_ref.shape[0] // rows):
            start = (k * turns + turn) * rows
            cot_ref[k * rows : (k + 1) * rows] = cot_all[start : start + rows]

    two = two_ref[...]
    gate_w, up_w = gate_ref[...], up_ref[...]
    gate_val, gate_slope = gelu_parts(jnp.dot(two, gate_w, preferred_element_type=F32))
    up_pre = jnp.dot(two, up_w, preferred_element_type=F32)
    hidden_ref[...] = (gate_val * up_pre).astype(BF16)
    hidden_grad = jnp.dot(cot_ref[...], down_ref[...], preferred_element_type=F32)
    gate_low = (hidden_grad * up_pre * gate_slope).astype(BF16)
    up_low = (hidden_grad * gate_val).astype(BF16)
    pair_ref[0] = gate_low
    pair_ref[1] = up_low
    term = dot_nt(gate_low, gate_w) + dot_nt(up_low, up_w)

    @pl.when(step == 0)
    def _():
        acc[...] = term

    @pl.when(step > 0)
    def _():
        acc[...] += term

    @pl.when(step == pl.num_programs(0) - 1)
    def _():
        rows = parts[0].shape[0]
        for k, out in enumerate(parts):
            start = 0 if outs == 1 else pl.multiple_of(lax.rem(two_blocks[0][0] + k, outs) * rows, 2 * TILE)
            out[...] = acc[pl.ds(start, rows)].astype(BF16)


def mlp(clock, place, two_blocks, cot_all, turn, turns, unit, weight, outs, tile, after=()):
    model, units = weight.shape[0], weight.shape[1] // 3
    rows = sum(block.shape[0] for block in two_blocks)
    steps = units // tile
    results = clock.call(
        partial(mlp_kernel, len(two_blocks), turn, turns, unit, outs), (steps,),
        [place, *two_blocks, cot_all, weight, weight, weight],
        [place_spec()] + [held(b) for b in two_blocks + [cot_all]]
        + [pl.BlockSpec((model, tile), lambda j: (0, j)), pl.BlockSpec((model, tile), lambda j: (0, steps + j)),
           pl.BlockSpec((model, tile), lambda j: (0, 2 * steps + j))],
        [kept((rows, model)), kept((rows, model)), pl.BlockSpec((rows, tile), lambda j: (0, j)),
         pl.BlockSpec((2, rows, tile), lambda j: (0, 0, j))] + [kept((rows // outs, model))] * outs,
        [shape((rows, model), BF16), shape((rows, model), BF16), shape((rows, units), BF16),
         shape((2, rows, units), BF16)] + [shape((rows // outs, model), BF16)] * outs,
        [pltpu.VMEM((rows, model), F32)], after,
        cost=27.0,
    )
    return *results[:4], results[4:]


def down_kernel(count, unit, *refs):
    right, out_ref = refs[count], refs[-1]
    for i in range(count):
        value = dot_nt(refs[i][...], right[...]).astype(BF16)
        for k in range(value.shape[0] // unit):
            start = (k * count + i) * unit
            out_ref[start : start + unit] = value[k * unit : (k + 1) * unit]


def down_out(clock, lefts, right, unit, tile):
    cols, depth = right.shape[0], lefts[0].shape[1]
    count = len(lefts)
    total = count * lefts[0].shape[0]
    return clock.call(
        partial(down_kernel, count, unit), (cols // tile,), [*lefts, right],
        [held(a) for a in lefts] + [pl.BlockSpec((tile, depth), lambda j: (j, 2))],
        [pl.BlockSpec((total, tile), lambda j: (0, j))], [shape((total, cols), BF16)],
        cost=0.01,
    )[0]


def norm_grad(values, grad, gain):
    inv = lax.rsqrt(mean_of(values * values) + EPS)
    unit = values * inv
    scaled = grad * gain
    return inv * (scaled - unit * mean_of(scaled * unit)), grad * unit


def third_kernel(resid_ref, cot_ref, gain_ref, *refs):
    terms, (grad_ref, low_ref, sum_ref) = refs[:-3], refs[-3:]
    rows = resid_ref.shape[0]
    grad = added(terms, rows).astype(BF16).astype(F32)
    term, product = norm_grad(resid_ref[...], grad, gain_ref[...])
    total = cot_ref[...].astype(F32) + term
    grad_ref[...] = total
    sum_ref[...] = jnp.sum(product, axis=0, keepdims=True)
    repeat_to(low_ref, total.astype(BF16), rows)


def third(clock, resid, cot, gain, terms, copies, cost):
    rows, model = resid.shape
    return clock.call(
        third_kernel, (1,), [resid, cot, gain, *terms], [held(resid), held(cot), held(gain)] + [held(t) for t in terms],
        [kept((rows, model)), kept((copies * rows, model)), kept((1, model))],
        [shape((rows, model), F32), shape((copies * rows, model), BF16), shape((1, model), F32)],
        cost=cost,
    )


def back_kernel(outs, place_ref, branch_ref, inner_ref, edge_ref, weight_ref, one_ref, *refs):
    low_ref, gain_ref = refs[:2]
    both_ref, work = refs[-2:]
    rows, width = branch_ref.shape

    @pl.when(pl.program_id(0) == 0)
    def _():
        both_ref[:, :width] = branch_ref[...]
        both_ref[: rows - 2 * TILE, width:] = inner_ref[: rows - 2 * TILE].astype(BF16)
        last = inner_ref[rows - 2 * TILE :]
        fixed = jnp.concatenate([last[:TILE], last[TILE:] + edge_ref[...]], axis=0)
        both_ref[rows - 2 * TILE :, width:] = fixed.astype(BF16)
        low_ref[...] = both_ref[:, width:]

    value = dot_nt(both_ref[...], weight_ref[...])
    gain_ref[...] = jnp.sum(value * one_ref[...].astype(F32), axis=0, keepdims=True)
    deal(value, place_ref, refs[2 : 2 + outs], work)


def back_one(clock, place, branch_low, inner_grad, edge_in, weight, wide_one, outs, tile):
    rows, width = branch_low.shape
    model = weight.shape[0]
    part_spec, part_shape, work = part_specs(rows, model, tile, outs)
    results = clock.call(
        partial(back_kernel, outs), (model // tile,), [place, branch_low, inner_grad, edge_in, weight, wide_one],
        [place_spec(), held(branch_low), held(inner_grad), held(edge_in),
         pl.BlockSpec((tile, 2 * width), lambda j: (j, 0)), pl.BlockSpec((rows, tile), lambda j: (0, j))],
        [kept((rows, width)), pl.BlockSpec((1, tile), lambda j: (0, j))] + part_spec,
        [shape((rows, width), BF16), shape((1, model), F32)] + part_shape,
        [pltpu.VMEM((rows, 2 * width), BF16), work],
        cost=6.2,
    )
    return results[0], results[1], results[2:]


def last_kernel(x_ref, resid_ref, gain_ref, *refs):
    terms, out_ref = refs[:-1], refs[-1]
    grad = added(terms, x_ref.shape[0]).astype(BF16).astype(F32)
    out_ref[...] = resid_ref[...] + norm_grad(x_ref[...].astype(F32), grad, gain_ref[...])[0]


def last(clock, x, resid_grad, gain, terms, cost):
    return clock.call(
        last_kernel, (1,), [x, resid_grad, gain, *terms],
        [held(x), held(resid_grad), held(gain)] + [held(t) for t in terms],
        [kept(resid_grad.shape)], [shape(resid_grad.shape, F32)], cost=cost,
    )[0]


def out_kernel(count, *refs):
    terms, outs = refs[count], refs[count + 1 :]
    rows = refs[0].shape[0]
    for i in range(count):
        total = refs[i][...]
        for k in range(terms.shape[0] // (count * rows)):
            start = (k * count + i) * rows
            total = total + terms[start : start + rows].astype(F32)
        outs[i][...] = total.astype(BF16)


def block_results(clock, residuals, terms):
    count = len(residuals)
    dims = residuals[0].shape
    return clock.call(
        partial(out_kernel, count), (1,), [*residuals, terms], [held(r) for r in residuals] + [held(terms)],
        [kept(dims)] * count, [shape(dims, BF16)] * count,
        cost=3.0,
    )


def stack_rows(refs):
    return jnp.concatenate(refs, axis=0) if len(refs) > 1 else refs[0]


def term_kernel(count, *refs):
    halved = len(refs[count].shape) == 3
    left = stack_rows([refs[i][...] for i in range(count)])
    right = stack_rows([refs[count + i][0] if halved else refs[count + i][...] for i in range(count)])
    refs[-1][...] = dot_tn(left, right).astype(refs[-1].dtype)


def weight_term(clock, lefts, rights, tile, cost, after=()):
    count = len(lefts)
    rows, depth = lefts[0].shape
    halves = rights[0].shape[0] if rights[0].ndim == 3 else 1
    cols = rights[0].shape[-1]
    if halves == 1:
        grid, left_at, out_at = (depth // tile,), (lambda j: (0, j)), (lambda j: (j, 0))
        right_spec = held(rights[0])
    else:
        grid, left_at, out_at = (halves, depth // tile), (lambda h, j: (0, j)), (lambda h, j: (j, h))
        right_spec = pl.BlockSpec((1, rows, cols), lambda h, j: (h, 0, 0))
    return clock.call(
        partial(term_kernel, count), grid, [*lefts, *rights],
        [pl.BlockSpec((rows, tile), left_at)] * count + [right_spec] * count,
        [pl.BlockSpec((tile, cols), out_at)], [shape((depth, halves * cols), BF16)], after=after,
        cost=cost,
    )[0]


def diagonal_kernel(count, cells, *refs):
    out_ref, work = refs[-2:]
    total = None
    for i in range(count):
        value = dot_tn(refs[i][...], refs[count + i][...])
        total = value if total is None else total + value
    work[...] = total
    cell = out_ref.shape[1]
    for i in range(cells):
        for h in range(2):
            col = (h * cells + i) * cell
            out_ref[h * cells + i] = work[i * cell : (i + 1) * cell, col : col + cell].astype(BF16)


def diagonal_terms(clock, lefts, rights, cells):
    count = len(lefts)
    width = lefts[0].shape[1]
    cell = width // cells
    return clock.call(
        partial(diagonal_kernel, count, cells), (1,), [*lefts, *rights],
        [held(a) for a in lefts] + [held(a) for a in rights],
        [kept((2 * cells, cell, cell))], [shape((2 * cells, cell, cell), BF16)],
        [pltpu.VMEM((width, 2 * width), F32)],
        cost=4.5,
    )[0]


def split_term_kernel(count, groups, unit, place_ref, *refs):
    k, c = pl.program_id(0), pl.program_id(1)
    owner = lax.rem(place_ref[0] + k, groups) * pl.num_programs(1) + c
    start = pl.multiple_of(owner * unit, unit)
    left = stack_rows([refs[i][:, pl.ds(start, unit)] for i in range(count)])
    total = dot_tn(left, stack_rows([refs[count + i][...] for i in range(count)])).astype(BF16)
    for g in range(groups):
        @pl.when(k == g)
        def _(g=g):
            refs[2 * count + g][...] = total


def split_term(clock, place, lefts, rights, groups, steps, cost, after=()):
    count = len(lefts)
    depth = lefts[0].shape[1]
    cols = rights[0].size // rights[0].shape[-2]
    unit = depth // (groups * steps)

    def spec(g):
        return pl.BlockSpec(
            (unit, cols), lambda k, c: (jnp.where(k < g, 0, jnp.where(k > g, steps - 1, c)), 0)
        )

    parts = clock.call(
        partial(split_term_kernel, count, groups, unit), (groups, steps), [place, *lefts, *rights],
        [place_spec()] + [held(a) for a in lefts] + [held(a) for a in rights],
        [spec(g) for g in range(groups)], [shape((unit * steps, cols), BF16)] * groups, after=after, cost=cost,
    )
    return [parts[0]] + [shift(parts[k], "fsdp", k) for k in range(1, groups)]


def member_kernel(groups, *refs):
    out_ref = refs[-1]
    col = 0
    for i in range(0, len(refs) - 1, groups):
        total = added(refs[i : i + groups], refs[i].shape[0])
        out_ref[:, col : col + total.shape[1]] = total.astype(BF16)
        col += total.shape[1]


def member_sums(clock, terms, cost=8.0):
    flat = [t for some in terms for t in some]
    rows, cols = flat[0].shape[0], sum(some[0].shape[1] for some in terms)
    tile = rows // 4
    added_up = clock.call(
        partial(member_kernel, len(terms[0])), (4,), flat,
        [pl.BlockSpec((tile, t.shape[1]), lambda j: (j, 0)) for t in flat],
        [pl.BlockSpec((tile, cols), lambda j: (j, 0))], [shape((rows, cols), BF16)], cost=cost,
    )[0]
    return lax.psum_scatter(added_up, "context", scatter_dimension=0, tiled=True)


def turned_kernel(cuts, in_ref, *outs):
    total = in_ref[...].astype(F32)
    col = 0
    for out, turned in zip(outs, cuts):
        step = out.shape[0] if turned else out.shape[1]
        piece = total[:, col : col + step]
        out[...] = piece.T if turned else piece
        col += step


def turned_pieces(clock, low, cuts):
    rows = low.shape[0]
    dims = [(cols, rows) if turned else (rows, cols) for cols, turned in cuts]
    return clock.call(
        partial(turned_kernel, [turned for _, turned in cuts]), (1,), [low], [held(low)], [kept(d) for d in dims],
        [shape(d, F32) for d in dims], cost=3.0,
    )


def sum_kernel(*refs):
    refs[-1][...] = added(refs[:-1], refs[0].shape[0]).astype(refs[-1].dtype)


def sum_of(clock, arrays, dtype):
    dims = arrays[0].shape
    return clock.call(
        sum_kernel, (1,), arrays, [held(a) for a in arrays], [kept(dims)], [shape(dims, dtype)], cost=1.0,
    )[0]


def everyone(value, axis):
    return [value] + [shift(value, axis, k) for k in range(1, lax.axis_size(axis))]


def forward_scan(clock, both_pre, halo, mask, params, gate_w, parts):
    total, width = both_pre.shape[0], params.shape[1]
    rows = total // parts
    spec = partial(rows_spec, rows, width, parts)
    return clock.call(
        forward_kernel, (parts,), [both_pre, halo, mask, params, gate_w],
        [spec(column=1), held(halo), rows_spec(rows, mask.shape[1], parts), held(params), held(gate_w)],
        [spec(), rows_spec(rows, 2 * width, parts), spec(), spec(), spec(), kept((2, width))],
        [shape((total, width), BF16), shape((total, 2 * width), F32), shape((total, width), F32),
         shape((total, width), F32), shape((total, width), F32), shape((2, width), F32)],
        [pltpu.VMEM((rows + TILE, width), F32), pltpu.VMEM((TILE, width), F32)],
        cost=7.0,
    )


def reverse_scan(clock, place, blocks, out_w, both_pre, states, decays, parts, after=()):
    total, width = states.shape
    rows = total // parts
    model = out_w.shape[0]
    spec = rows_spec(rows, width, parts, reverse=True)
    return clock.call(
        partial(reverse_kernel, len(blocks)), (parts,), [place, *blocks, out_w, both_pre, states, decays],
        [place_spec()] + [held(b) for b in blocks] + [pl.BlockSpec((model, width), lambda step: (0, 2), pipeline_mode=pl.Buffered(1)), spec, spec, spec],
        [kept((total, model)), spec, spec, spec, kept((2, width))],
        [shape((total, model), BF16), shape((total, width), BF16), shape((total, width), F32),
         shape((total, width), F32), shape((2, width), F32)],
        [pltpu.VMEM((total, width), F32), pltpu.VMEM((rows + TILE, width), F32), pltpu.VMEM((TILE, width), F32)],
        after,
        cost=7.5,
    )


def gates_back(clock, prods, grads, grad_in, states, state_in, decays, pre, conv_low, both_pre, halo, mask,
               params, gate_w, parts):
    total, width = states.shape
    rows = total // parts
    spec = partial(rows_spec, rows, width, parts, reverse=True)
    return clock.call(
        gates_kernel, (parts,),
        [prods, grads, grad_in, states, state_in, states, decays, pre, conv_low, both_pre, both_pre, halo, mask,
         params, gate_w],
        [spec(), spec(), held(grad_in), before_spec(rows, width, parts), held(state_in),
         spec(), spec(), rows_spec(rows, 2 * width, parts, reverse=True), spec(), spec(column=1),
         before_spec(rows, width, parts, column=1), held(halo),
         rows_spec(rows, mask.shape[1], parts, reverse=True), held(params), held(gate_w)],
        [rows_spec(rows, 2 * width, parts, reverse=True), spec(), kept((TILE, width)), kept((TILE, width))],
        [shape((total, 2 * width), BF16), shape((total, width), F32), shape((TILE, width), F32),
         shape((TILE, width), F32)],
        [pltpu.VMEM((rows + TILE, width), F32), pltpu.VMEM((CONV - 1, TILE, width), F32)],
        cost=8.5,
    )


def carry_over(ends, direction):
    size = lax.axis_size("context")
    incoming = jnp.zeros_like(ends[1:2])
    parts = [step_by(ends, "context", direction * k) for k in range(1, size)]
    for part in reversed(parts):
        incoming = part[1:2] + part[0:1] * incoming
    return incoming


def carry_all(ends, direction):
    stacked = jnp.concatenate([e[:1] for e in ends] + [e[1:] for e in ends], axis=0)
    count = len(ends)
    incoming = jnp.zeros_like(stacked[:count])
    for part in reversed([step_by(stacked, "context", direction * k) for k in range(1, lax.axis_size("context"))]):
        incoming = part[count:] + part[:count] * incoming
    return [incoming[i : i + 1] for i in range(count)]


def block_diagonal(weight):
    count, rows, cols = weight.shape
    return jnp.concatenate(
        [jnp.pad(weight[i], ((0, 0), (i * cols, (count - 1 - i) * cols))) for i in range(count)], axis=0
    )


def per_device(
    inputs, segments, norm_gain, branch_weight, inner_weight, conv_weight, conv_bias, rate_weight, rate_bias,
    input_weight, input_bias, decay_param, out_weight, mlp_gain, gate_weight, up_weight, down_weight, cotangent,
):
    micro, seqs, rows, model = inputs.shape
    parts = lax.axis_size("tensor")
    span = rows * parts
    width = conv_bias.shape[0]
    blocks = rate_weight.shape[0]
    units = gate_weight.shape[1]
    chains = [(m, s) for m in range(micro) for s in range(seqs)]
    context_pos = lax.axis_index("context")
    owners = ("fsdp", "context")

    first_w = lax.all_gather(
        jnp.concatenate([branch_weight, inner_weight, out_weight.T], 1), owners, axis=0, tiled=True
    )
    second_w = lax.all_gather(
        jnp.concatenate([gate_weight, up_weight, down_weight.T], 1), owners, axis=0, tiled=True
    )
    gate_w = jnp.concatenate([block_diagonal(rate_weight), block_diagonal(input_weight)], axis=1)
    slope = -CPOW * jax.nn.softplus(-decay_param)
    params = jnp.concatenate(
        [conv_weight, conv_bias[None], slope[None], rate_bias[None], input_bias[None]], axis=0
    )

    def masks_of(row):
        pad = jnp.concatenate([jnp.full((CONV - 1,), -1, jnp.int32), row])
        ext = lax.dynamic_slice_in_dim(pad, context_pos * span, span + CONV - 1)
        own = ext[CONV - 1 :]
        cols = [(ext[CONV - 1 - k : CONV - 1 - k + span] == own).astype(F32) for k in range(1, CONV)]
        return jnp.stack(cols + [1.0 - cols[0]], axis=1)

    count = len(chains)
    turns = range(count)
    apart = [i % 2 == 1 for i in turns]
    copies = [1 if a else parts for a in apart]
    outs = [parts if a else 1 for a in apart]
    place = lax.axis_index("tensor").reshape(1).astype(jnp.int32)
    x_rows = [inputs[m, s] for m, s in chains]
    cot_rows = [cotangent[m, s] for m, s in chains]
    gain_one_row, gain_two_row = norm_gain[None], mlp_gain[None]
    mask = [masks_of(segments[m, s]) for m, s in chains]
    clock = Clock()

    groups, members = lax.axis_size("fsdp"), lax.axis_size("context")
    group_place = lax.axis_index("fsdp").reshape(1).astype(jnp.int32)
    normed = [first(clock, x_rows[0], gain_one_row, copies[0])]
    cot_copies = all_copies(clock, cot_rows, parts, (gate_w, params, *mask))
    normed += [first(clock, x_rows[i], gain_one_row, copies[i]) for i in turns if i]
    one_blocks = [spread(normed[i], apart[i]) for i in turns]
    (cot_all,) = spread(cot_copies, False)
    projections, halo, scans, mixes, ends_in = [], [], [], [], []

    def start_chain(i):
        projections.append(project(clock, place, one_blocks[i], first_w, 2 * width))
        halo.append(step_by(projections[i][2], "context", 1))

    def scan_chain(i):
        scans.append(forward_scan(clock, projections[i][1], halo[i], mask[i], params, gate_w, parts))
        ends_in.append(carry_over(scans[i][5], 1))

    def mix_chain(i):
        mixes.append(mix_out(
            clock, place, scans[i][4], scans[i][3], ends_in[i], projections[i][1], first_w, outs[i], 512,
            () if i else (cot_all,),
        ))

    for step in (start_chain, scan_chain, mix_chain):
        for i in turns:
            step(i)
    wide_one, both_pre, tails = map(list, zip(*projections))
    conv_low, pre, decays, prods, locals_, ends = map(list, zip(*scans))
    state_in = ends_in
    states, mixed_low, out_part = map(list, zip(*mixes))
    out_terms = [gathered_sums(p) for p in out_part]
    residual, two_blocks = [], []
    for i in turns:
        res, low = second(clock, x_rows[i], gain_two_row, out_terms[i], copies[i], two_blocks[-1] if i else out_terms[-1])
        residual.append(res)
        two_blocks.append(spread(low, apart[i]))
    mlps = [
        mlp(clock, place, two_blocks[i], cot_all, i, count, rows, second_w, outs[i], 256) for i in turns
    ]
    wide_two, wide_cot, hidden_low, pair_low, two_part = map(list, zip(*mlps))
    two_terms = [gathered_sums(p) for p in two_part]

    thirds = []
    for i in turns:
        thirds.append(third(
            clock, residual[i], cot_rows[i], gain_two_row, two_terms[i], copies[i], 60.0 if i else 3.4
        ))
        if i == 0:
            pair_grad = lax.psum_scatter(
                weight_term(clock, wide_two, pair_low, 512, 21.0), owners, scatter_dimension=0, tiled=True
            )
    resid_grad, resid_low, gain_two = map(list, zip(*thirds))
    resid_blocks = [spread(resid_low[i], apart[i]) for i in turns]
    down_split = split_term(clock, group_place, wide_cot, hidden_low, groups, 2, 0.01)
    (down_terms,) = gathered_sums([down_out(clock, hidden_low, second_w, rows, 512)])

    reversed_ = [
        reverse_scan(clock, place, resid_blocks[i], first_w, both_pre[i], states[i], decays[i], parts) for i in turns
    ]
    wide_resid, branch_low, rev_prods, rev_grads, ends_back = map(list, zip(*reversed_))
    grad_in = carry_all(ends_back, -1)
    branch_split = split_term(clock, group_place, wide_one, branch_low, groups, 1, 6.0)
    out_split = split_term(clock, group_place, wide_resid, mixed_low, groups, 1, 7.0)
    early = member_sums(clock, [down_split, branch_split], 8.0)
    backs = [
        gates_back(
            clock, rev_prods[i], rev_grads[i], grad_in[i], states[i], state_in[i], decays[i], pre[i], conv_low[i],
            both_pre[i], halo[i], mask[i], params, gate_w, parts,
        )
        for i in turns
    ]
    gates_low, inner_grad, edge, sums = map(list, zip(*backs))
    gate_grad, up_grad = turned_pieces(clock, pair_grad, [(units, False), (units, False)])
    edges = step_by(jnp.concatenate(edge, axis=0), "context", -1)
    edge_in = [edges[i * TILE : (i + 1) * TILE] for i in turns]
    gate_blocks = diagonal_terms(clock, conv_low, gates_low, blocks)
    ones = []
    for i in turns:
        ones.append(back_one(
            clock, place, branch_low[i], inner_grad[i], edge_in[i], first_w, wide_one[i], 1 if i else parts, 512
        ))
        if i == 0:
            block_out = block_results(clock, residual, down_terms)
    inner_low, gain_one, one_part = map(list, zip(*ones))
    one_terms = [gathered_sums(p) for p in one_part]
    inner_split = split_term(clock, group_place, wide_one, inner_low, groups, 1, 8.0)
    gains = sum_over(jnp.concatenate([sum(gain_one) / gain_one_row, sum(gain_two)]), "tensor")
    small = jnp.concatenate([sum(sums).reshape(-1), gains.reshape(-1)]).astype(BF16)
    cells, side = gate_blocks.shape[0], gate_blocks.shape[2]
    extra = -(-small.size // (cells * side * 2 * TILE)) * 2 * TILE
    small = jnp.pad(small, (0, cells * extra * side - small.size)).reshape(cells, extra, side)
    packed_all = everyone(jnp.concatenate([gate_blocks, small], axis=1), "fsdp")
    late = member_sums(clock, [out_split, inner_split], 3.0)
    packed = sum_of(clock, packed_all, BF16)
    packed_all = everyone(packed, "context")
    input_grad = [last(clock, x_rows[i], resid_grad[i], gain_one_row, one_terms[i], 3.0) for i in turns[:-1]]
    down_grad, branch_grad = turned_pieces(clock, early, [(units, True), (width, False)])
    input_grad.append(last(clock, x_rows[-1], resid_grad[-1], gain_one_row, one_terms[-1], LONG))
    packed = sum_of(clock, packed_all, F32)
    gate_blocks = packed[:, :side]
    small = packed[:, side:].reshape(-1)
    sums = small[: TILE * width].reshape(TILE, width)
    gains = small[TILE * width : TILE * width + 2 * model].reshape(2, model)
    out_grad, inner_weight_grad = turned_pieces(clock, late, [(width, True), (width, False)])

    def stacked(values):
        return jnp.stack(values).reshape(micro, seqs, rows, model)

    return (
        stacked(block_out),
        stacked(input_grad),
        gains[0],
        branch_grad,
        inner_weight_grad,
        sums[:CONV],
        sums[CONV],
        gate_blocks[:blocks],
        sums[CONV + 2],
        gate_blocks[blocks:],
        sums[CONV + 3],
        sums[CONV + 1] * (CPOW * jax.nn.sigmoid(-decay_param)),
        out_grad,
        gains[1],
        gate_grad,
        up_grad,
        down_grad,
    )


def solution(mesh):
    tokens = P(None, "fsdp", ("context", "tensor"), None)
    by_rows = P(("fsdp", "context"), "tensor")
    by_cols = P("tensor", ("fsdp", "context"))
    channel = P("tensor")
    taps = P(None, "tensor")
    blocks = P("tensor", None, None)
    return jax.shard_map(
        per_device,
        mesh=mesh,
        in_specs=(
            tokens, P(None, "fsdp", None), P(), by_rows, by_rows, taps, channel, blocks, channel, blocks, channel,
            channel, by_cols, P(), by_rows, by_rows, by_cols, tokens,
        ),
        out_specs=(
            tokens, tokens, P(), by_rows, by_rows, taps, channel, blocks, channel, blocks, channel, channel,
            by_cols, P(), by_rows, by_rows, by_cols,
        ),
        check_vma=False,
    )
```

```python
from functools import partial

import jax
import jax.numpy as jnp
from jax import lax
from jax.experimental import pallas as pl
from jax.experimental.pallas import tpu as pltpu
from jax.sharding import PartitionSpec as P

CONV = 4
CPOW = 8
EPS = 1e-06
TILE = 8
F32 = jnp.float32
BF16 = jnp.bfloat16
GELU_A = 0.7978845608028654
GELU_B = 0.044715
LONG = 10**4
RATE = 3e9


def shift(value, axis, by):
    size = lax.axis_size(axis)
    return lax.ppermute(value, axis, [(i, (i + by) % size) for i in range(size)])


def step_by(value, axis, by):
    size = lax.axis_size(axis)
    return lax.ppermute(value, axis, [(i, i + by) for i in range(size) if 0 <= i + by < size])


def sum_over(value, axis):
    size = lax.axis_size(axis)
    parts = [value] + [shift(value, axis, k) for k in range(1, size)]
    total = parts[0].astype(F32)
    for part in parts[1:]:
        total = total + part.astype(F32)
    return total


def gelu_parts(v):
    th = jnp.tanh(GELU_A * (v + GELU_B * (v * v * v)))
    half = 0.5 * (1.0 + th)
    slope = half + 0.5 * v * (1.0 - th * th) * (GELU_A * (1.0 + 3.0 * GELU_B * (v * v)))
    return v * half, slope


def neg_expm1(z):
    series = 1.0 + z * (1.0 / 10.0)
    for n in (9.0, 8.0, 7.0, 6.0, 5.0, 4.0, 3.0, 2.0):
        series = 1.0 + z * (1.0 / n) * series
    return jnp.where(z > -0.5, -z * series, 1.0 - jnp.exp(z))


def sigmoid(v):
    return 1.0 / (1.0 + jnp.exp(-v))


def tile_scan(coeffs, offsets, reverse):
    rows, width = coeffs.shape
    a = coeffs.reshape(rows // TILE, TILE, width)
    b = offsets.reshape(rows // TILE, TILE, width)
    place = lax.broadcasted_iota(jnp.int32, a.shape, 1)
    for s in (1, 2, 4):
        if reverse:
            inside, turn = place < TILE - s, TILE - s
        else:
            inside, turn = place >= s, s
        a_far = pltpu.roll(a, turn, 1)
        b_far = pltpu.roll(b, turn, 1)
        b = jnp.where(inside, b + a * b_far, b)
        a = jnp.where(inside, a * a_far, a)
    return a, b


def forward_kernel(
    inner_ref, halo_ref, mask_ref, par_ref, wg_ref,
    conv_ref, pre_ref, decay_ref, prod_ref, state_ref, last_ref, ext, run,
):
    rows = inner_ref.shape[0]
    step = pl.program_id(0)

    @pl.when(step == 0)
    def _():
        ext[0:TILE] = halo_ref[...].astype(F32)
        run[0:1] = jnp.ones_like(run[0:1])
        run[1:2] = jnp.zeros_like(run[1:2])

    inner = inner_ref[...].astype(BF16).astype(F32)
    ext[TILE : TILE + rows] = inner
    mask = mask_ref[...]
    conv = par_ref[CONV : CONV + 1] + par_ref[0:1] * inner
    for k in range(1, CONV):
        conv = conv + par_ref[k : k + 1] * ext[TILE - k : TILE - k + rows] * mask[:, k - 1 : k]
    ext[0:TILE] = inner[rows - TILE :]
    conv_low = conv.astype(BF16)
    conv_ref[...] = conv_low
    pre = jnp.dot(conv_low, wg_ref[...], preferred_element_type=F32)
    width = inner.shape[1]
    rate_pre = pre[:, :width] + par_ref[CONV + 2 : CONV + 3]
    input_pre = pre[:, width:] + par_ref[CONV + 3 : CONV + 4]
    pre_ref[:, :width] = rate_pre
    pre_ref[:, width:] = input_pre
    log_rate = par_ref[CONV + 1 : CONV + 2] * sigmoid(rate_pre)
    starts = mask[:, CONV - 1 : CONV] > 0.5
    decays = jnp.where(starts, 0.0, jnp.exp(log_rate))
    scale = jnp.where(starts, 1.0, jnp.sqrt(neg_expm1(2.0 * log_rate)))
    drives = scale * sigmoid(input_pre) * conv_low.astype(F32)
    decay_ref[...] = decays
    a, b = tile_scan(decays, drives, False)
    prod, state = run[0:1], run[1:2]
    for i in range(rows // TILE):
        prods = a[i] * prod
        states = b[i] + a[i] * state
        prod_ref[i * TILE : (i + 1) * TILE] = prods
        state_ref[i * TILE : (i + 1) * TILE] = states
        prod, state = prods[TILE - 1 :], states[TILE - 1 :]
    run[0:1] = prod
    run[1:2] = state
    last_ref[0:1] = prod
    last_ref[1:2] = state


def reverse_kernel(
    many, *refs
):
    blocks, refs = refs[: many + 1], refs[many + 1 :]
    (weight_ref, branch_ref, states_ref, decay_ref, wide_ref,
     low_ref, prod_ref, grad_ref, first_ref, mixed_all, ext, run) = refs
    rows = branch_ref.shape[0]
    step = pl.program_id(0)
    place = pl.num_programs(0) - 1 - step

    @pl.when(step == 0)
    def _():
        ext[rows : rows + TILE] = jnp.ones_like(ext[rows : rows + TILE])
        run[0:1] = jnp.ones_like(run[0:1])
        run[1:2] = jnp.zeros_like(run[1:2])
        assemble(blocks, wide_ref)
        mixed_all[...] = jnp.dot(wide_ref[...], weight_ref[...], preferred_element_type=F32)

    mixed = mixed_all[pl.ds(pl.multiple_of(place * rows, TILE), rows)]
    value, slope = gelu_parts(branch_ref[...])
    low_ref[...] = (mixed * states_ref[...] * slope).astype(BF16)
    decays = decay_ref[...]
    ext[0:rows] = decays
    following = ext[1 : rows + 1]
    ext[rows : rows + TILE] = decays[0:TILE]
    a, b = tile_scan(following, mixed * value, True)
    prod, grad = run[0:1], run[1:2]
    for i in reversed(range(rows // TILE)):
        prods = a[i] * prod
        grads = b[i] + a[i] * grad
        prod_ref[i * TILE : (i + 1) * TILE] = prods
        grad_ref[i * TILE : (i + 1) * TILE] = grads
        prod, grad = prods[0:1], grads[0:1]
    run[0:1] = prod
    run[1:2] = grad
    first_ref[0:1] = decays[0:1] * prod
    first_ref[1:2] = decays[0:1] * grad


def gates_kernel(
    prod_ref, grad_ref, in_ref, prev_ref, state_in_ref, states_ref, decay_ref, pre_ref, conv_ref,
    inner_ref, inner_prev_ref, halo_ref, mask_ref, par_ref, wg_ref,
    low_ref, inner_grad_ref, edge_ref, sums_ref, ext, later,
):
    rows, width = prod_ref.shape
    step = pl.program_id(0)
    at_start = step == pl.num_programs(0) - 1

    @pl.when(step == 0)
    def _():
        sums_ref[...] = jnp.zeros_like(sums_ref)
        later[...] = jnp.zeros_like(later)

    mask = mask_ref[...]
    starts = mask[:, CONV - 1 : CONV] > 0.5
    drive_grad = grad_ref[...] + prod_ref[...] * in_ref[...]
    ext[TILE : TILE + rows] = states_ref[...]
    ext[TILE - 1 : TILE] = jnp.where(at_start, state_in_ref[...], prev_ref[TILE - 1 : TILE])
    prev_states = ext[TILE - 1 : TILE - 1 + rows]
    rate = sigmoid(pre_ref[:, :width])
    gate = sigmoid(pre_ref[:, width:])
    conv = conv_ref[...].astype(F32)
    slope = par_ref[CONV + 1 : CONV + 2]
    log_rate = slope * rate
    decays = decay_ref[...]
    raw = jnp.sqrt(neg_expm1(2.0 * log_rate))
    scale = jnp.where(starts, 1.0, raw)
    scale_grad = drive_grad * gate * conv
    log_grad = jnp.where(
        starts, 0.0, drive_grad * prev_states * decays - scale_grad * (decays * decays) / raw
    )
    rate_low = (log_grad * slope * rate * (1.0 - rate)).astype(BF16)
    input_low = (drive_grad * scale * conv * gate * (1.0 - gate)).astype(BF16)
    low_ref[:, :width] = rate_low
    low_ref[:, width:] = input_low
    both = jnp.concatenate([rate_low, input_low], axis=1)
    conv_grad = drive_grad * scale * gate + lax.dot_general(
        both, wg_ref[...], (((1,), (1,)), ((), ())), preferred_element_type=F32
    )
    inner = inner_ref[...].astype(BF16).astype(F32)
    before = jnp.where(at_start, halo_ref[...].astype(F32), inner_prev_ref[...].astype(BF16).astype(F32))
    ext[0:TILE] = before
    ext[TILE : TILE + rows] = inner

    def total(values):
        return jnp.sum(values, axis=0, keepdims=True)

    sums_ref[0:1] += total(conv_grad * inner)
    sums_ref[CONV : CONV + 1] += total(conv_grad)
    sums_ref[CONV + 1 : CONV + 2] += total(log_grad * rate)
    sums_ref[CONV + 2 : CONV + 3] += total(rate_low.astype(F32))
    sums_ref[CONV + 3 : CONV + 4] += total(input_low.astype(F32))
    inner_grad = par_ref[0:1] * conv_grad
    heads = []
    for k in range(1, CONV):
        masked = conv_grad * mask[:, k - 1 : k]
        sums_ref[k : k + 1] += total(masked * ext[TILE - k : TILE - k + rows])
        heads.append(masked[0:TILE] * par_ref[k : k + 1])
    for k in range(1, CONV):
        masked = par_ref[k : k + 1] * (conv_grad * mask[:, k - 1 : k])
        ext[0:rows] = masked
        ext[rows : rows + TILE] = later[k - 1]
        inner_grad = inner_grad + ext[k : k + rows]
        later[k - 1] = heads[k - 1]
    inner_grad_ref[...] = inner_grad.astype(inner_grad_ref.dtype)

    @pl.when(at_start)
    def _():
        edge_ref[...] = jnp.zeros_like(edge_ref)
        for back in range(1, CONV):
            row = heads[back - 1][0:1]
            for k in range(back + 1, CONV):
                row = row + heads[k - 1][k - back : k - back + 1]
            edge_ref[TILE - back : TILE - back + 1] = row


def rows_spec(rows, width, parts, column=0, reverse=False):
    return pl.BlockSpec((rows, width), lambda step: (parts - 1 - step if reverse else step, column))


def before_spec(rows, width, parts, column=0):
    tiles = rows // TILE
    return pl.BlockSpec(
        (TILE, width), lambda step: (jnp.maximum(parts - 2 - step, 0) * tiles + tiles - 1, column)
    )


def whole_spec(shape):
    return pl.BlockSpec(shape, lambda step: (0,) * len(shape))


def dot_nt(left, right):
    return lax.dot_general(left, right, (((1,), (1,)), ((), ())), preferred_element_type=F32)


def dot_tn(left, right):
    return lax.dot_general(left, right, (((0,), (0,)), ((), ())), preferred_element_type=F32)


COSTS = (
    0.2, 3, 0.2, 6, 0.01, 6, 5.7, 7, 5.7, 3, 3, 27, 27, 3.4, 21, 60, 0.01, 0.01, 7.5, 7.5, 6, 7, 8, 40, 40, 0.01, 0.01, 0.01, 0.01, 0.01, 0.01, 0.01, 0.01, 0.01, 3, 10000.0, 1, 3,
)


class Clock:
    def __init__(self):
        self.tick = jnp.zeros((TILE, 128), F32)
        self.calls = 0

    def call(self, kernel, grid, operands, in_specs, out_specs, out_shape, scratch=(), after=(), cost=3.0):
        cost = COSTS[self.calls] if self.calls < len(COSTS) else cost
        self.calls += 1
        count, extra, outs = len(operands), len(after) + 1, len(out_shape)

        def body(*refs):
            given, refs = refs[:count], refs[count + extra :]
            kernel(*given, *refs[:outs], *refs[outs + 1 :])
            refs[outs][...] = jnp.zeros_like(refs[outs])

        whole = pl.BlockSpec((TILE, 128), lambda *step: (0, 0))
        *results, self.tick = pl.pallas_call(
            body,
            out_shape=list(out_shape) + [jax.ShapeDtypeStruct((TILE, 128), F32)],
            grid=grid,
            in_specs=list(in_specs) + [pl.BlockSpec(memory_space=pl.ANY)] * extra,
            out_specs=list(out_specs) + [whole],
            scratch_shapes=list(scratch),
            cost_estimate=pl.CostEstimate(flops=int(cost * RATE), bytes_accessed=int(cost * RATE), transcendentals=0),
        )(*operands, *after, self.tick)
        return results


def shape(dims, dtype):
    return jax.ShapeDtypeStruct(dims, dtype)


def held(array):
    dims = array.shape
    return pl.BlockSpec(dims, lambda *step: (0,) * len(dims), pipeline_mode=pl.Buffered(1))


def kept(dims):
    return pl.BlockSpec(dims, lambda *step: (0,) * len(dims))


def place_spec():
    return pl.BlockSpec(memory_space=pltpu.SMEM)


def spread(copies, apart):
    if not apart:
        return [lax.all_to_all(copies, "tensor", split_axis=0, concat_axis=0, tiled=True)]
    return [copies] + [shift(copies, "tensor", k) for k in range(1, lax.axis_size("tensor"))]


def gathered_sums(parts):
    if len(parts) == 1:
        return [lax.all_to_all(parts[0], "tensor", split_axis=0, concat_axis=0, tiled=True)]
    return [parts[0]] + [shift(parts[k], "tensor", k) for k in range(1, len(parts))]


def assemble(refs, wide_ref):
    place, blocks = refs[0], refs[1:]
    if len(blocks) == 1:
        wide_ref[...] = blocks[0][...]
        return
    rows = blocks[0].shape[0]
    for k, block in enumerate(blocks):
        owner = lax.rem(place[0] - k + len(blocks), len(blocks))
        wide_ref[pl.ds(pl.multiple_of(owner * rows, 2 * TILE), rows)] = block[...]


def deal(values, place, outs, work):
    if len(outs) == 1:
        outs[0][...] = values.astype(BF16)
        return
    work[...] = values
    rows = outs[0].shape[0]
    for k, out in enumerate(outs):
        owner = lax.rem(place[0] + k, len(outs))
        out[...] = work[pl.ds(pl.multiple_of(owner * rows, 2 * TILE), rows)].astype(BF16)


def added(refs, rows):
    if len(refs) == 1:
        count = refs[0].shape[0] // rows
        terms = [refs[0][k * rows : (k + 1) * rows].astype(F32) for k in range(count)]
    else:
        terms = [ref[...].astype(F32) for ref in refs]
    return sum(terms[1:], terms[0])


def repeat_to(ref, values, rows):
    for k in range(ref.shape[0] // rows):
        ref[k * rows : (k + 1) * rows] = values


def mean_of(values):
    return jnp.mean(values, axis=-1, keepdims=True)


def first_kernel(x_ref, gain_ref, out_ref):
    x = x_ref[...].astype(F32)
    repeat_to(out_ref, (x * lax.rsqrt(mean_of(x * x) + EPS) * gain_ref[...]).astype(BF16), x_ref.shape[0])


def first(clock, x, gain, copies):
    rows, model = x.shape
    return clock.call(
        first_kernel, (1,), [x, gain], [held(x), held(gain)],
        [kept((copies * rows, model))], [shape((copies * rows, model), BF16)],
        cost=0.2,
    )[0]


def copies_kernel(*refs):
    out_ref = refs[-1]
    rows = refs[0].shape[0]
    for k in range(out_ref.shape[0] // rows):
        out_ref[k * rows : (k + 1) * rows] = refs[k % (len(refs) - 1)][...]


def all_copies(clock, arrays, copies, after):
    rows, model = arrays[0].shape
    total = rows * len(arrays) * copies
    return clock.call(
        copies_kernel, (1,), arrays, [held(a) for a in arrays], [kept((total, model))],
        [shape((total, model), BF16)], after=after,
        cost=3.0,
    )[0]


def project_kernel(many, *refs):
    blocks, (weight_ref, wide_ref, out_ref, halo_ref) = refs[: many + 1], refs[many + 1 :]

    @pl.when(pl.program_id(0) == 0)
    def _():
        assemble(blocks, wide_ref)

    value = jnp.dot(wide_ref[...], weight_ref[...], preferred_element_type=F32)
    out_ref[...] = value

    @pl.when(pl.program_id(0) == pl.num_programs(0) - 1)
    def _():
        halo_ref[...] = value[value.shape[0] - TILE :].astype(BF16)


def project(clock, place, blocks, weight, cols, after=()):
    model = weight.shape[0]
    rows = sum(block.shape[0] for block in blocks)
    width = cols // 2
    return clock.call(
        partial(project_kernel, len(blocks)), (2,), [place, *blocks, weight],
        [place_spec()] + [held(b) for b in blocks] + [pl.BlockSpec((model, width), lambda j: (0, j))],
        [kept((rows, model)), pl.BlockSpec((rows, width), lambda j: (0, j)), kept((TILE, width))],
        [shape((rows, model), BF16), shape((rows, cols), F32), shape((TILE, width), BF16)], after=after,
        cost=6.0,
    )


def mix_kernel(outs, place_ref, local_ref, prod_ref, in_ref, branch_ref, weight_ref, *refs):
    states_ref, mixed_ref = refs[:2]

    @pl.when(pl.program_id(0) == 0)
    def _():
        states = local_ref[...] + prod_ref[...] * in_ref[...]
        states_ref[...] = states
        mixed_ref[...] = (states * gelu_parts(branch_ref[...])[0]).astype(BF16)

    value = dot_nt(mixed_ref[...], weight_ref[...])
    deal(value, place_ref, refs[2 : 2 + outs], refs[-1])


def part_specs(rows, cols, tile, outs):
    return (
        [pl.BlockSpec((rows // outs, tile), lambda j: (0, j))] * outs,
        [shape((rows // outs, cols), BF16)] * outs,
        pltpu.VMEM((rows, tile), F32),
    )


def mix_out(clock, place, local, prods, state_in, both_pre, weight, outs, tile, after=()):
    rows, width = local.shape
    cols = weight.shape[0]
    part_spec, part_shape, work = part_specs(rows, cols, tile, outs)
    results = clock.call(
        partial(mix_kernel, outs), (cols // tile,), [place, local, prods, state_in, both_pre, weight],
        [place_spec(), held(local), held(prods), held(state_in),
         pl.BlockSpec((rows, width), lambda j: (0, 0), pipeline_mode=pl.Buffered(1)),
         pl.BlockSpec((tile, width), lambda j: (j, 2))],
        [kept((rows, width)), kept((rows, width))] + part_spec,
        [shape((rows, width), F32), shape((rows, width), BF16)] + part_shape, [work], after,
        cost=5.7,
    )
    return results[0], results[1], results[2:]


def second_kernel(x_ref, gain_ref, *refs):
    terms, (resid_ref, out_ref) = refs[:-2], refs[-2:]
    rows = x_ref.shape[0]
    resid = x_ref[...].astype(F32) + added(terms, rows)
    resid_ref[...] = resid
    repeat_to(out_ref, (resid * lax.rsqrt(mean_of(resid * resid) + EPS) * gain_ref[...]).astype(BF16), rows)


def second(clock, x, gain, terms, copies, after=()):
    rows, model = x.shape
    return clock.call(
        second_kernel, (1,), [x, gain, *terms], [held(x), held(gain)] + [held(t) for t in terms],
        [kept((rows, model)), kept((copies * rows, model))],
        [shape((rows, model), F32), shape((copies * rows, model), BF16)],
        after=after,
        cost=3.0,
    )


def mlp_kernel(two_many, turn, turns, unit, outs, *refs):
    two_blocks, refs = refs[: two_many + 1], refs[two_many + 1 :]
    cot_all, gate_ref, up_ref, down_ref, two_ref, cot_ref, hidden_ref, pair_ref = refs[:8]
    parts, acc = refs[8 : 8 + outs], refs[-1]
    step = pl.program_id(0)

    @pl.when(step == 0)
    def _():
        assemble(two_blocks, two_ref)
        rows = unit
        for k in range(two_ref.shape[0] // rows):
            start = (k * turns + turn) * rows
            cot_ref[k * rows : (k + 1) * rows] = cot_all[start : start + rows]

    two = two_ref[...]
    gate_w, up_w = gate_ref[...], up_ref[...]
    gate_val, gate_slope = gelu_parts(jnp.dot(two, gate_w, preferred_element_type=F32))
    up_pre = jnp.dot(two, up_w, preferred_element_type=F32)
    hidden_ref[...] = (gate_val * up_pre).astype(BF16)
    hidden_grad = jnp.dot(cot_ref[...], down_ref[...], preferred_element_type=F32)
    gate_low = (hidden_grad * up_pre * gate_slope).astype(BF16)
    up_low = (hidden_grad * gate_val).astype(BF16)
    pair_ref[0] = gate_low
    pair_ref[1] = up_low
    term = dot_nt(gate_low, gate_w) + dot_nt(up_low, up_w)

    @pl.when(step == 0)
    def _():
        acc[...] = term

    @pl.when(step > 0)
    def _():
        acc[...] += term

    @pl.when(step == pl.num_programs(0) - 1)
    def _():
        rows = parts[0].shape[0]
        for k, out in enumerate(parts):
            start = 0 if outs == 1 else pl.multiple_of(lax.rem(two_blocks[0][0] + k, outs) * rows, 2 * TILE)
            out[...] = acc[pl.ds(start, rows)].astype(BF16)


def mlp(clock, place, two_blocks, cot_all, turn, turns, unit, weight, outs, tile, after=()):
    model, units = weight.shape[0], weight.shape[1] // 3
    rows = sum(block.shape[0] for block in two_blocks)
    steps = units // tile
    results = clock.call(
        partial(mlp_kernel, len(two_blocks), turn, turns, unit, outs), (steps,),
        [place, *two_blocks, cot_all, weight, weight, weight],
        [place_spec()] + [held(b) for b in two_blocks + [cot_all]]
        + [pl.BlockSpec((model, tile), lambda j: (0, j)), pl.BlockSpec((model, tile), lambda j: (0, steps + j)),
           pl.BlockSpec((model, tile), lambda j: (0, 2 * steps + j))],
        [kept((rows, model)), kept((rows, model)), pl.BlockSpec((rows, tile), lambda j: (0, j)),
         pl.BlockSpec((2, rows, tile), lambda j: (0, 0, j))] + [kept((rows // outs, model))] * outs,
        [shape((rows, model), BF16), shape((rows, model), BF16), shape((rows, units), BF16),
         shape((2, rows, units), BF16)] + [shape((rows // outs, model), BF16)] * outs,
        [pltpu.VMEM((rows, model), F32)], after,
        cost=27.0,
    )
    return *results[:4], results[4:]


def down_kernel(count, unit, *refs):
    right, out_ref = refs[count], refs[-1]
    for i in range(count):
        value = dot_nt(refs[i][...], right[...]).astype(BF16)
        for k in range(value.shape[0] // unit):
            start = (k * count + i) * unit
            out_ref[start : start + unit] = value[k * unit : (k + 1) * unit]


def down_out(clock, lefts, right, unit, tile):
    cols, depth = right.shape[0], lefts[0].shape[1]
    count = len(lefts)
    total = count * lefts[0].shape[0]
    return clock.call(
        partial(down_kernel, count, unit), (cols // tile,), [*lefts, right],
        [held(a) for a in lefts] + [pl.BlockSpec((tile, depth), lambda j: (j, 2))],
        [pl.BlockSpec((total, tile), lambda j: (0, j))], [shape((total, cols), BF16)],
        cost=0.01,
    )[0]


def norm_grad(values, grad, gain):
    inv = lax.rsqrt(mean_of(values * values) + EPS)
    unit = values * inv
    scaled = grad * gain
    return inv * (scaled - unit * mean_of(scaled * unit)), grad * unit


def third_kernel(resid_ref, cot_ref, gain_ref, *refs):
    terms, (grad_ref, low_ref, sum_ref) = refs[:-3], refs[-3:]
    rows = resid_ref.shape[0]
    grad = added(terms, rows).astype(BF16).astype(F32)
    term, product = norm_grad(resid_ref[...], grad, gain_ref[...])
    total = cot_ref[...].astype(F32) + term
    grad_ref[...] = total
    sum_ref[...] = jnp.sum(product, axis=0, keepdims=True)
    repeat_to(low_ref, total.astype(BF16), rows)


def third(clock, resid, cot, gain, terms, copies, cost):
    rows, model = resid.shape
    return clock.call(
        third_kernel, (1,), [resid, cot, gain, *terms], [held(resid), held(cot), held(gain)] + [held(t) for t in terms],
        [kept((rows, model)), kept((copies * rows, model)), kept((1, model))],
        [shape((rows, model), F32), shape((copies * rows, model), BF16), shape((1, model), F32)],
        cost=cost,
    )


def back_kernel(outs, place_ref, branch_ref, inner_ref, edge_ref, weight_ref, one_ref, *refs):
    low_ref, gain_ref = refs[:2]
    both_ref, work = refs[-2:]
    rows, width = branch_ref.shape

    @pl.when(pl.program_id(0) == 0)
    def _():
        both_ref[:, :width] = branch_ref[...]
        both_ref[: rows - 2 * TILE, width:] = inner_ref[: rows - 2 * TILE].astype(BF16)
        last = inner_ref[rows - 2 * TILE :]
        fixed = jnp.concatenate([last[:TILE], last[TILE:] + edge_ref[...]], axis=0)
        both_ref[rows - 2 * TILE :, width:] = fixed.astype(BF16)
        low_ref[...] = both_ref[:, width:]

    value = dot_nt(both_ref[...], weight_ref[...])
    gain_ref[...] = jnp.sum(value * one_ref[...].astype(F32), axis=0, keepdims=True)
    deal(value, place_ref, refs[2 : 2 + outs], work)


def back_one(clock, place, branch_low, inner_grad, edge_in, weight, wide_one, outs, tile):
    rows, width = branch_low.shape
    model = weight.shape[0]
    part_spec, part_shape, work = part_specs(rows, model, tile, outs)
    results = clock.call(
        partial(back_kernel, outs), (model // tile,), [place, branch_low, inner_grad, edge_in, weight, wide_one],
        [place_spec(), held(branch_low), held(inner_grad), held(edge_in),
         pl.BlockSpec((tile, 2 * width), lambda j: (j, 0)), pl.BlockSpec((rows, tile), lambda j: (0, j))],
        [kept((rows, width)), pl.BlockSpec((1, tile), lambda j: (0, j))] + part_spec,
        [shape((rows, width), BF16), shape((1, model), F32)] + part_shape,
        [pltpu.VMEM((rows, 2 * width), BF16), work],
        cost=6.2,
    )
    return results[0], results[1], results[2:]


def last_kernel(x_ref, resid_ref, gain_ref, *refs):
    terms, out_ref = refs[:-1], refs[-1]
    grad = added(terms, x_ref.shape[0]).astype(BF16).astype(F32)
    out_ref[...] = resid_ref[...] + norm_grad(x_ref[...].astype(F32), grad, gain_ref[...])[0]


def last(clock, x, resid_grad, gain, terms, cost):
    return clock.call(
        last_kernel, (1,), [x, resid_grad, gain, *terms],
        [held(x), held(resid_grad), held(gain)] + [held(t) for t in terms],
        [kept(resid_grad.shape)], [shape(resid_grad.shape, F32)], cost=cost,
    )[0]


def out_kernel(count, *refs):
    terms, outs = refs[count], refs[count + 1 :]
    rows = refs[0].shape[0]
    for i in range(count):
        total = refs[i][...]
        for k in range(terms.shape[0] // (count * rows)):
            start = (k * count + i) * rows
            total = total + terms[start : start + rows].astype(F32)
        outs[i][...] = total.astype(BF16)


def block_results(clock, residuals, terms):
    count = len(residuals)
    dims = residuals[0].shape
    return clock.call(
        partial(out_kernel, count), (1,), [*residuals, terms], [held(r) for r in residuals] + [held(terms)],
        [kept(dims)] * count, [shape(dims, BF16)] * count,
        cost=3.0,
    )


def stack_rows(refs):
    return jnp.concatenate(refs, axis=0) if len(refs) > 1 else refs[0]


def term_kernel(count, *refs):
    halved = len(refs[count].shape) == 3
    left = stack_rows([refs[i][...] for i in range(count)])
    right = stack_rows([refs[count + i][0] if halved else refs[count + i][...] for i in range(count)])
    refs[-1][...] = dot_tn(left, right).astype(refs[-1].dtype)


def weight_term(clock, lefts, rights, tile, cost, after=()):
    count = len(lefts)
    rows, depth = lefts[0].shape
    halves = rights[0].shape[0] if rights[0].ndim == 3 else 1
    cols = rights[0].shape[-1]
    if halves == 1:
        grid, left_at, out_at = (depth // tile,), (lambda j: (0, j)), (lambda j: (j, 0))
        right_spec = held(rights[0])
    else:
        grid, left_at, out_at = (halves, depth // tile), (lambda h, j: (0, j)), (lambda h, j: (j, h))
        right_spec = pl.BlockSpec((1, rows, cols), lambda h, j: (h, 0, 0))
    return clock.call(
        partial(term_kernel, count), grid, [*lefts, *rights],
        [pl.BlockSpec((rows, tile), left_at)] * count + [right_spec] * count,
        [pl.BlockSpec((tile, cols), out_at)], [shape((depth, halves * cols), BF16)], after=after,
        cost=cost,
    )[0]


def diagonal_kernel(count, cells, *refs):
    out_ref, work = refs[-2:]
    total = None
    for i in range(count):
        value = dot_tn(refs[i][...], refs[count + i][...])
        total = value if total is None else total + value
    work[...] = total
    cell = out_ref.shape[1]
    for i in range(cells):
        for h in range(2):
            col = (h * cells + i) * cell
            out_ref[h * cells + i] = work[i * cell : (i + 1) * cell, col : col + cell].astype(BF16)


def diagonal_terms(clock, lefts, rights, cells):
    count = len(lefts)
    width = lefts[0].shape[1]
    cell = width // cells
    return clock.call(
        partial(diagonal_kernel, count, cells), (1,), [*lefts, *rights],
        [held(a) for a in lefts] + [held(a) for a in rights],
        [kept((2 * cells, cell, cell))], [shape((2 * cells, cell, cell), BF16)],
        [pltpu.VMEM((width, 2 * width), F32)],
        cost=4.5,
    )[0]


def split_term_kernel(count, groups, unit, place_ref, *refs):
    k, c = pl.program_id(0), pl.program_id(1)
    owner = lax.rem(place_ref[0] + k, groups) * pl.num_programs(1) + c
    start = pl.multiple_of(owner * unit, unit)
    left = stack_rows([refs[i][:, pl.ds(start, unit)] for i in range(count)])
    total = dot_tn(left, stack_rows([refs[count + i][...] for i in range(count)])).astype(BF16)
    for g in range(groups):
        @pl.when(k == g)
        def _(g=g):
            refs[2 * count + g][...] = total


def split_term(clock, place, lefts, rights, groups, steps, cost, after=()):
    count = len(lefts)
    depth = lefts[0].shape[1]
    cols = rights[0].size // rights[0].shape[-2]
    unit = depth // (groups * steps)

    def spec(g):
        return pl.BlockSpec(
            (unit, cols), lambda k, c: (jnp.where(k < g, 0, jnp.where(k > g, steps - 1, c)), 0)
        )

    parts = clock.call(
        partial(split_term_kernel, count, groups, unit), (groups, steps), [place, *lefts, *rights],
        [place_spec()] + [held(a) for a in lefts] + [held(a) for a in rights],
        [spec(g) for g in range(groups)], [shape((unit * steps, cols), BF16)] * groups, after=after, cost=cost,
    )
    return [parts[0]] + [shift(parts[k], "fsdp", k) for k in range(1, groups)]


def member_kernel(groups, *refs):
    out_ref = refs[-1]
    col = 0
    for i in range(0, len(refs) - 1, groups):
        total = added(refs[i : i + groups], refs[i].shape[0])
        out_ref[:, col : col + total.shape[1]] = total.astype(BF16)
        col += total.shape[1]


def member_sums(clock, terms, cost=8.0):
    flat = [t for some in terms for t in some]
    rows, cols = flat[0].shape[0], sum(some[0].shape[1] for some in terms)
    tile = rows // 4
    added_up = clock.call(
        partial(member_kernel, len(terms[0])), (4,), flat,
        [pl.BlockSpec((tile, t.shape[1]), lambda j: (j, 0)) for t in flat],
        [pl.BlockSpec((tile, cols), lambda j: (j, 0))], [shape((rows, cols), BF16)], cost=cost,
    )[0]
    return lax.psum_scatter(added_up, "context", scatter_dimension=0, tiled=True)


def turned_kernel(cuts, in_ref, *outs):
    total = in_ref[...].astype(F32)
    col = 0
    for out, turned in zip(outs, cuts):
        step = out.shape[0] if turned else out.shape[1]
        piece = total[:, col : col + step]
        out[...] = piece.T if turned else piece
        col += step


def turned_pieces(clock, low, cuts):
    rows = low.shape[0]
    dims = [(cols, rows) if turned else (rows, cols) for cols, turned in cuts]
    return clock.call(
        partial(turned_kernel, [turned for _, turned in cuts]), (1,), [low], [held(low)], [kept(d) for d in dims],
        [shape(d, F32) for d in dims], cost=3.0,
    )


def sum_kernel(*refs):
    refs[-1][...] = added(refs[:-1], refs[0].shape[0]).astype(refs[-1].dtype)


def sum_of(clock, arrays, dtype):
    dims = arrays[0].shape
    return clock.call(
        sum_kernel, (1,), arrays, [held(a) for a in arrays], [kept(dims)], [shape(dims, dtype)], cost=1.0,
    )[0]


def everyone(value, axis):
    return [value] + [shift(value, axis, k) for k in range(1, lax.axis_size(axis))]


def forward_scan(clock, both_pre, halo, mask, params, gate_w, parts):
    total, width = both_pre.shape[0], params.shape[1]
    rows = total // parts
    spec = partial(rows_spec, rows, width, parts)
    return clock.call(
        forward_kernel, (parts,), [both_pre, halo, mask, params, gate_w],
        [spec(column=1), held(halo), rows_spec(rows, mask.shape[1], parts), held(params), held(gate_w)],
        [spec(), rows_spec(rows, 2 * width, parts), spec(), spec(), spec(), kept((2, width))],
        [shape((total, width), BF16), shape((total, 2 * width), F32), shape((total, width), F32),
         shape((total, width), F32), shape((total, width), F32), shape((2, width), F32)],
        [pltpu.VMEM((rows + TILE, width), F32), pltpu.VMEM((TILE, width), F32)],
        cost=7.0,
    )


def reverse_scan(clock, place, blocks, out_w, both_pre, states, decays, parts, after=()):
    total, width = states.shape
    rows = total // parts
    model = out_w.shape[0]
    spec = rows_spec(rows, width, parts, reverse=True)
    return clock.call(
        partial(reverse_kernel, len(blocks)), (parts,), [place, *blocks, out_w, both_pre, states, decays],
        [place_spec()] + [held(b) for b in blocks] + [pl.BlockSpec((model, width), lambda step: (0, 2), pipeline_mode=pl.Buffered(1)), spec, spec, spec],
        [kept((total, model)), spec, spec, spec, kept((2, width))],
        [shape((total, model), BF16), shape((total, width), BF16), shape((total, width), F32),
         shape((total, width), F32), shape((2, width), F32)],
        [pltpu.VMEM((total, width), F32), pltpu.VMEM((rows + TILE, width), F32), pltpu.VMEM((TILE, width), F32)],
        after,
        cost=7.5,
    )


def gates_back(clock, prods, grads, grad_in, states, state_in, decays, pre, conv_low, both_pre, halo, mask,
               params, gate_w, parts):
    total, width = states.shape
    rows = total // parts
    spec = partial(rows_spec, rows, width, parts, reverse=True)
    return clock.call(
        gates_kernel, (parts,),
        [prods, grads, grad_in, states, state_in, states, decays, pre, conv_low, both_pre, both_pre, halo, mask,
         params, gate_w],
        [spec(), spec(), held(grad_in), before_spec(rows, width, parts), held(state_in),
         spec(), spec(), rows_spec(rows, 2 * width, parts, reverse=True), spec(), spec(column=1),
         before_spec(rows, width, parts, column=1), held(halo),
         rows_spec(rows, mask.shape[1], parts, reverse=True), held(params), held(gate_w)],
        [rows_spec(rows, 2 * width, parts, reverse=True), spec(), kept((TILE, width)), kept((TILE, width))],
        [shape((total, 2 * width), BF16), shape((total, width), F32), shape((TILE, width), F32),
         shape((TILE, width), F32)],
        [pltpu.VMEM((rows + TILE, width), F32), pltpu.VMEM((CONV - 1, TILE, width), F32)],
        cost=8.5,
    )


def carry_over(ends, direction):
    size = lax.axis_size("context")
    incoming = jnp.zeros_like(ends[1:2])
    parts = [step_by(ends, "context", direction * k) for k in range(1, size)]
    for part in reversed(parts):
        incoming = part[1:2] + part[0:1] * incoming
    return incoming


def carry_all(ends, direction):
    stacked = jnp.concatenate([e[:1] for e in ends] + [e[1:] for e in ends], axis=0)
    count = len(ends)
    incoming = jnp.zeros_like(stacked[:count])
    for part in reversed([step_by(stacked, "context", direction * k) for k in range(1, lax.axis_size("context"))]):
        incoming = part[count:] + part[:count] * incoming
    return [incoming[i : i + 1] for i in range(count)]


def block_diagonal(weight):
    count, rows, cols = weight.shape
    return jnp.concatenate(
        [jnp.pad(weight[i], ((0, 0), (i * cols, (count - 1 - i) * cols))) for i in range(count)], axis=0
    )


def per_device(
    inputs, segments, norm_gain, branch_weight, inner_weight, conv_weight, conv_bias, rate_weight, rate_bias,
    input_weight, input_bias, decay_param, out_weight, mlp_gain, gate_weight, up_weight, down_weight, cotangent,
):
    micro, seqs, rows, model = inputs.shape
    parts = lax.axis_size("tensor")
    span = rows * parts
    width = conv_bias.shape[0]
    blocks = rate_weight.shape[0]
    units = gate_weight.shape[1]
    chains = [(m, s) for m in range(micro) for s in range(seqs)]
    context_pos = lax.axis_index("context")
    owners = ("fsdp", "context")

    first_w = lax.all_gather(
        jnp.concatenate([branch_weight, inner_weight, out_weight.T], 1), owners, axis=0, tiled=True
    )
    second_w = lax.all_gather(
        jnp.concatenate([gate_weight, up_weight, down_weight.T], 1), owners, axis=0, tiled=True
    )
    gate_w = jnp.concatenate([block_diagonal(rate_weight), block_diagonal(input_weight)], axis=1)
    slope = -CPOW * jax.nn.softplus(-decay_param)
    params = jnp.concatenate(
        [conv_weight, conv_bias[None], slope[None], rate_bias[None], input_bias[None]], axis=0
    )

    def masks_of(row):
        pad = jnp.concatenate([jnp.full((CONV - 1,), -1, jnp.int32), row])
        ext = lax.dynamic_slice_in_dim(pad, context_pos * span, span + CONV - 1)
        own = ext[CONV - 1 :]
        cols = [(ext[CONV - 1 - k : CONV - 1 - k + span] == own).astype(F32) for k in range(1, CONV)]
        return jnp.stack(cols + [1.0 - cols[0]], axis=1)

    count = len(chains)
    turns = range(count)
    apart = [i % 2 == 1 for i in turns]
    copies = [1 if a else parts for a in apart]
    outs = [parts if a else 1 for a in apart]
    place = lax.axis_index("tensor").reshape(1).astype(jnp.int32)
    x_rows = [inputs[m, s] for m, s in chains]
    cot_rows = [cotangent[m, s] for m, s in chains]
    gain_one_row, gain_two_row = norm_gain[None], mlp_gain[None]
    mask = [masks_of(segments[m, s]) for m, s in chains]
    clock = Clock()

    groups, members = lax.axis_size("fsdp"), lax.axis_size("context")
    group_place = lax.axis_index("fsdp").reshape(1).astype(jnp.int32)
    normed = [first(clock, x_rows[0], gain_one_row, copies[0])]
    cot_copies = all_copies(clock, cot_rows[:1], parts, (gate_w, params, *mask))
    normed += [first(clock, x_rows[i], gain_one_row, copies[i]) for i in turns if i]
    one_blocks = [spread(normed[i], apart[i]) for i in turns]
    cots = spread(cot_copies, False)
    later = cot_rows[1:]
    if later:
        second_w, later = lax.optimization_barrier((second_w, later))
        cots += [lax.all_gather(rows_in, "tensor", axis=0, tiled=True) for rows_in in later]
    projections, halo, scans, mixes, ends_in = [], [], [], [], []

    def start_chain(i):
        projections.append(project(clock, place, one_blocks[i], first_w, 2 * width))
        halo.append(step_by(projections[i][2], "context", 1))

    def scan_chain(i):
        scans.append(forward_scan(clock, projections[i][1], halo[i], mask[i], params, gate_w, parts))
        ends_in.append(carry_over(scans[i][5], 1))

    def mix_chain(i):
        mixes.append(mix_out(
            clock, place, scans[i][4], scans[i][3], ends_in[i], projections[i][1], first_w, outs[i], 512,
            () if i else tuple(cots[:1]),
        ))

    start_chain(0)
    scan_chain(0)
    for i in turns:
        if i + 1 < count:
            start_chain(i + 1)
        mix_chain(i)
        if i + 1 < count:
            scan_chain(i + 1)
    wide_one, both_pre, tails = map(list, zip(*projections))
    conv_low, pre, decays, prods, locals_, ends = map(list, zip(*scans))
    state_in = ends_in
    states, mixed_low, out_part = map(list, zip(*mixes))
    out_terms = [gathered_sums(p) for p in out_part]
    residual, two_blocks = [], []
    for i in turns:
        res, low = second(clock, x_rows[i], gain_two_row, out_terms[i], copies[i])
        residual.append(res)
        two_blocks.append(spread(low, apart[i]))
    mlps = [
        mlp(clock, place, two_blocks[i], cots[i], 0, 1, rows, second_w, outs[i], 256) for i in turns
    ]
    wide_two, wide_cot, hidden_low, pair_low, two_part = map(list, zip(*mlps))
    two_terms = [gathered_sums(p) for p in two_part]

    thirds = []
    for i in turns:
        thirds.append(third(
            clock, residual[i], cot_rows[i], gain_two_row, two_terms[i], copies[i], 60.0 if i else 3.4
        ))
        if i == 0:
            pair_grad = lax.psum_scatter(
                weight_term(clock, wide_two, pair_low, 512, 21.0), owners, scatter_dimension=0, tiled=True
            )
    resid_grad, resid_low, gain_two = map(list, zip(*thirds))
    resid_blocks = [spread(resid_low[i], apart[i]) for i in turns]
    down_split = split_term(clock, group_place, wide_cot, hidden_low, groups, 2, 0.01)
    (down_terms,) = gathered_sums([down_out(clock, hidden_low, second_w, rows, 512)])

    reversed_ = [
        reverse_scan(clock, place, resid_blocks[i], first_w, both_pre[i], states[i], decays[i], parts) for i in turns
    ]
    wide_resid, branch_low, rev_prods, rev_grads, ends_back = map(list, zip(*reversed_))
    grad_in = carry_all(ends_back, -1)
    branch_split = split_term(clock, group_place, wide_one, branch_low, groups, 1, 6.0)
    out_split = split_term(clock, group_place, wide_resid, mixed_low, groups, 1, 7.0)
    early = member_sums(clock, [down_split, branch_split], 8.0)
    backs = [
        gates_back(
            clock, rev_prods[i], rev_grads[i], grad_in[i], states[i], state_in[i], decays[i], pre[i], conv_low[i],
            both_pre[i], halo[i], mask[i], params, gate_w, parts,
        )
        for i in turns
    ]
    gates_low, inner_grad, edge, sums = map(list, zip(*backs))
    gate_grad, up_grad = turned_pieces(clock, pair_grad, [(units, False), (units, False)])
    edges = step_by(jnp.concatenate(edge, axis=0), "context", -1)
    edge_in = [edges[i * TILE : (i + 1) * TILE] for i in turns]
    gate_blocks = diagonal_terms(clock, conv_low, gates_low, blocks)
    ones = []
    for i in turns:
        ones.append(back_one(
            clock, place, branch_low[i], inner_grad[i], edge_in[i], first_w, wide_one[i], 1 if i else parts, 512
        ))
        if i == 0:
            block_out = block_results(clock, residual, down_terms)
    inner_low, gain_one, one_part = map(list, zip(*ones))
    one_terms = [gathered_sums(p) for p in one_part]
    inner_split = split_term(clock, group_place, wide_one, inner_low, groups, 1, 8.0)
    gains = sum_over(jnp.concatenate([sum(gain_one) / gain_one_row, sum(gain_two)]), "tensor")
    small = jnp.concatenate([sum(sums).reshape(-1), gains.reshape(-1)]).astype(BF16)
    cells, side = gate_blocks.shape[0], gate_blocks.shape[2]
    extra = -(-small.size // (cells * side * 2 * TILE)) * 2 * TILE
    small = jnp.pad(small, (0, cells * extra * side - small.size)).reshape(cells, extra, side)
    packed_all = everyone(jnp.concatenate([gate_blocks, small], axis=1), "fsdp")
    late = member_sums(clock, [out_split, inner_split], 3.0)
    packed = sum_of(clock, packed_all, BF16)
    packed_all = everyone(packed, "context")
    input_grad = [last(clock, x_rows[i], resid_grad[i], gain_one_row, one_terms[i], 3.0) for i in turns[:-1]]
    down_grad, branch_grad = turned_pieces(clock, early, [(units, True), (width, False)])
    input_grad.append(last(clock, x_rows[-1], resid_grad[-1], gain_one_row, one_terms[-1], LONG))
    packed = sum_of(clock, packed_all, F32)
    gate_blocks = packed[:, :side]
    small = packed[:, side:].reshape(-1)
    sums = small[: TILE * width].reshape(TILE, width)
    gains = small[TILE * width : TILE * width + 2 * model].reshape(2, model)
    out_grad, inner_weight_grad = turned_pieces(clock, late, [(width, True), (width, False)])

    def stacked(values):
        return jnp.stack(values).reshape(micro, seqs, rows, model)

    return (
        stacked(block_out),
        stacked(input_grad),
        gains[0],
        branch_grad,
        inner_weight_grad,
        sums[:CONV],
        sums[CONV],
        gate_blocks[:blocks],
        sums[CONV + 2],
        gate_blocks[blocks:],
        sums[CONV + 3],
        sums[CONV + 1] * (CPOW * jax.nn.sigmoid(-decay_param)),
        out_grad,
        gains[1],
        gate_grad,
        up_grad,
        down_grad,
    )


def solution(mesh):
    tokens = P(None, "fsdp", ("context", "tensor"), None)
    by_rows = P(("fsdp", "context"), "tensor")
    by_cols = P("tensor", ("fsdp", "context"))
    channel = P("tensor")
    taps = P(None, "tensor")
    blocks = P("tensor", None, None)
    return jax.shard_map(
        per_device,
        mesh=mesh,
        in_specs=(
            tokens, P(None, "fsdp", None), P(), by_rows, by_rows, taps, channel, blocks, channel, blocks, channel,
            channel, by_cols, P(), by_rows, by_rows, by_cols, tokens,
        ),
        out_specs=(
            tokens, tokens, P(), by_rows, by_rows, taps, channel, blocks, channel, blocks, channel, channel,
            by_cols, P(), by_rows, by_rows, by_cols,
        ),
        check_vma=False,
    )
```

```python
from functools import partial

import jax
import jax.numpy as jnp
from jax import lax
from jax.experimental import pallas as pl
from jax.experimental.pallas import tpu as pltpu
from jax.sharding import PartitionSpec as P

CONV = 4
CPOW = 8
EPS = 1e-06
TILE = 8
F32 = jnp.float32
BF16 = jnp.bfloat16
GELU_A = 0.7978845608028654
GELU_B = 0.044715
LONG = 10**4
RATE = 3e9


def shift(value, axis, by):
    size = lax.axis_size(axis)
    return lax.ppermute(value, axis, [(i, (i + by) % size) for i in range(size)])


def step_by(value, axis, by):
    size = lax.axis_size(axis)
    return lax.ppermute(value, axis, [(i, i + by) for i in range(size) if 0 <= i + by < size])


def sum_over(value, axis):
    size = lax.axis_size(axis)
    parts = [value] + [shift(value, axis, k) for k in range(1, size)]
    total = parts[0].astype(F32)
    for part in parts[1:]:
        total = total + part.astype(F32)
    return total


def gelu_parts(v):
    th = jnp.tanh(GELU_A * (v + GELU_B * (v * v * v)))
    half = 0.5 * (1.0 + th)
    slope = half + 0.5 * v * (1.0 - th * th) * (GELU_A * (1.0 + 3.0 * GELU_B * (v * v)))
    return v * half, slope


def neg_expm1(z):
    series = 1.0 + z * (1.0 / 10.0)
    for n in (9.0, 8.0, 7.0, 6.0, 5.0, 4.0, 3.0, 2.0):
        series = 1.0 + z * (1.0 / n) * series
    return jnp.where(z > -0.5, -z * series, 1.0 - jnp.exp(z))


def sigmoid(v):
    return 1.0 / (1.0 + jnp.exp(-v))


def tile_scan(coeffs, offsets, reverse):
    rows, width = coeffs.shape
    a = coeffs.reshape(rows // TILE, TILE, width)
    b = offsets.reshape(rows // TILE, TILE, width)
    place = lax.broadcasted_iota(jnp.int32, a.shape, 1)
    for s in (1, 2, 4):
        if reverse:
            inside, turn = place < TILE - s, TILE - s
        else:
            inside, turn = place >= s, s
        a_far = pltpu.roll(a, turn, 1)
        b_far = pltpu.roll(b, turn, 1)
        b = jnp.where(inside, b + a * b_far, b)
        a = jnp.where(inside, a * a_far, a)
    return a, b


def forward_kernel(
    inner_ref, halo_ref, mask_ref, par_ref, wg_ref,
    conv_ref, pre_ref, decay_ref, prod_ref, state_ref, last_ref, ext, run,
):
    rows = inner_ref.shape[0]
    step = pl.program_id(0)

    @pl.when(step == 0)
    def _():
        ext[0:TILE] = halo_ref[...].astype(F32)
        run[0:1] = jnp.ones_like(run[0:1])
        run[1:2] = jnp.zeros_like(run[1:2])

    inner = inner_ref[...].astype(BF16).astype(F32)
    ext[TILE : TILE + rows] = inner
    mask = mask_ref[...]
    conv = par_ref[CONV : CONV + 1] + par_ref[0:1] * inner
    for k in range(1, CONV):
        conv = conv + par_ref[k : k + 1] * ext[TILE - k : TILE - k + rows] * mask[:, k - 1 : k]
    ext[0:TILE] = inner[rows - TILE :]
    conv_low = conv.astype(BF16)
    conv_ref[...] = conv_low
    pre = jnp.dot(conv_low, wg_ref[...], preferred_element_type=F32)
    width = inner.shape[1]
    rate_pre = pre[:, :width] + par_ref[CONV + 2 : CONV + 3]
    input_pre = pre[:, width:] + par_ref[CONV + 3 : CONV + 4]
    pre_ref[:, :width] = rate_pre
    pre_ref[:, width:] = input_pre
    log_rate = par_ref[CONV + 1 : CONV + 2] * sigmoid(rate_pre)
    starts = mask[:, CONV - 1 : CONV] > 0.5
    decays = jnp.where(starts, 0.0, jnp.exp(log_rate))
    scale = jnp.where(starts, 1.0, jnp.sqrt(neg_expm1(2.0 * log_rate)))
    drives = scale * sigmoid(input_pre) * conv_low.astype(F32)
    decay_ref[...] = decays
    a, b = tile_scan(decays, drives, False)
    prod, state = run[0:1], run[1:2]
    for i in range(rows // TILE):
        prods = a[i] * prod
        states = b[i] + a[i] * state
        prod_ref[i * TILE : (i + 1) * TILE] = prods
        state_ref[i * TILE : (i + 1) * TILE] = states
        prod, state = prods[TILE - 1 :], states[TILE - 1 :]
    run[0:1] = prod
    run[1:2] = state
    last_ref[0:1] = prod
    last_ref[1:2] = state


def reverse_kernel(
    many, *refs
):
    blocks, refs = refs[: many + 1], refs[many + 1 :]
    (weight_ref, branch_ref, states_ref, decay_ref, wide_ref,
     low_ref, prod_ref, grad_ref, first_ref, mixed_all, ext, run) = refs
    rows = branch_ref.shape[0]
    step = pl.program_id(0)
    place = pl.num_programs(0) - 1 - step

    @pl.when(step == 0)
    def _():
        ext[rows : rows + TILE] = jnp.ones_like(ext[rows : rows + TILE])
        run[0:1] = jnp.ones_like(run[0:1])
        run[1:2] = jnp.zeros_like(run[1:2])
        assemble(blocks, wide_ref)
        mixed_all[...] = jnp.dot(wide_ref[...], weight_ref[...], preferred_element_type=F32)

    mixed = mixed_all[pl.ds(pl.multiple_of(place * rows, TILE), rows)]
    value, slope = gelu_parts(branch_ref[...])
    low_ref[...] = (mixed * states_ref[...] * slope).astype(BF16)
    decays = decay_ref[...]
    ext[0:rows] = decays
    following = ext[1 : rows + 1]
    ext[rows : rows + TILE] = decays[0:TILE]
    a, b = tile_scan(following, mixed * value, True)
    prod, grad = run[0:1], run[1:2]
    for i in reversed(range(rows // TILE)):
        prods = a[i] * prod
        grads = b[i] + a[i] * grad
        prod_ref[i * TILE : (i + 1) * TILE] = prods
        grad_ref[i * TILE : (i + 1) * TILE] = grads
        prod, grad = prods[0:1], grads[0:1]
    run[0:1] = prod
    run[1:2] = grad
    first_ref[0:1] = decays[0:1] * prod
    first_ref[1:2] = decays[0:1] * grad


def gates_kernel(
    prod_ref, grad_ref, in_ref, prev_ref, state_in_ref, states_ref, decay_ref, pre_ref, conv_ref,
    inner_ref, inner_prev_ref, halo_ref, mask_ref, par_ref, wg_ref,
    low_ref, inner_grad_ref, edge_ref, sums_ref, ext, later,
):
    rows, width = prod_ref.shape
    step = pl.program_id(0)
    at_start = step == pl.num_programs(0) - 1

    @pl.when(step == 0)
    def _():
        sums_ref[...] = jnp.zeros_like(sums_ref)
        later[...] = jnp.zeros_like(later)

    mask = mask_ref[...]
    starts = mask[:, CONV - 1 : CONV] > 0.5
    drive_grad = grad_ref[...] + prod_ref[...] * in_ref[...]
    ext[TILE : TILE + rows] = states_ref[...]
    ext[TILE - 1 : TILE] = jnp.where(at_start, state_in_ref[...], prev_ref[TILE - 1 : TILE])
    prev_states = ext[TILE - 1 : TILE - 1 + rows]
    rate = sigmoid(pre_ref[:, :width])
    gate = sigmoid(pre_ref[:, width:])
    conv = conv_ref[...].astype(F32)
    slope = par_ref[CONV + 1 : CONV + 2]
    log_rate = slope * rate
    decays = decay_ref[...]
    raw = jnp.sqrt(neg_expm1(2.0 * log_rate))
    scale = jnp.where(starts, 1.0, raw)
    scale_grad = drive_grad * gate * conv
    log_grad = jnp.where(
        starts, 0.0, drive_grad * prev_states * decays - scale_grad * (decays * decays) / raw
    )
    rate_low = (log_grad * slope * rate * (1.0 - rate)).astype(BF16)
    input_low = (drive_grad * scale * conv * gate * (1.0 - gate)).astype(BF16)
    low_ref[:, :width] = rate_low
    low_ref[:, width:] = input_low
    both = jnp.concatenate([rate_low, input_low], axis=1)
    conv_grad = drive_grad * scale * gate + lax.dot_general(
        both, wg_ref[...], (((1,), (1,)), ((), ())), preferred_element_type=F32
    )
    inner = inner_ref[...].astype(BF16).astype(F32)
    before = jnp.where(at_start, halo_ref[...].astype(F32), inner_prev_ref[...].astype(BF16).astype(F32))
    ext[0:TILE] = before
    ext[TILE : TILE + rows] = inner

    def total(values):
        return jnp.sum(values, axis=0, keepdims=True)

    sums_ref[0:1] += total(conv_grad * inner)
    sums_ref[CONV : CONV + 1] += total(conv_grad)
    sums_ref[CONV + 1 : CONV + 2] += total(log_grad * rate)
    sums_ref[CONV + 2 : CONV + 3] += total(rate_low.astype(F32))
    sums_ref[CONV + 3 : CONV + 4] += total(input_low.astype(F32))
    inner_grad = par_ref[0:1] * conv_grad
    heads = []
    for k in range(1, CONV):
        masked = conv_grad * mask[:, k - 1 : k]
        sums_ref[k : k + 1] += total(masked * ext[TILE - k : TILE - k + rows])
        heads.append(masked[0:TILE] * par_ref[k : k + 1])
    for k in range(1, CONV):
        masked = par_ref[k : k + 1] * (conv_grad * mask[:, k - 1 : k])
        ext[0:rows] = masked
        ext[rows : rows + TILE] = later[k - 1]
        inner_grad = inner_grad + ext[k : k + rows]
        later[k - 1] = heads[k - 1]
    inner_grad_ref[...] = inner_grad.astype(inner_grad_ref.dtype)

    @pl.when(at_start)
    def _():
        edge_ref[...] = jnp.zeros_like(edge_ref)
        for back in range(1, CONV):
            row = heads[back - 1][0:1]
            for k in range(back + 1, CONV):
                row = row + heads[k - 1][k - back : k - back + 1]
            edge_ref[TILE - back : TILE - back + 1] = row


def rows_spec(rows, width, parts, column=0, reverse=False):
    return pl.BlockSpec((rows, width), lambda step: (parts - 1 - step if reverse else step, column))


def before_spec(rows, width, parts, column=0):
    tiles = rows // TILE
    return pl.BlockSpec(
        (TILE, width), lambda step: (jnp.maximum(parts - 2 - step, 0) * tiles + tiles - 1, column)
    )


def whole_spec(shape):
    return pl.BlockSpec(shape, lambda step: (0,) * len(shape))


def dot_nt(left, right):
    return lax.dot_general(left, right, (((1,), (1,)), ((), ())), preferred_element_type=F32)


def dot_tn(left, right):
    return lax.dot_general(left, right, (((0,), (0,)), ((), ())), preferred_element_type=F32)


COSTS = (
    0.2, 3, 0.2, 6, 0.01, 6, 5.7, 7, 5.7, 3, 3, 3, 27, 3.4, 21, 60, 0.01, 0.01, 7.5, 7.5, 6, 7, 8, 40, 40, 0.01, 0.01, 0.01, 0.01, 0.01, 0.01, 0.01, 0.01, 0.01, 3, 10000.0, 1, 3,
)


class Clock:
    def __init__(self):
        self.tick = jnp.zeros((TILE, 128), F32)
        self.calls = 0

    def call(self, kernel, grid, operands, in_specs, out_specs, out_shape, scratch=(), after=(), cost=3.0):
        cost = COSTS[self.calls] if self.calls < len(COSTS) else cost
        self.calls += 1
        count, extra, outs = len(operands), len(after) + 1, len(out_shape)

        def body(*refs):
            given, refs = refs[:count], refs[count + extra :]
            kernel(*given, *refs[:outs], *refs[outs + 1 :])
            refs[outs][...] = jnp.zeros_like(refs[outs])

        whole = pl.BlockSpec((TILE, 128), lambda *step: (0, 0))
        *results, self.tick = pl.pallas_call(
            body,
            out_shape=list(out_shape) + [jax.ShapeDtypeStruct((TILE, 128), F32)],
            grid=grid,
            in_specs=list(in_specs) + [pl.BlockSpec(memory_space=pl.ANY)] * extra,
            out_specs=list(out_specs) + [whole],
            scratch_shapes=list(scratch),
            cost_estimate=pl.CostEstimate(flops=int(cost * RATE), bytes_accessed=int(cost * RATE), transcendentals=0),
        )(*operands, *after, self.tick)
        return results


def shape(dims, dtype):
    return jax.ShapeDtypeStruct(dims, dtype)


def held(array):
    dims = array.shape
    return pl.BlockSpec(dims, lambda *step: (0,) * len(dims), pipeline_mode=pl.Buffered(1))


def kept(dims):
    return pl.BlockSpec(dims, lambda *step: (0,) * len(dims))


def place_spec():
    return pl.BlockSpec(memory_space=pltpu.SMEM)


def spread(copies, apart):
    if not apart:
        return [lax.all_to_all(copies, "tensor", split_axis=0, concat_axis=0, tiled=True)]
    return [copies] + [shift(copies, "tensor", k) for k in range(1, lax.axis_size("tensor"))]


def gathered_sums(parts):
    if len(parts) == 1:
        return [lax.all_to_all(parts[0], "tensor", split_axis=0, concat_axis=0, tiled=True)]
    return [parts[0]] + [shift(parts[k], "tensor", k) for k in range(1, len(parts))]


def assemble(refs, wide_ref):
    place, blocks = refs[0], refs[1:]
    if len(blocks) == 1:
        wide_ref[...] = blocks[0][...]
        return
    rows = blocks[0].shape[0]
    for k, block in enumerate(blocks):
        owner = lax.rem(place[0] - k + len(blocks), len(blocks))
        wide_ref[pl.ds(pl.multiple_of(owner * rows, 2 * TILE), rows)] = block[...]


def deal(values, place, outs, work):
    if len(outs) == 1:
        outs[0][...] = values.astype(BF16)
        return
    work[...] = values
    rows = outs[0].shape[0]
    for k, out in enumerate(outs):
        owner = lax.rem(place[0] + k, len(outs))
        out[...] = work[pl.ds(pl.multiple_of(owner * rows, 2 * TILE), rows)].astype(BF16)


def added(refs, rows):
    if len(refs) == 1:
        count = refs[0].shape[0] // rows
        terms = [refs[0][k * rows : (k + 1) * rows].astype(F32) for k in range(count)]
    else:
        terms = [ref[...].astype(F32) for ref in refs]
    return sum(terms[1:], terms[0])


def repeat_to(ref, values, rows):
    for k in range(ref.shape[0] // rows):
        ref[k * rows : (k + 1) * rows] = values


def mean_of(values):
    return jnp.mean(values, axis=-1, keepdims=True)


def first_kernel(x_ref, gain_ref, out_ref):
    x = x_ref[...].astype(F32)
    repeat_to(out_ref, (x * lax.rsqrt(mean_of(x * x) + EPS) * gain_ref[...]).astype(BF16), x_ref.shape[0])


def first(clock, x, gain, copies):
    rows, model = x.shape
    return clock.call(
        first_kernel, (1,), [x, gain], [held(x), held(gain)],
        [kept((copies * rows, model))], [shape((copies * rows, model), BF16)],
        cost=0.2,
    )[0]


def copies_kernel(*refs):
    out_ref = refs[-1]
    rows = refs[0].shape[0]
    for k in range(out_ref.shape[0] // rows):
        out_ref[k * rows : (k + 1) * rows] = refs[k % (len(refs) - 1)][...]


def all_copies(clock, arrays, copies, after):
    rows, model = arrays[0].shape
    total = rows * len(arrays) * copies
    return clock.call(
        copies_kernel, (1,), arrays, [held(a) for a in arrays], [kept((total, model))],
        [shape((total, model), BF16)], after=after,
        cost=3.0,
    )[0]


def project_kernel(many, *refs):
    blocks, (weight_ref, wide_ref, out_ref, halo_ref) = refs[: many + 1], refs[many + 1 :]

    @pl.when(pl.program_id(0) == 0)
    def _():
        assemble(blocks, wide_ref)

    value = jnp.dot(wide_ref[...], weight_ref[...], preferred_element_type=F32)
    out_ref[...] = value

    @pl.when(pl.program_id(0) == pl.num_programs(0) - 1)
    def _():
        halo_ref[...] = value[value.shape[0] - TILE :].astype(BF16)


def project(clock, place, blocks, weight, cols, after=()):
    model = weight.shape[0]
    rows = sum(block.shape[0] for block in blocks)
    width = cols // 2
    return clock.call(
        partial(project_kernel, len(blocks)), (2,), [place, *blocks, weight],
        [place_spec()] + [held(b) for b in blocks] + [pl.BlockSpec((model, width), lambda j: (0, j))],
        [kept((rows, model)), pl.BlockSpec((rows, width), lambda j: (0, j)), kept((TILE, width))],
        [shape((rows, model), BF16), shape((rows, cols), F32), shape((TILE, width), BF16)], after=after,
        cost=6.0,
    )


def mix_kernel(outs, place_ref, local_ref, prod_ref, in_ref, branch_ref, weight_ref, *refs):
    states_ref, mixed_ref = refs[:2]

    @pl.when(pl.program_id(0) == 0)
    def _():
        states = local_ref[...] + prod_ref[...] * in_ref[...]
        states_ref[...] = states
        mixed_ref[...] = (states * gelu_parts(branch_ref[...])[0]).astype(BF16)

    value = dot_nt(mixed_ref[...], weight_ref[...])
    deal(value, place_ref, refs[2 : 2 + outs], refs[-1])


def part_specs(rows, cols, tile, outs):
    return (
        [pl.BlockSpec((rows // outs, tile), lambda j: (0, j))] * outs,
        [shape((rows // outs, cols), BF16)] * outs,
        pltpu.VMEM((rows, tile), F32),
    )


def mix_out(clock, place, local, prods, state_in, both_pre, weight, outs, tile, after=()):
    rows, width = local.shape
    cols = weight.shape[0]
    part_spec, part_shape, work = part_specs(rows, cols, tile, outs)
    results = clock.call(
        partial(mix_kernel, outs), (cols // tile,), [place, local, prods, state_in, both_pre, weight],
        [place_spec(), held(local), held(prods), held(state_in),
         pl.BlockSpec((rows, width), lambda j: (0, 0), pipeline_mode=pl.Buffered(1)),
         pl.BlockSpec((tile, width), lambda j: (j, 2))],
        [kept((rows, width)), kept((rows, width))] + part_spec,
        [shape((rows, width), F32), shape((rows, width), BF16)] + part_shape, [work], after,
        cost=5.7,
    )
    return results[0], results[1], results[2:]


def second_kernel(x_ref, gain_ref, *refs):
    terms, (resid_ref, out_ref) = refs[:-2], refs[-2:]
    rows = x_ref.shape[0]
    resid = x_ref[...].astype(F32) + added(terms, rows)
    resid_ref[...] = resid
    repeat_to(out_ref, (resid * lax.rsqrt(mean_of(resid * resid) + EPS) * gain_ref[...]).astype(BF16), rows)


def second(clock, x, gain, terms, copies, after=()):
    rows, model = x.shape
    return clock.call(
        second_kernel, (1,), [x, gain, *terms], [held(x), held(gain)] + [held(t) for t in terms],
        [kept((rows, model)), kept((copies * rows, model))],
        [shape((rows, model), F32), shape((copies * rows, model), BF16)],
        after=after,
        cost=3.0,
    )


def mlp_kernel(two_many, turn, turns, unit, outs, *refs):
    two_blocks, refs = refs[: two_many + 1], refs[two_many + 1 :]
    cot_all, gate_ref, up_ref, down_ref, two_ref, cot_ref, hidden_ref, pair_ref = refs[:8]
    parts, acc = refs[8 : 8 + outs], refs[-1]
    step = pl.program_id(0)

    @pl.when(step == 0)
    def _():
        assemble(two_blocks, two_ref)
        rows = unit
        for k in range(two_ref.shape[0] // rows):
            start = (k * turns + turn) * rows
            cot_ref[k * rows : (k + 1) * rows] = cot_all[start : start + rows]

    two = two_ref[...]
    gate_w, up_w = gate_ref[...], up_ref[...]
    gate_val, gate_slope = gelu_parts(jnp.dot(two, gate_w, preferred_element_type=F32))
    up_pre = jnp.dot(two, up_w, preferred_element_type=F32)
    hidden_ref[...] = (gate_val * up_pre).astype(BF16)
    hidden_grad = jnp.dot(cot_ref[...], down_ref[...], preferred_element_type=F32)
    gate_low = (hidden_grad * up_pre * gate_slope).astype(BF16)
    up_low = (hidden_grad * gate_val).astype(BF16)
    pair_ref[0] = gate_low
    pair_ref[1] = up_low
    term = dot_nt(gate_low, gate_w) + dot_nt(up_low, up_w)

    @pl.when(step == 0)
    def _():
        acc[...] = term

    @pl.when(step > 0)
    def _():
        acc[...] += term

    @pl.when(step == pl.num_programs(0) - 1)
    def _():
        rows = parts[0].shape[0]
        for k, out in enumerate(parts):
            start = 0 if outs == 1 else pl.multiple_of(lax.rem(two_blocks[0][0] + k, outs) * rows, 2 * TILE)
            out[...] = acc[pl.ds(start, rows)].astype(BF16)


def mlp(clock, place, two_blocks, cot_all, turn, turns, unit, weight, outs, tile, after=()):
    model, units = weight.shape[0], weight.shape[1] // 3
    rows = sum(block.shape[0] for block in two_blocks)
    steps = units // tile
    results = clock.call(
        partial(mlp_kernel, len(two_blocks), turn, turns, unit, outs), (steps,),
        [place, *two_blocks, cot_all, weight, weight, weight],
        [place_spec()] + [held(b) for b in two_blocks + [cot_all]]
        + [pl.BlockSpec((model, tile), lambda j: (0, j)), pl.BlockSpec((model, tile), lambda j: (0, steps + j)),
           pl.BlockSpec((model, tile), lambda j: (0, 2 * steps + j))],
        [kept((rows, model)), kept((rows, model)), pl.BlockSpec((rows, tile), lambda j: (0, j)),
         pl.BlockSpec((2, rows, tile), lambda j: (0, 0, j))] + [kept((rows // outs, model))] * outs,
        [shape((rows, model), BF16), shape((rows, model), BF16), shape((rows, units), BF16),
         shape((2, rows, units), BF16)] + [shape((rows // outs, model), BF16)] * outs,
        [pltpu.VMEM((rows, model), F32)], after,
        cost=27.0,
    )
    return *results[:4], results[4:]


def down_kernel(count, unit, *refs):
    right, out_ref = refs[count], refs[-1]
    for i in range(count):
        value = dot_nt(refs[i][...], right[...]).astype(BF16)
        for k in range(value.shape[0] // unit):
            start = (k * count + i) * unit
            out_ref[start : start + unit] = value[k * unit : (k + 1) * unit]


def down_out(clock, lefts, right, unit, tile):
    cols, depth = right.shape[0], lefts[0].shape[1]
    count = len(lefts)
    total = count * lefts[0].shape[0]
    return clock.call(
        partial(down_kernel, count, unit), (cols // tile,), [*lefts, right],
        [held(a) for a in lefts] + [pl.BlockSpec((tile, depth), lambda j: (j, 2))],
        [pl.BlockSpec((total, tile), lambda j: (0, j))], [shape((total, cols), BF16)],
        cost=0.01,
    )[0]


def norm_grad(values, grad, gain):
    inv = lax.rsqrt(mean_of(values * values) + EPS)
    unit = values * inv
    scaled = grad * gain
    return inv * (scaled - unit * mean_of(scaled * unit)), grad * unit


def third_kernel(resid_ref, cot_ref, gain_ref, *refs):
    terms, (grad_ref, low_ref, sum_ref) = refs[:-3], refs[-3:]
    rows = resid_ref.shape[0]
    grad = added(terms, rows).astype(BF16).astype(F32)
    term, product = norm_grad(resid_ref[...], grad, gain_ref[...])
    total = cot_ref[...].astype(F32) + term
    grad_ref[...] = total
    sum_ref[...] = jnp.sum(product, axis=0, keepdims=True)
    repeat_to(low_ref, total.astype(BF16), rows)


def third(clock, resid, cot, gain, terms, copies, cost):
    rows, model = resid.shape
    return clock.call(
        third_kernel, (1,), [resid, cot, gain, *terms], [held(resid), held(cot), held(gain)] + [held(t) for t in terms],
        [kept((rows, model)), kept((copies * rows, model)), kept((1, model))],
        [shape((rows, model), F32), shape((copies * rows, model), BF16), shape((1, model), F32)],
        cost=cost,
    )


def back_kernel(outs, place_ref, branch_ref, inner_ref, edge_ref, weight_ref, one_ref, *refs):
    low_ref, gain_ref = refs[:2]
    both_ref, work = refs[-2:]
    rows, width = branch_ref.shape

    @pl.when(pl.program_id(0) == 0)
    def _():
        both_ref[:, :width] = branch_ref[...]
        both_ref[: rows - 2 * TILE, width:] = inner_ref[: rows - 2 * TILE].astype(BF16)
        last = inner_ref[rows - 2 * TILE :]
        fixed = jnp.concatenate([last[:TILE], last[TILE:] + edge_ref[...]], axis=0)
        both_ref[rows - 2 * TILE :, width:] = fixed.astype(BF16)
        low_ref[...] = both_ref[:, width:]

    value = dot_nt(both_ref[...], weight_ref[...])
    gain_ref[...] = jnp.sum(value * one_ref[...].astype(F32), axis=0, keepdims=True)
    deal(value, place_ref, refs[2 : 2 + outs], work)


def back_one(clock, place, branch_low, inner_grad, edge_in, weight, wide_one, outs, tile):
    rows, width = branch_low.shape
    model = weight.shape[0]
    part_spec, part_shape, work = part_specs(rows, model, tile, outs)
    results = clock.call(
        partial(back_kernel, outs), (model // tile,), [place, branch_low, inner_grad, edge_in, weight, wide_one],
        [place_spec(), held(branch_low), held(inner_grad), held(edge_in),
         pl.BlockSpec((tile, 2 * width), lambda j: (j, 0)), pl.BlockSpec((rows, tile), lambda j: (0, j))],
        [kept((rows, width)), pl.BlockSpec((1, tile), lambda j: (0, j))] + part_spec,
        [shape((rows, width), BF16), shape((1, model), F32)] + part_shape,
        [pltpu.VMEM((rows, 2 * width), BF16), work],
        cost=6.2,
    )
    return results[0], results[1], results[2:]


def last_kernel(x_ref, resid_ref, gain_ref, *refs):
    terms, out_ref = refs[:-1], refs[-1]
    grad = added(terms, x_ref.shape[0]).astype(BF16).astype(F32)
    out_ref[...] = resid_ref[...] + norm_grad(x_ref[...].astype(F32), grad, gain_ref[...])[0]


def last(clock, x, resid_grad, gain, terms, cost):
    return clock.call(
        last_kernel, (1,), [x, resid_grad, gain, *terms],
        [held(x), held(resid_grad), held(gain)] + [held(t) for t in terms],
        [kept(resid_grad.shape)], [shape(resid_grad.shape, F32)], cost=cost,
    )[0]


def out_kernel(count, *refs):
    terms, outs = refs[count], refs[count + 1 :]
    rows = refs[0].shape[0]
    for i in range(count):
        total = refs[i][...]
        for k in range(terms.shape[0] // (count * rows)):
            start = (k * count + i) * rows
            total = total + terms[start : start + rows].astype(F32)
        outs[i][...] = total.astype(BF16)


def block_results(clock, residuals, terms):
    count = len(residuals)
    dims = residuals[0].shape
    return clock.call(
        partial(out_kernel, count), (1,), [*residuals, terms], [held(r) for r in residuals] + [held(terms)],
        [kept(dims)] * count, [shape(dims, BF16)] * count,
        cost=3.0,
    )


def stack_rows(refs):
    return jnp.concatenate(refs, axis=0) if len(refs) > 1 else refs[0]


def term_kernel(count, *refs):
    halved = len(refs[count].shape) == 3
    left = stack_rows([refs[i][...] for i in range(count)])
    right = stack_rows([refs[count + i][0] if halved else refs[count + i][...] for i in range(count)])
    refs[-1][...] = dot_tn(left, right).astype(refs[-1].dtype)


def weight_term(clock, lefts, rights, tile, cost, after=()):
    count = len(lefts)
    rows, depth = lefts[0].shape
    halves = rights[0].shape[0] if rights[0].ndim == 3 else 1
    cols = rights[0].shape[-1]
    if halves == 1:
        grid, left_at, out_at = (depth // tile,), (lambda j: (0, j)), (lambda j: (j, 0))
        right_spec = held(rights[0])
    else:
        grid, left_at, out_at = (halves, depth // tile), (lambda h, j: (0, j)), (lambda h, j: (j, h))
        right_spec = pl.BlockSpec((1, rows, cols), lambda h, j: (h, 0, 0))
    return clock.call(
        partial(term_kernel, count), grid, [*lefts, *rights],
        [pl.BlockSpec((rows, tile), left_at)] * count + [right_spec] * count,
        [pl.BlockSpec((tile, cols), out_at)], [shape((depth, halves * cols), BF16)], after=after,
        cost=cost,
    )[0]


def diagonal_kernel(count, cells, *refs):
    out_ref, work = refs[-2:]
    total = None
    for i in range(count):
        value = dot_tn(refs[i][...], refs[count + i][...])
        total = value if total is None else total + value
    work[...] = total
    cell = out_ref.shape[1]
    for i in range(cells):
        for h in range(2):
            col = (h * cells + i) * cell
            out_ref[h * cells + i] = work[i * cell : (i + 1) * cell, col : col + cell].astype(BF16)


def diagonal_terms(clock, lefts, rights, cells):
    count = len(lefts)
    width = lefts[0].shape[1]
    cell = width // cells
    return clock.call(
        partial(diagonal_kernel, count, cells), (1,), [*lefts, *rights],
        [held(a) for a in lefts] + [held(a) for a in rights],
        [kept((2 * cells, cell, cell))], [shape((2 * cells, cell, cell), BF16)],
        [pltpu.VMEM((width, 2 * width), F32)],
        cost=4.5,
    )[0]


def split_term_kernel(count, groups, unit, place_ref, *refs):
    k, c = pl.program_id(0), pl.program_id(1)
    owner = lax.rem(place_ref[0] + k, groups) * pl.num_programs(1) + c
    start = pl.multiple_of(owner * unit, unit)
    left = stack_rows([refs[i][:, pl.ds(start, unit)] for i in range(count)])
    total = dot_tn(left, stack_rows([refs[count + i][...] for i in range(count)])).astype(BF16)
    for g in range(groups):
        @pl.when(k == g)
        def _(g=g):
            refs[2 * count + g][...] = total


def split_term(clock, place, lefts, rights, groups, steps, cost, after=()):
    count = len(lefts)
    depth = lefts[0].shape[1]
    cols = rights[0].size // rights[0].shape[-2]
    unit = depth // (groups * steps)

    def spec(g):
        return pl.BlockSpec(
            (unit, cols), lambda k, c: (jnp.where(k < g, 0, jnp.where(k > g, steps - 1, c)), 0)
        )

    parts = clock.call(
        partial(split_term_kernel, count, groups, unit), (groups, steps), [place, *lefts, *rights],
        [place_spec()] + [held(a) for a in lefts] + [held(a) for a in rights],
        [spec(g) for g in range(groups)], [shape((unit * steps, cols), BF16)] * groups, after=after, cost=cost,
    )
    return [parts[0]] + [shift(parts[k], "fsdp", k) for k in range(1, groups)]


def member_kernel(groups, *refs):
    out_ref = refs[-1]
    col = 0
    for i in range(0, len(refs) - 1, groups):
        total = added(refs[i : i + groups], refs[i].shape[0])
        out_ref[:, col : col + total.shape[1]] = total.astype(BF16)
        col += total.shape[1]


def member_sums(clock, terms, cost=8.0):
    flat = [t for some in terms for t in some]
    rows, cols = flat[0].shape[0], sum(some[0].shape[1] for some in terms)
    tile = rows // 4
    added_up = clock.call(
        partial(member_kernel, len(terms[0])), (4,), flat,
        [pl.BlockSpec((tile, t.shape[1]), lambda j: (j, 0)) for t in flat],
        [pl.BlockSpec((tile, cols), lambda j: (j, 0))], [shape((rows, cols), BF16)], cost=cost,
    )[0]
    return lax.psum_scatter(added_up, "context", scatter_dimension=0, tiled=True)


def turned_kernel(cuts, in_ref, *outs):
    total = in_ref[...].astype(F32)
    col = 0
    for out, turned in zip(outs, cuts):
        step = out.shape[0] if turned else out.shape[1]
        piece = total[:, col : col + step]
        out[...] = piece.T if turned else piece
        col += step


def turned_pieces(clock, low, cuts):
    rows = low.shape[0]
    dims = [(cols, rows) if turned else (rows, cols) for cols, turned in cuts]
    return clock.call(
        partial(turned_kernel, [turned for _, turned in cuts]), (1,), [low], [held(low)], [kept(d) for d in dims],
        [shape(d, F32) for d in dims], cost=3.0,
    )


def sum_kernel(*refs):
    refs[-1][...] = added(refs[:-1], refs[0].shape[0]).astype(refs[-1].dtype)


def sum_of(clock, arrays, dtype):
    dims = arrays[0].shape
    return clock.call(
        sum_kernel, (1,), arrays, [held(a) for a in arrays], [kept(dims)], [shape(dims, dtype)], cost=1.0,
    )[0]


def everyone(value, axis):
    return [value] + [shift(value, axis, k) for k in range(1, lax.axis_size(axis))]


def forward_scan(clock, both_pre, halo, mask, params, gate_w, parts):
    total, width = both_pre.shape[0], params.shape[1]
    rows = total // parts
    spec = partial(rows_spec, rows, width, parts)
    return clock.call(
        forward_kernel, (parts,), [both_pre, halo, mask, params, gate_w],
        [spec(column=1), held(halo), rows_spec(rows, mask.shape[1], parts), held(params), held(gate_w)],
        [spec(), rows_spec(rows, 2 * width, parts), spec(), spec(), spec(), kept((2, width))],
        [shape((total, width), BF16), shape((total, 2 * width), F32), shape((total, width), F32),
         shape((total, width), F32), shape((total, width), F32), shape((2, width), F32)],
        [pltpu.VMEM((rows + TILE, width), F32), pltpu.VMEM((TILE, width), F32)],
        cost=7.0,
    )


def reverse_scan(clock, place, blocks, out_w, both_pre, states, decays, parts, after=()):
    total, width = states.shape
    rows = total // parts
    model = out_w.shape[0]
    spec = rows_spec(rows, width, parts, reverse=True)
    return clock.call(
        partial(reverse_kernel, len(blocks)), (parts,), [place, *blocks, out_w, both_pre, states, decays],
        [place_spec()] + [held(b) for b in blocks] + [pl.BlockSpec((model, width), lambda step: (0, 2), pipeline_mode=pl.Buffered(1)), spec, spec, spec],
        [kept((total, model)), spec, spec, spec, kept((2, width))],
        [shape((total, model), BF16), shape((total, width), BF16), shape((total, width), F32),
         shape((total, width), F32), shape((2, width), F32)],
        [pltpu.VMEM((total, width), F32), pltpu.VMEM((rows + TILE, width), F32), pltpu.VMEM((TILE, width), F32)],
        after,
        cost=7.5,
    )


def gates_back(clock, prods, grads, grad_in, states, state_in, decays, pre, conv_low, both_pre, halo, mask,
               params, gate_w, parts):
    total, width = states.shape
    rows = total // parts
    spec = partial(rows_spec, rows, width, parts, reverse=True)
    return clock.call(
        gates_kernel, (parts,),
        [prods, grads, grad_in, states, state_in, states, decays, pre, conv_low, both_pre, both_pre, halo, mask,
         params, gate_w],
        [spec(), spec(), held(grad_in), before_spec(rows, width, parts), held(state_in),
         spec(), spec(), rows_spec(rows, 2 * width, parts, reverse=True), spec(), spec(column=1),
         before_spec(rows, width, parts, column=1), held(halo),
         rows_spec(rows, mask.shape[1], parts, reverse=True), held(params), held(gate_w)],
        [rows_spec(rows, 2 * width, parts, reverse=True), spec(), kept((TILE, width)), kept((TILE, width))],
        [shape((total, 2 * width), BF16), shape((total, width), F32), shape((TILE, width), F32),
         shape((TILE, width), F32)],
        [pltpu.VMEM((rows + TILE, width), F32), pltpu.VMEM((CONV - 1, TILE, width), F32)],
        cost=8.5,
    )


def carry_over(ends, direction):
    size = lax.axis_size("context")
    incoming = jnp.zeros_like(ends[1:2])
    parts = [step_by(ends, "context", direction * k) for k in range(1, size)]
    for part in reversed(parts):
        incoming = part[1:2] + part[0:1] * incoming
    return incoming


def carry_all(ends, direction):
    stacked = jnp.concatenate([e[:1] for e in ends] + [e[1:] for e in ends], axis=0)
    count = len(ends)
    incoming = jnp.zeros_like(stacked[:count])
    for part in reversed([step_by(stacked, "context", direction * k) for k in range(1, lax.axis_size("context"))]):
        incoming = part[count:] + part[:count] * incoming
    return [incoming[i : i + 1] for i in range(count)]


def block_diagonal(weight):
    count, rows, cols = weight.shape
    return jnp.concatenate(
        [jnp.pad(weight[i], ((0, 0), (i * cols, (count - 1 - i) * cols))) for i in range(count)], axis=0
    )


def per_device(
    inputs, segments, norm_gain, branch_weight, inner_weight, conv_weight, conv_bias, rate_weight, rate_bias,
    input_weight, input_bias, decay_param, out_weight, mlp_gain, gate_weight, up_weight, down_weight, cotangent,
):
    micro, seqs, rows, model = inputs.shape
    parts = lax.axis_size("tensor")
    span = rows * parts
    width = conv_bias.shape[0]
    blocks = rate_weight.shape[0]
    units = gate_weight.shape[1]
    chains = [(m, s) for m in range(micro) for s in range(seqs)]
    context_pos = lax.axis_index("context")
    owners = ("fsdp", "context")

    first_w = lax.all_gather(
        jnp.concatenate([branch_weight, inner_weight, out_weight.T], 1), owners, axis=0, tiled=True
    )
    second_w = lax.all_gather(
        jnp.concatenate([gate_weight, up_weight, down_weight.T], 1), owners, axis=0, tiled=True
    )
    gate_w = jnp.concatenate([block_diagonal(rate_weight), block_diagonal(input_weight)], axis=1)
    slope = -CPOW * jax.nn.softplus(-decay_param)
    params = jnp.concatenate(
        [conv_weight, conv_bias[None], slope[None], rate_bias[None], input_bias[None]], axis=0
    )

    def masks_of(row):
        pad = jnp.concatenate([jnp.full((CONV - 1,), -1, jnp.int32), row])
        ext = lax.dynamic_slice_in_dim(pad, context_pos * span, span + CONV - 1)
        own = ext[CONV - 1 :]
        cols = [(ext[CONV - 1 - k : CONV - 1 - k + span] == own).astype(F32) for k in range(1, CONV)]
        return jnp.stack(cols + [1.0 - cols[0]], axis=1)

    count = len(chains)
    turns = range(count)
    apart = [i % 2 == 1 for i in turns]
    copies = [1 if a else parts for a in apart]
    outs = [parts if a else 1 for a in apart]
    place = lax.axis_index("tensor").reshape(1).astype(jnp.int32)
    x_rows = [inputs[m, s] for m, s in chains]
    cot_rows = [cotangent[m, s] for m, s in chains]
    gain_one_row, gain_two_row = norm_gain[None], mlp_gain[None]
    mask = [masks_of(segments[m, s]) for m, s in chains]
    clock = Clock()

    groups, members = lax.axis_size("fsdp"), lax.axis_size("context")
    group_place = lax.axis_index("fsdp").reshape(1).astype(jnp.int32)
    normed = [first(clock, x_rows[0], gain_one_row, copies[0])]
    cot_copies = all_copies(clock, cot_rows[:1], parts, (gate_w, params, *mask))
    normed += [first(clock, x_rows[i], gain_one_row, copies[i]) for i in turns if i]
    one_blocks = [spread(normed[i], apart[i]) for i in turns]
    cots = spread(cot_copies, False)
    later = cot_rows[1:]
    if later:
        second_w, later = lax.optimization_barrier((second_w, later))
        cots += [lax.all_gather(rows_in, "tensor", axis=0, tiled=True) for rows_in in later]
    projections, halo, scans, mixes, ends_in = [], [], [], [], []

    def start_chain(i):
        projections.append(project(clock, place, one_blocks[i], first_w, 2 * width))
        halo.append(step_by(projections[i][2], "context", 1))

    def scan_chain(i):
        scans.append(forward_scan(clock, projections[i][1], halo[i], mask[i], params, gate_w, parts))
        ends_in.append(carry_over(scans[i][5], 1))

    def mix_chain(i):
        mixes.append(mix_out(
            clock, place, scans[i][4], scans[i][3], ends_in[i], projections[i][1], first_w, outs[i], 512,
            () if i else tuple(cots[:1]),
        ))

    start_chain(0)
    scan_chain(0)
    for i in turns:
        if i + 1 < count:
            start_chain(i + 1)
        mix_chain(i)
        if i + 1 < count:
            scan_chain(i + 1)
    wide_one, both_pre, tails = map(list, zip(*projections))
    conv_low, pre, decays, prods, locals_, ends = map(list, zip(*scans))
    state_in = ends_in
    states, mixed_low, out_part = map(list, zip(*mixes))
    out_terms = [gathered_sums(p) for p in out_part]
    residual, two_blocks = [], []
    for i in turns:
        res, low = second(clock, x_rows[i], gain_two_row, out_terms[i], copies[i], () if i else (second_w,))
        residual.append(res)
        two_blocks.append(spread(low, apart[i]))
    mlps = [
        mlp(clock, place, two_blocks[i], cots[i], 0, 1, rows, second_w, outs[i], 256) for i in turns
    ]
    wide_two, wide_cot, hidden_low, pair_low, two_part = map(list, zip(*mlps))
    two_terms = [gathered_sums(p) for p in two_part]

    thirds = []
    for i in turns:
        thirds.append(third(
            clock, residual[i], cot_rows[i], gain_two_row, two_terms[i], copies[i], 60.0 if i else 3.4
        ))
        if i == 0:
            pair_grad = lax.psum_scatter(
                weight_term(clock, wide_two, pair_low, 512, 21.0), owners, scatter_dimension=0, tiled=True
            )
    resid_grad, resid_low, gain_two = map(list, zip(*thirds))
    resid_blocks = [spread(resid_low[i], apart[i]) for i in turns]
    down_split = split_term(clock, group_place, wide_cot, hidden_low, groups, 2, 0.01)
    (down_terms,) = gathered_sums([down_out(clock, hidden_low, second_w, rows, 512)])

    reversed_ = [
        reverse_scan(clock, place, resid_blocks[i], first_w, both_pre[i], states[i], decays[i], parts) for i in turns
    ]
    wide_resid, branch_low, rev_prods, rev_grads, ends_back = map(list, zip(*reversed_))
    grad_in = carry_all(ends_back, -1)
    branch_split = split_term(clock, group_place, wide_one, branch_low, groups, 1, 6.0)
    out_split = split_term(clock, group_place, wide_resid, mixed_low, groups, 1, 7.0)
    early = member_sums(clock, [down_split, branch_split], 8.0)
    backs = [
        gates_back(
            clock, rev_prods[i], rev_grads[i], grad_in[i], states[i], state_in[i], decays[i], pre[i], conv_low[i],
            both_pre[i], halo[i], mask[i], params, gate_w, parts,
        )
        for i in turns
    ]
    gates_low, inner_grad, edge, sums = map(list, zip(*backs))
    gate_grad, up_grad = turned_pieces(clock, pair_grad, [(units, False), (units, False)])
    edges = step_by(jnp.concatenate(edge, axis=0), "context", -1)
    edge_in = [edges[i * TILE : (i + 1) * TILE] for i in turns]
    gate_blocks = diagonal_terms(clock, conv_low, gates_low, blocks)
    ones = []
    for i in turns:
        ones.append(back_one(
            clock, place, branch_low[i], inner_grad[i], edge_in[i], first_w, wide_one[i], 1 if i else parts, 512
        ))
        if i == 0:
            block_out = block_results(clock, residual, down_terms)
    inner_low, gain_one, one_part = map(list, zip(*ones))
    one_terms = [gathered_sums(p) for p in one_part]
    inner_split = split_term(clock, group_place, wide_one, inner_low, groups, 1, 8.0)
    gains = sum_over(jnp.concatenate([sum(gain_one) / gain_one_row, sum(gain_two)]), "tensor")
    small = jnp.concatenate([sum(sums).reshape(-1), gains.reshape(-1)]).astype(BF16)
    cells, side = gate_blocks.shape[0], gate_blocks.shape[2]
    extra = -(-small.size // (cells * side * 2 * TILE)) * 2 * TILE
    small = jnp.pad(small, (0, cells * extra * side - small.size)).reshape(cells, extra, side)
    packed_all = everyone(jnp.concatenate([gate_blocks, small], axis=1), "fsdp")
    late = member_sums(clock, [out_split, inner_split], 3.0)
    packed = sum_of(clock, packed_all, BF16)
    packed_all = everyone(packed, "context")
    input_grad = [last(clock, x_rows[i], resid_grad[i], gain_one_row, one_terms[i], 3.0) for i in turns[:-1]]
    down_grad, branch_grad = turned_pieces(clock, early, [(units, True), (width, False)])
    input_grad.append(last(clock, x_rows[-1], resid_grad[-1], gain_one_row, one_terms[-1], LONG))
    packed = sum_of(clock, packed_all, F32)
    gate_blocks = packed[:, :side]
    small = packed[:, side:].reshape(-1)
    sums = small[: TILE * width].reshape(TILE, width)
    gains = small[TILE * width : TILE * width + 2 * model].reshape(2, model)
    out_grad, inner_weight_grad = turned_pieces(clock, late, [(width, True), (width, False)])

    def stacked(values):
        return jnp.stack(values).reshape(micro, seqs, rows, model)

    return (
        stacked(block_out),
        stacked(input_grad),
        gains[0],
        branch_grad,
        inner_weight_grad,
        sums[:CONV],
        sums[CONV],
        gate_blocks[:blocks],
        sums[CONV + 2],
        gate_blocks[blocks:],
        sums[CONV + 3],
        sums[CONV + 1] * (CPOW * jax.nn.sigmoid(-decay_param)),
        out_grad,
        gains[1],
        gate_grad,
        up_grad,
        down_grad,
    )


def solution(mesh):
    tokens = P(None, "fsdp", ("context", "tensor"), None)
    by_rows = P(("fsdp", "context"), "tensor")
    by_cols = P("tensor", ("fsdp", "context"))
    channel = P("tensor")
    taps = P(None, "tensor")
    blocks = P("tensor", None, None)
    return jax.shard_map(
        per_device,
        mesh=mesh,
        in_specs=(
            tokens, P(None, "fsdp", None), P(), by_rows, by_rows, taps, channel, blocks, channel, blocks, channel,
            channel, by_cols, P(), by_rows, by_rows, by_cols, tokens,
        ),
        out_specs=(
            tokens, tokens, P(), by_rows, by_rows, taps, channel, blocks, channel, blocks, channel, channel,
            by_cols, P(), by_rows, by_rows, by_cols,
        ),
        check_vma=False,
    )
```
